32 devices in a mesh: gx: 4 (over y, core), gy: 2 (over x), gz: 4 (over z).
Axes of the slice: x: 2, y: 2, z: 4, core: 2. Of those that a mesh axis runs over, the one named last changes fastest.
Arguments:
- warmth_values: float32 [256, 32, 512], P('gx', 'gy', 'gz'), may hold values from -4 to 4
- dissolved_sugar: float32 [256, 32, 512], P('gx', 'gy', 'gz'), may hold values from 0.5 to 2
- nucleus_population: float32 [8, 256, 32, 512], P(None, 'gx', 'gy', 'gz'), may hold values from 0.05 to 1
- enlarge_coefficient_grid: float32 [256, 32, 512], P('gx', 'gy', 'gz'), may hold values from 0.05 to 0.5
- sensor_readings: bfloat16 [2, 256, 32, 512], P(None, 'gx', 'gy', 'gz'), may hold values from -4 to 4
Outputs:
- sensitivity: float32 [256, 32, 512], P('gx', 'gy', 'gz')
- misfit: float32 [], replicated
- gradient: float32 [], replicated
The draws below stay inside these ranges and needn't reach their ends.
All inputs are finite; a program needn't handle non-finite values.
Results may differ from the reference program's by a relative error of at most 0.0003.
Values sent between devices are 32-bit elements; how exact they have to be, the bound alone decides.
No kernel may reach another device: no remote copies, remote signals or barrier semaphores. Data moves between devices by JAX's collectives and lax.ppermute only.
A program may use at most 128 MiB of HBM per device.

```python
import math
import jax
import jax.numpy as jnp
from jax import lax

NB = 8
LONG_COUNT = 256
BROAD_COUNT = 32
TALL_COUNT = 512


def block_levels(rng, dims, cuts, smallest, largest):
    def one(position, shards_of):
        steps = jax.random.uniform(jax.random.fold_in(jax.random.fold_in(rng, 6), position), (shards_of,), jnp.float32, smallest / len(cuts), largest / len(cuts))
        return jnp.repeat(jnp.exp(steps), dims[position] // shards_of).reshape((-1,) + (1,) * (len(dims) - position - 1))

    level = one(*cuts[0])
    for cut in cuts[1:]:
        level = level * one(*cut)
    return level


def centred(own_key, extent, scale, limit, shards=(), dtype=jnp.bfloat16):
    array = scale * jax.random.normal(own_key, extent, jnp.float32)
    if shards:
        array = array * block_levels(own_key, extent, shards, -0.22, 0.18)
    return jnp.clip(array, -limit, limit).astype(dtype)


def setup_inputs(seed: int = 0) -> dict:
    splits = jax.random.split(jax.random.key(seed), 6)
    warmth_values = centred(splits[0], (LONG_COUNT, BROAD_COUNT, TALL_COUNT), 1.0, 4.0, ((0, 4), (1, 2), (2, 4)), jnp.float32)
    dissolved_sugar = jnp.clip(0.5 + 1.5 * jax.random.uniform(splits[1], (LONG_COUNT, BROAD_COUNT, TALL_COUNT), jnp.float32) ** block_levels(splits[1], (LONG_COUNT, BROAD_COUNT, TALL_COUNT), ((0, 4), (1, 2), (2, 4)), -0.2, 0.2), 0.5, 2.0)
    nucleus_population = jnp.clip(jnp.exp(math.log(1.0) - 2.9957323 * jax.random.uniform(splits[2], (NB, LONG_COUNT, BROAD_COUNT, TALL_COUNT), jnp.float32) ** block_levels(splits[2], (NB, LONG_COUNT, BROAD_COUNT, TALL_COUNT), ((1, 4), (2, 2), (3, 4)), -0.2, 0.2)), 0.05, 1.0)
    enlarge_coefficient_grid = jnp.clip(jnp.exp(math.log(0.5) - 2.3025851 * jax.random.uniform(splits[3], (LONG_COUNT, BROAD_COUNT, TALL_COUNT), jnp.float32) ** block_levels(splits[3], (LONG_COUNT, BROAD_COUNT, TALL_COUNT), ((0, 4), (1, 2), (2, 4)), -0.2, 0.2)), 0.05, 0.5)
    sensor_readings = centred(splits[4], (2, LONG_COUNT, BROAD_COUNT, TALL_COUNT), 1.0, 4.0, ((1, 4), (2, 2), (3, 4)))
    return dict(warmth_values=warmth_values, dissolved_sugar=dissolved_sugar, nucleus_population=nucleus_population, enlarge_coefficient_grid=enlarge_coefficient_grid, sensor_readings=sensor_readings)


SOLIDIFY_POINT = 0.5
LOWERING_COEF = 0.5
GROW = 0.3
NUCLEATE = 0.2
VOLUME = 0.005
ALPHA = 1.0
COND = 1.0
WARMTH_ADVANCE = 0.08
STEP_SOLUTE = 0.1
HIDDEN_WARMTH = 0.5
REJECT = 0.3

def volumes(bin_count):
    bin_rank = jnp.arange(bin_count).astype(jnp.float32) + 1.0
    return VOLUME * bin_rank * bin_rank

def conduct(nucleus_population):
    volume_table = volumes(nucleus_population.shape[0])
    return COND * (1.0 + ALPHA * lax.optimization_barrier(jnp.sum(volume_table[:, None, None, None] * nucleus_population, axis=0)))

def neighbours(padded):
    centre = padded[1:-1, 1:-1, 1:-1]
    near_list = [padded[2:, 1:-1, 1:-1], padded[:-2, 1:-1, 1:-1], padded[1:-1, 2:, 1:-1], padded[1:-1, :-2, 1:-1], padded[1:-1, 1:-1, 2:], padded[1:-1, 1:-1, :-2]]
    return (centre, near_list)

def conduction(field_pad, kappa_pad):
    centre, field_near = neighbours(field_pad)
    kappa_centre, kappa_near = neighbours(kappa_pad)
    summed = jnp.zeros_like(centre)
    for f_near, k_near in zip(field_near, kappa_near):
        summed = summed + 0.5 * (kappa_centre + k_near) * (f_near - centre)
    return summed

def kappa_pull(warmth_bordered, adjoint_pad):
    temp_centre, temp_near = neighbours(warmth_bordered)
    adj_centre, adj_near = neighbours(adjoint_pad)
    summed = jnp.zeros_like(temp_centre)
    for t_near, a_near in zip(temp_near, adj_near):
        summed = summed + 0.5 * (t_near - temp_centre) * (adj_centre - a_near)
    return summed

def laplace(padded):
    centre, near_list = neighbours(padded)
    summed = jnp.zeros_like(centre)
    for f_near in near_list:
        summed = summed + f_near
    return summed - 6.0 * centre

def enlarge_factor(warmth_values, dissolved_sugar, nucleus_population, enlarge_coefficient_grid, warming_part, spreading_part):
    below_threshold = SOLIDIFY_POINT - LOWERING_COEF * dissolved_sugar - warmth_values
    growth_speed = enlarge_coefficient_grid * jax.nn.softplus(below_threshold)
    bin_count = nucleus_population.shape[0]
    open_bins = (jnp.arange(bin_count) < bin_count - 1).astype(jnp.float32)
    bin_flux = GROW * growth_speed[None] * nucleus_population * open_bins[:, None, None, None]
    inflow = jnp.concatenate([(NUCLEATE * growth_speed)[None], bin_flux[:-1]], axis=0)
    change = inflow - bin_flux
    frost_change = lax.optimization_barrier(jnp.sum(volumes(bin_count)[:, None, None, None] * change, axis=0))
    later_warmth = warmth_values + WARMTH_ADVANCE * warming_part + HIDDEN_WARMTH * frost_change
    new_solute = dissolved_sugar + STEP_SOLUTE * spreading_part + REJECT * frost_change
    return (later_warmth, new_solute, nucleus_population + change)

def advance_model(warmth_values, dissolved_sugar, nucleus_population, enlarge_coefficient_grid):
    voxel_conductance = conduct(nucleus_population)
    warmth_bordered = jnp.pad(warmth_values, 1)
    kappa_pad = jnp.pad(voxel_conductance, 1)
    warming_part = conduction(warmth_bordered, kappa_pad)
    spreading_part = laplace(jnp.pad(dissolved_sugar, 1))
    snapshot_later = enlarge_factor(warmth_values, dissolved_sugar, nucleus_population, enlarge_coefficient_grid, warming_part, spreading_part)
    return (snapshot_later, (warmth_bordered, kappa_pad, warming_part, spreading_part))

def backward(snapshot_present, saved_now, enlarge_coefficient_grid, adjoint):
    warmth_values, dissolved_sugar, nucleus_population = snapshot_present
    warmth_bordered, kappa_pad, warming_part, spreading_part = saved_now
    model_results, reverse_mapping = jax.vjp(enlarge_factor, warmth_values, dissolved_sugar, nucleus_population, enlarge_coefficient_grid, warming_part, spreading_part)
    adj_t, adj_s, adj_c, adj_g, adj_h, adj_d = reverse_mapping(adjoint)
    adj_h_pad = jnp.pad(adj_h, 1)
    adj_t = adj_t + conduction(adj_h_pad, kappa_pad)
    adj_s = adj_s + laplace(jnp.pad(adj_d, 1))
    kappa_term = kappa_pull(warmth_bordered, adj_h_pad)
    adj_c = adj_c + COND * ALPHA * volumes(nucleus_population.shape[0])[:, None, None, None] * kappa_term[None]
    cond_part = jnp.sum(adj_h * warming_part) / COND
    return ((adj_t, adj_s, adj_c), adj_g, cond_part)

def reference(warmth_values, dissolved_sugar, nucleus_population, enlarge_coefficient_grid, sensor_readings):
    snapshot_start = (warmth_values, dissolved_sugar, nucleus_population)
    snapshot_first, kept_start = advance_model(warmth_values, dissolved_sugar, nucleus_population, enlarge_coefficient_grid)
    state_two, saved_one = advance_model(snapshot_first[0], snapshot_first[1], snapshot_first[2], enlarge_coefficient_grid)
    miss_t = state_two[0] - sensor_readings[0].astype(jnp.float32)
    miss_s = state_two[1] - sensor_readings[1].astype(jnp.float32)
    cell_count = float(LONG_COUNT * BROAD_COUNT * TALL_COUNT)
    misfit = 0.5 * jnp.sum(miss_t * miss_t + miss_s * miss_s) / cell_count
    adjoint = (miss_t, miss_s, jnp.zeros_like(nucleus_population))
    adjoint, sense_one, part_one = backward(snapshot_first, saved_one, enlarge_coefficient_grid, adjoint)
    adjoint, sense_zero, part_zero = backward(snapshot_start, kept_start, enlarge_coefficient_grid, adjoint)
    return (sense_one + sense_zero, misfit, (part_one + part_zero) / cell_count)
```

```python
import functools

import jax
import jax.numpy as jnp
import numpy as np
from jax import lax
from jax.experimental import pallas as pl
from jax.experimental.pallas import tpu as pltpu
from jax.sharding import PartitionSpec as P

F32 = jnp.float32
AXES = ("gx", "gy", "gz")

SOLIDIFY_POINT = 0.5
LOWERING_COEF = 0.5
GROW = 0.3
NUCLEATE = 0.2
VOLUME = 0.005
WARMTH_ADVANCE = 0.08
STEP_SOLUTE = 0.1
HIDDEN_WARMTH = 0.5
REJECT = 0.3
LANES = 128


def volumes(bin_count):
    rank = np.arange(bin_count, dtype=np.float64) + 1.0
    return VOLUME * rank * rank


def functional_weights(bin_count):
    vol = volumes(bin_count)
    step = vol[1:] - vol[:-1]
    k = (1.0, vol)
    l = (NUCLEATE * vol[0], np.concatenate([GROW * step, [0.0]]))
    m_const = GROW * step[0] * NUCLEATE
    m = np.zeros(bin_count)
    for b in range(bin_count - 1):
        m[b] -= GROW * step[b] * GROW
        if b >= 1:
            m[b - 1] += GROW * step[b] * GROW
    return k, l, (m_const, m)


def swap_pairs(count, kind):
    if kind == 0:
        return [(i, i ^ 1) for i in range(count)]
    return [(i, (i + 1) % count if i % 2 else (i - 1) % count) for i in range(count)]


def swaps(count):
    return {1: 0, 2: 1}.get(count, 2)


def exchange(payloads, axis):
    count = lax.axis_size(axis)
    assert count == 1 or count % 2 == 0
    return [lax.ppermute(p, axis, swap_pairs(count, kind)) for kind, p in enumerate(payloads)]


class Side:
    def __init__(self, axis, count):
        self.count = count
        self.index = lax.axis_index(axis)
        self.odd = lax.rem(self.index, 2) == 1

    def outgoing(self, first, last):
        kinds = [jnp.where(self.odd, first, last), jnp.where(self.odd, last, first)]
        return kinds[: swaps(self.count)]

    def incoming(self, got):
        if self.count == 1:
            return None
        if self.count == 2:
            zero = jnp.zeros_like(got[0])
            return jnp.where(self.odd, got[0], zero), jnp.where(self.odd, zero, got[0])
        a, b = got
        zero = jnp.zeros_like(a)
        before = jnp.where(self.index > 0, jnp.where(self.odd, a, b), zero)
        after = jnp.where(self.index < self.count - 1, jnp.where(self.odd, b, a), zero)
        return before, after


def grid_iota(ny):
    row = lax.broadcasted_iota(jnp.int32, (ny, LANES), 0)
    lane = lax.broadcasted_iota(jnp.int32, (ny, LANES), 1)
    return row, lane


def pack_z(acc, value, x, lane):
    high = pltpu.roll(value, lax.rem(2 * x + 1, LANES), 1)
    low = pltpu.roll(value, lax.rem(2 * x + LANES - 1, LANES), 1)
    acc = jnp.where(lane == 2 * x, high, acc)
    return jnp.where(lane == lax.rem(2 * x + LANES - 1, LANES), low, acc)


class Halo:
    def __init__(self, dims, counts, fields, got, scratch):
        self.nx, self.ny = dims
        self.fields = fields
        self.xs, self.ys, self.zs = scratch
        nx, ny = dims
        gx, gy, gz = got
        sx, sy, sz = [Side(a, n) for a, n in zip(AXES, counts)]
        before, after = sx.incoming([r[...] for r in gx])
        self.xs[0], self.xs[1] = before, after
        before, after = sy.incoming([r[...] for r in gy])
        self.ys[0], self.ys[1] = before, after
        before, after = sz.incoming([r[...] for r in gz])
        lane = lax.broadcasted_iota(jnp.int32, before.shape, 1)
        self.zs[...] = jnp.where(lax.rem(lane, 2) == 0, before, after)

    def x(self, f, side):
        return self.xs[side, pl.ds(f * self.ny, self.ny), :]

    def y(self, f, side, x):
        return self.ys[side, pl.ds(f * self.nx + x, 1), :]

    def z(self, f, x):
        packed = self.zs[pl.ds(f * self.ny, self.ny), :]
        return pltpu.roll(packed, lax.rem(LANES - 2 * x + LANES, LANES), 1)


def halo_scratch(dims, fields):
    nx, ny = dims
    return [
        pltpu.VMEM((2, fields * ny, LANES), F32),
        pltpu.VMEM((2, fields * nx, LANES), F32),
        pltpu.VMEM((fields * ny, LANES), F32),
    ]


def around(cur, ym, yp, zr, row, lane):
    ny = cur.shape[0]
    return [
        jnp.where(row == 0, ym, pltpu.roll(cur, 1, 0)),
        jnp.where(row == ny - 1, yp, pltpu.roll(cur, ny - 1, 0)),
        jnp.where(lane == 0, zr, pltpu.roll(cur, 1, 1)),
        jnp.where(lane == LANES - 1, zr, pltpu.roll(cur, LANES - 1, 1)),
    ]


def put_faces(dims, counts, fields, outs, zaccs):
    nx, ny = dims
    ox, oy, oz = outs
    sx, sy, _ = [Side(a, n) for a, n in zip(AXES, counts)]
    for f, ref in enumerate(fields):
        first, last = ref[pl.ds(0, ny), :], ref[pl.ds((nx - 1) * ny, ny), :]
        for o, v in zip(ox, sx.outgoing(first, last)):
            o[pl.ds(f * ny, ny), :] = v
        first = ref[pl.ds(0, nx, stride=ny), :]
        last = ref[pl.ds(ny - 1, nx, stride=ny), :]
        for o, v in zip(oy, sy.outgoing(first, last)):
            o[pl.ds(f * nx, nx), :] = v
        for o in oz:
            o[pl.ds(f * ny, ny), :] = zaccs[f]


def face_shapes(dims, counts, fields):
    nx, ny = dims
    rows = (fields * ny, fields * nx, fields * ny)
    shapes = []
    for axis, (r, n) in enumerate(zip(rows, counts)):
        copies = min(swaps(n), 1) if axis == 2 else swaps(n)
        shapes += [((r, LANES), F32)] * copies
    return shapes


def split_faces(refs, counts):
    ax, ay = swaps(counts[0]), swaps(counts[1])
    return refs[:ax], refs[ax : ax + ay], refs[ax + ay :]


def send_faces(faces, counts):
    ox, oy, oz = split_faces(list(faces), counts)
    oz = [oz[0]] * swaps(counts[2])
    got = []
    for payload, axis in zip((ox, oy, oz), AXES):
        got += exchange(payload, axis)
    return got


def log1p_of(e, u, inv):
    return jnp.log(u) + (e - (u - 1.0)) * inv


def softplus_parts(v):
    e = jnp.exp(-jnp.abs(v))
    u = 1.0 + e
    inv = 1.0 / u
    soft = jnp.maximum(v, 0.0) + log1p_of(e, u, inv)
    return soft, jnp.where(v >= 0, inv, e * inv)


def prepare_kernel(dims, counts, bins, chunks, *refs):
    nx, ny = dims
    nface = len(face_shapes(dims, counts, 3))
    c_hbm, t_hbm, s_hbm = refs[:3]
    k_ref, l_ref, m_ref, t_ref, s_ref = refs[3:8]
    outs = split_faces(refs[8 : 8 + nface], counts)
    c_ref, sems = refs[8 + nface :]
    rows = nx * ny // chunks
    copies = [
        pltpu.make_async_copy(t_hbm, t_ref, sems.at[chunks]),
        pltpu.make_async_copy(s_hbm, s_ref, sems.at[chunks + 1]),
    ]
    for j in range(chunks):
        part = pl.ds(j * rows, rows)
        copies.append(pltpu.make_async_copy(c_hbm.at[:, part, :], c_ref.at[:, part, :], sems.at[j]))
    for copy in copies:
        copy.start()
    copies[0].wait()
    copies[1].wait()
    _, lane = grid_iota(ny)
    weights = functional_weights(bins)

    def plane(x, accs):
        here = pl.ds(x * ny, ny)
        c = [c_ref[b, here, :] for b in range(bins)]
        values = []
        for const, per_bin in weights:
            total = None
            for b in range(bins):
                if per_bin[b] != 0.0:
                    term = float(per_bin[b]) * c[b]
                    total = term if total is None else total + term
            values.append(float(const) + total)
        k_ref[here, :], l_ref[here, :], m_ref[here, :] = values
        faces = (t_ref[here, :], s_ref[here, :], values[0])
        return tuple(pack_z(a, v, x, lane) for a, v in zip(accs, faces))

    accs = tuple(jnp.zeros((ny, LANES), F32) for _ in range(3))
    planes = nx // chunks
    for j in range(chunks):
        copies[2 + j].wait()
        accs = lax.fori_loop(j * planes, (j + 1) * planes, plane, accs, unroll=2)
    put_faces(dims, counts, (t_ref, s_ref, k_ref), outs, accs)


def first_step_kernel(dims, counts, *refs):
    nx, ny = dims
    ngot = sum(swaps(n) for n in counts)
    nface = len(face_shapes(dims, counts, 4))
    t_ref, s_ref, g_ref, k_ref, l_ref, m_ref = refs[:6]
    got = refs[6 : 6 + ngot]
    t1, s1, k1, h0, l1, w0, v0 = refs[6 + ngot : 13 + ngot]
    outs = split_faces(refs[13 + ngot : 13 + ngot + nface], counts)
    scratch = refs[13 + ngot + nface :]
    a, b = swaps(counts[0]), swaps(counts[1])
    halo = Halo(dims, counts, 3, (got[:a], got[a : a + b], got[a + b :]), scratch)
    row, lane = grid_iota(ny)
    fields = (t_ref, s_ref, k_ref)

    def plane(x, carry):
        prev, cur, accs = carry
        here = pl.ds(x * ny, ny)
        ahead = pl.ds(jnp.minimum(x + 1, nx - 1) * ny, ny)
        nxt = tuple(
            jnp.where(x == nx - 1, halo.x(f, 1), r[ahead, :]) for f, r in enumerate(fields)
        )
        near = [
            [prev[f], nxt[f]]
            + around(cur[f], halo.y(f, 0, x), halo.y(f, 1, x), halo.z(f, x), row, lane)
            for f in range(3)
        ]
        t, s, k = cur
        heat = None
        for tn, kn in zip(near[0], near[2]):
            term = (k + kn) * (tn - t)
            heat = term if heat is None else heat + term
        heat = 0.5 * heat
        diff = near[1][0]
        for sn in near[1][1:]:
            diff = diff + sn
        diff = diff - 6.0 * s
        g, l, m = g_ref[here, :], l_ref[here, :], m_ref[here, :]
        soft, _ = softplus_parts(SOLIDIFY_POINT - LOWERING_COEF * s - t)
        w, v = soft * l, soft * m
        frost = g * w
        new_t = t + WARMTH_ADVANCE * heat + HIDDEN_WARMTH * frost
        new_s = s + STEP_SOLUTE * diff + REJECT * frost
        new_k = k + frost
        t1[here, :], s1[here, :], k1[here, :], h0[here, :] = new_t, new_s, new_k, heat
        l1[here, :], w0[here, :], v0[here, :] = l + g * v, w, v
        accs = tuple(
            pack_z(a, z, x, lane) for a, z in zip(accs, (new_t, new_s, new_k, heat))
        )
        return cur, nxt, accs

    prev = tuple(halo.x(f, 0) for f in range(3))
    cur = tuple(r[pl.ds(0, ny), :] for r in fields)
    accs = tuple(jnp.zeros((ny, LANES), F32) for _ in range(4))
    _, _, accs = lax.fori_loop(0, nx, plane, (prev, cur, accs), unroll=2)
    put_faces(dims, counts, (t1, s1, k1, h0), outs, accs)


def second_step_kernel(dims, counts, *refs):
    nx, ny = dims
    ngot = sum(swaps(n) for n in counts)
    nface = len(face_shapes(dims, counts, 2))
    t_ref, s_ref, k_ref, h_ref, l_ref, w_ref, v_ref, g_ref, r_ref = refs[:9]
    got = refs[9 : 9 + ngot]
    mt_ref, ms_ref, sense_ref, sums_ref = refs[9 + ngot : 13 + ngot]
    outs = split_faces(refs[13 + ngot : 13 + ngot + nface], counts)
    scratch = refs[13 + ngot + nface :]
    a, b = swaps(counts[0]), swaps(counts[1])
    halo = Halo(dims, counts, 4, (got[:a], got[a : a + b], got[a + b :]), scratch)
    row, lane = grid_iota(ny)
    fields = (t_ref, s_ref, k_ref, h_ref)

    def plane(x, carry):
        prev, cur, accs, sums = carry
        here = pl.ds(x * ny, ny)
        ahead = pl.ds(jnp.minimum(x + 1, nx - 1) * ny, ny)
        nxt = tuple(
            jnp.where(x == nx - 1, halo.x(f, 1), r[ahead, :]) for f, r in enumerate(fields)
        )
        near = [
            [prev[f], nxt[f]]
            + around(cur[f], halo.y(f, 0, x), halo.y(f, 1, x), halo.z(f, x), row, lane)
            for f in range(4)
        ]
        t, s, k, h = cur
        heat = again = None
        for tn, kn, hn in zip(near[0], near[2], near[3]):
            both = k + kn
            term, other = both * (tn - t), both * (hn - h)
            heat = term if heat is None else heat + term
            again = other if again is None else again + other
        heat = 0.5 * heat
        diff = near[1][0]
        for sn in near[1][1:]:
            diff = diff + sn
        diff = diff - 6.0 * s
        g, l = g_ref[here, :], l_ref[here, :]
        w, v = w_ref[here, :], v_ref[here, :]
        soft, slope = softplus_parts(SOLIDIFY_POINT - LOWERING_COEF * s - t)
        speed = g * soft
        frost = speed * l
        miss_t = (
            t + WARMTH_ADVANCE * heat + HIDDEN_WARMTH * frost - r_ref[0, here, :].astype(F32)
        )
        miss_s = s + STEP_SOLUTE * diff + REJECT * frost - r_ref[1, here, :].astype(F32)
        pull = HIDDEN_WARMTH * miss_t + REJECT * miss_s
        by_speed = pull * l
        below = by_speed * g * slope
        part_t = miss_t - below
        part_s = miss_s - LOWERING_COEF * below
        pull_0 = HIDDEN_WARMTH * part_t + REJECT * part_s
        mt_ref[here, :], ms_ref[here, :] = miss_t, miss_s
        sense_ref[here, :] = by_speed * soft + pull_0 * w + speed * pull * v
        misfit, part = sums
        misfit = misfit + (miss_t * miss_t + miss_s * miss_s)
        part = part + (
            miss_t * heat + part_t * h + (0.5 * WARMTH_ADVANCE) * miss_t * again
        )
        accs = tuple(pack_z(a, z, x, lane) for a, z in zip(accs, (miss_t, miss_s)))
        return cur, nxt, accs, (misfit, part)

    zero = jnp.zeros((ny, LANES), F32)
    prev = tuple(halo.x(f, 0) for f in range(4))
    cur = tuple(r[pl.ds(0, ny), :] for r in fields)
    _, _, accs, (misfit, part) = lax.fori_loop(
        0, nx, plane, (prev, cur, (zero, zero), (zero, zero)), unroll=2
    )
    put_faces(dims, counts, (mt_ref, ms_ref), outs, accs)
    lane_row = lax.broadcasted_iota(jnp.int32, (1, LANES), 1)
    line = jnp.where(lane_row == 0, 0.5 * jnp.sum(misfit), 0.0)
    line = jnp.where(lane_row == 1, WARMTH_ADVANCE * jnp.sum(part), line)
    sums_ref[...] = jnp.broadcast_to(line, sums_ref.shape)


def finish_kernel(dims, counts, cells, *refs):
    nx, ny = dims
    ngot = sum(swaps(n) for n in counts)
    t_ref, k_ref, mt_ref, ms_ref, w_ref, sense_ref, sums_ref = refs[:7]
    old = refs[7 : 7 + ngot]
    got = refs[7 + ngot : 7 + 2 * ngot]
    out_ref, misfit_ref, gradient_ref = refs[7 + 2 * ngot : 10 + 2 * ngot]
    scratch = refs[10 + 2 * ngot :]
    a, b = swaps(counts[0]), swaps(counts[1])
    before = Halo(dims, counts, 4, (old[:a], old[a : a + b], old[a + b :]), scratch[:3])
    halo = Halo(dims, counts, 2, (got[:a], got[a : a + b], got[a + b :]), scratch[3:])
    row, lane = grid_iota(ny)

    def edge(call):
        return 0.5 * call(before, 2) - call(before, 0), call(halo, 0), call(halo, 1)

    def load(here):
        return 0.5 * k_ref[here, :] - t_ref[here, :], mt_ref[here, :], ms_ref[here, :]

    def plane(x, carry):
        prev, cur = carry
        here = pl.ds(x * ny, ny)
        ahead = pl.ds(jnp.minimum(x + 1, nx - 1) * ny, ny)
        last = edge(lambda u, f: u.x(f, 1))
        nxt = tuple(jnp.where(x == nx - 1, e, v) for e, v in zip(last, load(ahead)))
        ym = edge(lambda u, f: u.y(f, 0, x))
        yp = edge(lambda u, f: u.y(f, 1, x))
        zr = edge(lambda u, f: u.z(f, x))
        near = [
            [prev[f], nxt[f]] + around(cur[f], ym[f], yp[f], zr[f], row, lane) for f in range(3)
        ]
        _, mt, ms = cur
        own = 0.5 * k_ref[here, :] + t_ref[here, :]
        flux = diff = None
        for qn, tn, sn in zip(*near):
            term = (tn - mt) * (own + qn)
            flux = term if flux is None else flux + term
            diff = sn if diff is None else diff + sn
        diff = diff - 6.0 * ms
        total = (0.5 * WARMTH_ADVANCE) * flux + (REJECT * STEP_SOLUTE) * diff
        out_ref[here, :] = sense_ref[here, :] + w_ref[here, :] * total
        return cur, nxt

    prev = edge(lambda u, f: u.x(f, 0))
    lax.fori_loop(0, nx, plane, (prev, load(pl.ds(0, ny))), unroll=2)
    sums = sums_ref[...]
    which = lax.broadcasted_iota(jnp.int32, sums.shape, 1)
    misfit_ref[0, 0] = jnp.sum(jnp.where(which == 0, sums, 0.0)) / cells
    gradient_ref[0, 0] = jnp.sum(jnp.where(which == 1, sums, 0.0)) / cells


VM = pl.BlockSpec(memory_space=pltpu.VMEM)
SM = pl.BlockSpec(memory_space=pltpu.SMEM)


def call(kernel, out, args, scratch=(), in_specs=None, out_specs=None, name=None):
    return pl.pallas_call(
        kernel,
        out_shape=[jax.ShapeDtypeStruct(s, d) for s, d in out],
        in_specs=in_specs or [VM] * len(args),
        out_specs=out_specs or [VM] * len(out),
        scratch_shapes=list(scratch),
        name=name,
        compiler_params=pltpu.CompilerParams(vmem_limit_bytes=32 << 20),
    )(*args)


def per_device(counts, warmth, sugar, population, coefficient, sensors):
    nx, ny, nz = warmth.shape
    assert nz == LANES and 2 * nx <= LANES
    bins = population.shape[0]
    dims = (nx, ny)
    cells = nx * ny
    t, s, g = [v.reshape(cells, nz) for v in (warmth, sugar, coefficient)]
    c = population.reshape(bins, cells, nz)
    r = sensors.reshape(2, cells, nz)
    field = ((cells, nz), F32)
    hbm = pl.BlockSpec(memory_space=pl.ANY)

    chunks = 8
    out = [field] * 5 + face_shapes(dims, counts, 3)
    res = call(
        functools.partial(prepare_kernel, dims, counts, bins, chunks),
        out,
        (c, t, s),
        [pltpu.VMEM((bins, cells, nz), F32), pltpu.SemaphoreType.DMA((chunks + 2,))],
        in_specs=[hbm] * 3,
        name="prepare",
    )
    k, l, m, t, s = res[:5]
    got = send_faces(res[5:], counts)

    out = [field] * 7 + face_shapes(dims, counts, 4)
    res = call(
        functools.partial(first_step_kernel, dims, counts),
        out,
        (t, s, g, k, l, m, *got),
        halo_scratch(dims, 3),
        name="first_step",
    )
    t1, s1, k1, h0, l1, w0, v0 = res[:7]
    got1 = send_faces(res[7:], counts)

    devices = int(np.prod(counts))
    out = [field] * 3 + [((devices, LANES), F32)] + face_shapes(dims, counts, 2)
    res = call(
        functools.partial(second_step_kernel, dims, counts),
        out,
        (t1, s1, k1, h0, l1, w0, v0, g, r, *got1),
        halo_scratch(dims, 4),
        name="second_step",
    )
    mt, ms, sense, sums = res[:4]
    got2 = send_faces(res[4:], counts)
    sums = lax.all_to_all(sums, AXES, 0, 0, tiled=True)

    sens, misfit, gradient = call(
        functools.partial(finish_kernel, dims, counts, float(cells * nz * devices)),
        [field, ((1, 1), F32), ((1, 1), F32)],
        (t1, k1, mt, ms, w0, sense, sums, *got1, *got2),
        halo_scratch(dims, 4) + halo_scratch(dims, 2),
        out_specs=[VM, SM, SM],
        name="finish",
    )
    return sens.reshape(nx, ny, nz), misfit.reshape(()), gradient.reshape(())


def solution(mesh):
    counts = tuple(mesh.shape[a] for a in AXES)
    placed = (
        P("gx", "gy", "gz"),
        P("gx", "gy", "gz"),
        P(None, "gx", "gy", "gz"),
        P("gx", "gy", "gz"),
        P(None, "gx", "gy", "gz"),
    )
    return jax.shard_map(
        functools.partial(per_device, counts),
        mesh=mesh,
        in_specs=placed,
        out_specs=(P("gx", "gy", "gz"), P(), P()),
        check_vma=False,
    )
```

```python
import functools

import jax
import jax.numpy as jnp
import numpy as np
from jax import lax
from jax.experimental import pallas as pl
from jax.experimental.pallas import tpu as pltpu
from jax.sharding import PartitionSpec as P

F32 = jnp.float32
AXES = ("gx", "gy", "gz")

SOLIDIFY_POINT = 0.5
LOWERING_COEF = 0.5
GROW = 0.3
NUCLEATE = 0.2
VOLUME = 0.005
WARMTH_ADVANCE = 0.08
STEP_SOLUTE = 0.1
HIDDEN_WARMTH = 0.5
REJECT = 0.3
LANES = 128


def volumes(bin_count):
    rank = np.arange(bin_count, dtype=np.float64) + 1.0
    return VOLUME * rank * rank


def functional_weights(bin_count):
    vol = volumes(bin_count)
    step = vol[1:] - vol[:-1]
    k = (1.0, vol)
    l = (NUCLEATE * vol[0], np.concatenate([GROW * step, [0.0]]))
    m_const = GROW * step[0] * NUCLEATE
    m = np.zeros(bin_count)
    for b in range(bin_count - 1):
        m[b] -= GROW * step[b] * GROW
        if b >= 1:
            m[b - 1] += GROW * step[b] * GROW
    return k, l, (m_const, m)


def swap_pairs(count, kind):
    if kind == 0:
        return [(i, i ^ 1) for i in range(count)]
    return [(i, (i + 1) % count if i % 2 else (i - 1) % count) for i in range(count)]


def swaps(count):
    return {1: 0, 2: 1}.get(count, 2)


def exchange(payloads, axis):
    count = lax.axis_size(axis)
    assert count == 1 or count % 2 == 0
    return [lax.ppermute(p, axis, swap_pairs(count, kind)) for kind, p in enumerate(payloads)]


class Side:
    def __init__(self, axis, count):
        self.count = count
        self.index = lax.axis_index(axis)
        self.odd = lax.rem(self.index, 2) == 1

    def outgoing(self, first, last):
        kinds = [jnp.where(self.odd, first, last), jnp.where(self.odd, last, first)]
        return kinds[: swaps(self.count)]

    def incoming(self, got):
        if self.count == 1:
            return None
        if self.count == 2:
            zero = jnp.zeros_like(got[0])
            return jnp.where(self.odd, got[0], zero), jnp.where(self.odd, zero, got[0])
        a, b = got
        zero = jnp.zeros_like(a)
        before = jnp.where(self.index > 0, jnp.where(self.odd, a, b), zero)
        after = jnp.where(self.index < self.count - 1, jnp.where(self.odd, b, a), zero)
        return before, after


def grid_iota(ny):
    row = lax.broadcasted_iota(jnp.int32, (ny, LANES), 0)
    lane = lax.broadcasted_iota(jnp.int32, (ny, LANES), 1)
    return row, lane


def pack_z(acc, value, x, lane):
    high = pltpu.roll(value, lax.rem(2 * x + 1, LANES), 1)
    low = pltpu.roll(value, lax.rem(2 * x + LANES - 1, LANES), 1)
    acc = jnp.where(lane == 2 * x, high, acc)
    return jnp.where(lane == lax.rem(2 * x + LANES - 1, LANES), low, acc)


class Halo:
    def __init__(self, dims, counts, fields, got, scratch):
        self.nx, self.ny = dims
        self.fields = fields
        self.xs, self.ys, self.zs = scratch
        nx, ny = dims
        gx, gy, gz = got
        sx, sy, sz = [Side(a, n) for a, n in zip(AXES, counts)]
        before, after = sx.incoming([r[...] for r in gx])
        self.xs[0], self.xs[1] = before, after
        before, after = sy.incoming([r[...] for r in gy])
        self.ys[0], self.ys[1] = before, after
        before, after = sz.incoming([r[...] for r in gz])
        lane = lax.broadcasted_iota(jnp.int32, before.shape, 1)
        self.zs[...] = jnp.where(lax.rem(lane, 2) == 0, before, after)

    def x(self, f, side):
        return self.xs[side, pl.ds(f * self.ny, self.ny), :]

    def y(self, f, side, x):
        return self.ys[side, pl.ds(f * self.nx + x, 1), :]

    def z(self, f, x):
        packed = self.zs[pl.ds(f * self.ny, self.ny), :]
        return pltpu.roll(packed, lax.rem(LANES - 2 * x + LANES, LANES), 1)


def halo_scratch(dims, fields):
    nx, ny = dims
    return [
        pltpu.VMEM((2, fields * ny, LANES), F32),
        pltpu.VMEM((2, fields * nx, LANES), F32),
        pltpu.VMEM((fields * ny, LANES), F32),
    ]


def around(cur, ym, yp, zr, row, lane):
    ny = cur.shape[0]
    return [
        jnp.where(row == 0, ym, pltpu.roll(cur, 1, 0)),
        jnp.where(row == ny - 1, yp, pltpu.roll(cur, ny - 1, 0)),
        jnp.where(lane == 0, zr, pltpu.roll(cur, 1, 1)),
        jnp.where(lane == LANES - 1, zr, pltpu.roll(cur, LANES - 1, 1)),
    ]


def put_faces(dims, counts, fields, outs, zaccs):
    nx, ny = dims
    ox, oy, oz = outs
    sx, sy, _ = [Side(a, n) for a, n in zip(AXES, counts)]
    for f, ref in enumerate(fields):
        first, last = ref[pl.ds(0, ny), :], ref[pl.ds((nx - 1) * ny, ny), :]
        for o, v in zip(ox, sx.outgoing(first, last)):
            o[pl.ds(f * ny, ny), :] = v
        first = ref[pl.ds(0, nx, stride=ny), :]
        last = ref[pl.ds(ny - 1, nx, stride=ny), :]
        for o, v in zip(oy, sy.outgoing(first, last)):
            o[pl.ds(f * nx, nx), :] = v
        for o in oz:
            o[pl.ds(f * ny, ny), :] = zaccs[f]


def face_shapes(dims, counts, fields):
    nx, ny = dims
    rows = (fields * ny, fields * nx, fields * ny)
    shapes = []
    for axis, (r, n) in enumerate(zip(rows, counts)):
        copies = min(swaps(n), 1) if axis == 2 else swaps(n)
        shapes += [((r, LANES), F32)] * copies
    return shapes


def split_faces(refs, counts):
    ax, ay = swaps(counts[0]), swaps(counts[1])
    return refs[:ax], refs[ax : ax + ay], refs[ax + ay :]


def send_faces(faces, counts):
    ox, oy, oz = split_faces(list(faces), counts)
    oz = [oz[0]] * swaps(counts[2])
    got = []
    for payload, axis in zip((ox, oy, oz), AXES):
        got += exchange(payload, axis)
    return got


def log1p_of(e, u, inv):
    return jnp.log(u) + (e - (u - 1.0)) * inv


def softplus_parts(v):
    e = jnp.exp(-jnp.abs(v))
    u = 1.0 + e
    inv = 1.0 / u
    soft = jnp.maximum(v, 0.0) + log1p_of(e, u, inv)
    return soft, jnp.where(v >= 0, inv, e * inv)


def prepare_kernel(dims, counts, bins, chunks, *refs):
    nx, ny = dims
    nface = len(face_shapes(dims, counts, 3))
    c_hbm, t_hbm, s_hbm = refs[:3]
    k_ref, l_ref, m_ref, t_ref, s_ref = refs[3:8]
    outs = split_faces(refs[8 : 8 + nface], counts)
    c_ref, sems = refs[8 + nface :]
    rows = nx * ny // chunks
    copies = [
        pltpu.make_async_copy(t_hbm, t_ref, sems.at[chunks]),
        pltpu.make_async_copy(s_hbm, s_ref, sems.at[chunks + 1]),
    ]
    for j in range(chunks):
        part = pl.ds(j * rows, rows)
        copies.append(pltpu.make_async_copy(c_hbm.at[:, part, :], c_ref.at[:, part, :], sems.at[j]))
    for copy in copies:
        copy.start()
    copies[0].wait()
    copies[1].wait()
    _, lane = grid_iota(ny)
    weights = functional_weights(bins)

    def plane(x, accs):
        here = pl.ds(x * ny, ny)
        c = [c_ref[b, here, :] for b in range(bins)]
        values = []
        for const, per_bin in weights:
            total = None
            for b in range(bins):
                if per_bin[b] != 0.0:
                    term = float(per_bin[b]) * c[b]
                    total = term if total is None else total + term
            values.append(float(const) + total)
        k_ref[here, :], l_ref[here, :], m_ref[here, :] = values
        faces = (t_ref[here, :], s_ref[here, :], values[0])
        return tuple(pack_z(a, v, x, lane) for a, v in zip(accs, faces))

    accs = tuple(jnp.zeros((ny, LANES), F32) for _ in range(3))
    planes = nx // chunks
    for j in range(chunks):
        copies[2 + j].wait()
        accs = lax.fori_loop(j * planes, (j + 1) * planes, plane, accs, unroll=8)
    put_faces(dims, counts, (t_ref, s_ref, k_ref), outs, accs)


def first_step_kernel(dims, counts, *refs):
    nx, ny = dims
    ngot = sum(swaps(n) for n in counts)
    nface = len(face_shapes(dims, counts, 4))
    t_ref, s_ref, g_ref, k_ref, l_ref, m_ref = refs[:6]
    got = refs[6 : 6 + ngot]
    t1, s1, k1, h0, l1, w0, v0 = refs[6 + ngot : 13 + ngot]
    outs = split_faces(refs[13 + ngot : 13 + ngot + nface], counts)
    scratch = refs[13 + ngot + nface :]
    a, b = swaps(counts[0]), swaps(counts[1])
    halo = Halo(dims, counts, 3, (got[:a], got[a : a + b], got[a + b :]), scratch)
    row, lane = grid_iota(ny)
    fields = (t_ref, s_ref, k_ref)

    def plane(x, carry):
        prev, cur, accs = carry
        here = pl.ds(x * ny, ny)
        ahead = pl.ds(jnp.minimum(x + 1, nx - 1) * ny, ny)
        nxt = tuple(
            jnp.where(x == nx - 1, halo.x(f, 1), r[ahead, :]) for f, r in enumerate(fields)
        )
        near = [
            [prev[f], nxt[f]]
            + around(cur[f], halo.y(f, 0, x), halo.y(f, 1, x), halo.z(f, x), row, lane)
            for f in range(3)
        ]
        t, s, k = cur
        heat = None
        for tn, kn in zip(near[0], near[2]):
            term = (k + kn) * (tn - t)
            heat = term if heat is None else heat + term
        heat = 0.5 * heat
        diff = near[1][0]
        for sn in near[1][1:]:
            diff = diff + sn
        diff = diff - 6.0 * s
        g, l, m = g_ref[here, :], l_ref[here, :], m_ref[here, :]
        soft, _ = softplus_parts(SOLIDIFY_POINT - LOWERING_COEF * s - t)
        w, v = soft * l, soft * m
        frost = g * w
        new_t = t + WARMTH_ADVANCE * heat + HIDDEN_WARMTH * frost
        new_s = s + STEP_SOLUTE * diff + REJECT * frost
        new_k = k + frost
        t1[here, :], s1[here, :], k1[here, :], h0[here, :] = new_t, new_s, new_k, heat
        l1[here, :], w0[here, :], v0[here, :] = l + g * v, w, v
        accs = tuple(
            pack_z(a, z, x, lane) for a, z in zip(accs, (new_t, new_s, new_k, heat))
        )
        return cur, nxt, accs

    prev = tuple(halo.x(f, 0) for f in range(3))
    cur = tuple(r[pl.ds(0, ny), :] for r in fields)
    accs = tuple(jnp.zeros((ny, LANES), F32) for _ in range(4))
    _, _, accs = lax.fori_loop(0, nx, plane, (prev, cur, accs), unroll=4)
    put_faces(dims, counts, (t1, s1, k1, h0), outs, accs)


def second_step_kernel(dims, counts, *refs):
    nx, ny = dims
    ngot = sum(swaps(n) for n in counts)
    nface = len(face_shapes(dims, counts, 2))
    t_ref, s_ref, k_ref, h_ref, l_ref, w_ref, v_ref, g_ref, r_ref = refs[:9]
    got = refs[9 : 9 + ngot]
    mt_ref, ms_ref, sense_ref, sums_ref = refs[9 + ngot : 13 + ngot]
    outs = split_faces(refs[13 + ngot : 13 + ngot + nface], counts)
    scratch = refs[13 + ngot + nface :]
    a, b = swaps(counts[0]), swaps(counts[1])
    halo = Halo(dims, counts, 4, (got[:a], got[a : a + b], got[a + b :]), scratch)
    row, lane = grid_iota(ny)
    fields = (t_ref, s_ref, k_ref, h_ref)

    def plane(x, carry):
        prev, cur, accs, sums = carry
        here = pl.ds(x * ny, ny)
        ahead = pl.ds(jnp.minimum(x + 1, nx - 1) * ny, ny)
        nxt = tuple(
            jnp.where(x == nx - 1, halo.x(f, 1), r[ahead, :]) for f, r in enumerate(fields)
        )
        near = [
            [prev[f], nxt[f]]
            + around(cur[f], halo.y(f, 0, x), halo.y(f, 1, x), halo.z(f, x), row, lane)
            for f in range(4)
        ]
        t, s, k, h = cur
        heat = again = None
        for tn, kn, hn in zip(near[0], near[2], near[3]):
            both = k + kn
            term, other = both * (tn - t), both * (hn - h)
            heat = term if heat is None else heat + term
            again = other if again is None else again + other
        heat = 0.5 * heat
        diff = near[1][0]
        for sn in near[1][1:]:
            diff = diff + sn
        diff = diff - 6.0 * s
        g, l = g_ref[here, :], l_ref[here, :]
        w, v = w_ref[here, :], v_ref[here, :]
        soft, slope = softplus_parts(SOLIDIFY_POINT - LOWERING_COEF * s - t)
        speed = g * soft
        frost = speed * l
        miss_t = (
            t + WARMTH_ADVANCE * heat + HIDDEN_WARMTH * frost - r_ref[0, here, :].astype(F32)
        )
        miss_s = s + STEP_SOLUTE * diff + REJECT * frost - r_ref[1, here, :].astype(F32)
        pull = HIDDEN_WARMTH * miss_t + REJECT * miss_s
        by_speed = pull * l
        below = by_speed * g * slope
        part_t = miss_t - below
        part_s = miss_s - LOWERING_COEF * below
        pull_0 = HIDDEN_WARMTH * part_t + REJECT * part_s
        mt_ref[here, :], ms_ref[here, :] = miss_t, miss_s
        sense_ref[here, :] = by_speed * soft + pull_0 * w + speed * pull * v
        misfit, part = sums
        misfit = misfit + (miss_t * miss_t + miss_s * miss_s)
        part = part + (
            miss_t * heat + part_t * h + (0.5 * WARMTH_ADVANCE) * miss_t * again
        )
        accs = tuple(pack_z(a, z, x, lane) for a, z in zip(accs, (miss_t, miss_s)))
        return cur, nxt, accs, (misfit, part)

    zero = jnp.zeros((ny, LANES), F32)
    prev = tuple(halo.x(f, 0) for f in range(4))
    cur = tuple(r[pl.ds(0, ny), :] for r in fields)
    _, _, accs, (misfit, part) = lax.fori_loop(
        0, nx, plane, (prev, cur, (zero, zero), (zero, zero)), unroll=4
    )
    put_faces(dims, counts, (mt_ref, ms_ref), outs, accs)
    lane_row = lax.broadcasted_iota(jnp.int32, (1, LANES), 1)
    line = jnp.where(lane_row == 0, 0.5 * jnp.sum(misfit), 0.0)
    line = jnp.where(lane_row == 1, WARMTH_ADVANCE * jnp.sum(part), line)
    sums_ref[...] = jnp.broadcast_to(line, sums_ref.shape)


def finish_kernel(dims, counts, cells, *refs):
    nx, ny = dims
    ngot = sum(swaps(n) for n in counts)
    t_ref, k_ref, mt_ref, ms_ref, w_ref, sense_ref, sums_ref = refs[:7]
    old = refs[7 : 7 + ngot]
    got = refs[7 + ngot : 7 + 2 * ngot]
    out_ref, misfit_ref, gradient_ref = refs[7 + 2 * ngot : 10 + 2 * ngot]
    scratch = refs[10 + 2 * ngot :]
    a, b = swaps(counts[0]), swaps(counts[1])
    before = Halo(dims, counts, 4, (old[:a], old[a : a + b], old[a + b :]), scratch[:3])
    halo = Halo(dims, counts, 2, (got[:a], got[a : a + b], got[a + b :]), scratch[3:])
    row, lane = grid_iota(ny)

    def edge(call):
        return 0.5 * call(before, 2) - call(before, 0), call(halo, 0), call(halo, 1)

    def load(here):
        return 0.5 * k_ref[here, :] - t_ref[here, :], mt_ref[here, :], ms_ref[here, :]

    def plane(x, carry):
        prev, cur = carry
        here = pl.ds(x * ny, ny)
        ahead = pl.ds(jnp.minimum(x + 1, nx - 1) * ny, ny)
        last = edge(lambda u, f: u.x(f, 1))
        nxt = tuple(jnp.where(x == nx - 1, e, v) for e, v in zip(last, load(ahead)))
        ym = edge(lambda u, f: u.y(f, 0, x))
        yp = edge(lambda u, f: u.y(f, 1, x))
        zr = edge(lambda u, f: u.z(f, x))
        near = [
            [prev[f], nxt[f]] + around(cur[f], ym[f], yp[f], zr[f], row, lane) for f in range(3)
        ]
        _, mt, ms = cur
        own = 0.5 * k_ref[here, :] + t_ref[here, :]
        flux = diff = None
        for qn, tn, sn in zip(*near):
            term = (tn - mt) * (own + qn)
            flux = term if flux is None else flux + term
            diff = sn if diff is None else diff + sn
        diff = diff - 6.0 * ms
        total = (0.5 * WARMTH_ADVANCE) * flux + (REJECT * STEP_SOLUTE) * diff
        out_ref[here, :] = sense_ref[here, :] + w_ref[here, :] * total
        return cur, nxt

    prev = edge(lambda u, f: u.x(f, 0))
    lax.fori_loop(0, nx, plane, (prev, load(pl.ds(0, ny))), unroll=8)
    sums = sums_ref[...]
    which = lax.broadcasted_iota(jnp.int32, sums.shape, 1)
    misfit_ref[0, 0] = jnp.sum(jnp.where(which == 0, sums, 0.0)) / cells
    gradient_ref[0, 0] = jnp.sum(jnp.where(which == 1, sums, 0.0)) / cells


VM = pl.BlockSpec(memory_space=pltpu.VMEM)
SM = pl.BlockSpec(memory_space=pltpu.SMEM)


def call(kernel, out, args, scratch=(), in_specs=None, out_specs=None, name=None, vmem=32):
    return pl.pallas_call(
        kernel,
        out_shape=[jax.ShapeDtypeStruct(s, d) for s, d in out],
        in_specs=in_specs or [VM] * len(args),
        out_specs=out_specs or [VM] * len(out),
        scratch_shapes=list(scratch),
        name=name,
        compiler_params=pltpu.CompilerParams(vmem_limit_bytes=vmem << 20),
    )(*args)


def per_device(counts, warmth, sugar, population, coefficient, sensors):
    nx, ny, nz = warmth.shape
    assert nz == LANES and 2 * nx <= LANES
    bins = population.shape[0]
    dims = (nx, ny)
    cells = nx * ny
    t, s, g = [v.reshape(cells, nz) for v in (warmth, sugar, coefficient)]
    c = population.reshape(bins, cells, nz)
    r = sensors.reshape(2, cells, nz)
    field = ((cells, nz), F32)
    hbm = pl.BlockSpec(memory_space=pl.ANY)

    chunks = 8
    out = [field] * 5 + face_shapes(dims, counts, 3)
    res = call(
        functools.partial(prepare_kernel, dims, counts, bins, chunks),
        out,
        (c, t, s),
        [pltpu.VMEM((bins, cells, nz), F32), pltpu.SemaphoreType.DMA((chunks + 2,))],
        in_specs=[hbm] * 3,
        name="prepare",
        vmem=51,
    )
    k, l, m, t, s = res[:5]
    got = send_faces(res[5:], counts)

    out = [field] * 7 + face_shapes(dims, counts, 4)
    res = call(
        functools.partial(first_step_kernel, dims, counts),
        out,
        (t, s, g, k, l, m, *got),
        halo_scratch(dims, 3),
        name="first_step",
    )
    t1, s1, k1, h0, l1, w0, v0 = res[:7]
    got1 = send_faces(res[7:], counts)

    devices = int(np.prod(counts))
    out = [field] * 3 + [((devices, LANES), F32)] + face_shapes(dims, counts, 2)
    res = call(
        functools.partial(second_step_kernel, dims, counts),
        out,
        (t1, s1, k1, h0, l1, w0, v0, g, r, *got1),
        halo_scratch(dims, 4),
        name="second_step",
    )
    mt, ms, sense, sums = res[:4]
    got2 = send_faces(res[4:], counts)
    sums = lax.all_to_all(sums, AXES, 0, 0, tiled=True)

    sens, misfit, gradient = call(
        functools.partial(finish_kernel, dims, counts, float(cells * nz * devices)),
        [field, ((1, 1), F32), ((1, 1), F32)],
        (t1, k1, mt, ms, w0, sense, sums, *got1, *got2),
        halo_scratch(dims, 4) + halo_scratch(dims, 2),
        out_specs=[VM, SM, SM],
        name="finish",
    )
    return sens.reshape(nx, ny, nz), misfit.reshape(()), gradient.reshape(())


def solution(mesh):
    counts = tuple(mesh.shape[a] for a in AXES)
    placed = (
        P("gx", "gy", "gz"),
        P("gx", "gy", "gz"),
        P(None, "gx", "gy", "gz"),
        P("gx", "gy", "gz"),
        P(None, "gx", "gy", "gz"),
    )
    return jax.shard_map(
        functools.partial(per_device, counts),
        mesh=mesh,
        in_specs=placed,
        out_specs=(P("gx", "gy", "gz"), P(), P()),
        check_vma=False,
    )
```

```python
import functools

import jax
import jax.numpy as jnp
import numpy as np
from jax import lax
from jax.experimental import pallas as pl
from jax.experimental.pallas import tpu as pltpu
from jax.sharding import PartitionSpec as P

F32 = jnp.float32
AXES = ("gx", "gy", "gz")

SOLIDIFY_POINT = 0.5
LOWERING_COEF = 0.5
GROW = 0.3
NUCLEATE = 0.2
VOLUME = 0.005
WARMTH_ADVANCE = 0.08
STEP_SOLUTE = 0.1
HIDDEN_WARMTH = 0.5
REJECT = 0.3
LANES = 128


def volumes(bin_count):
    rank = np.arange(bin_count, dtype=np.float64) + 1.0
    return VOLUME * rank * rank


def functional_weights(bin_count):
    vol = volumes(bin_count)
    step = vol[1:] - vol[:-1]
    k = (1.0, vol)
    l = (NUCLEATE * vol[0], np.concatenate([GROW * step, [0.0]]))
    m_const = GROW * step[0] * NUCLEATE
    m = np.zeros(bin_count)
    for b in range(bin_count - 1):
        m[b] -= GROW * step[b] * GROW
        if b >= 1:
            m[b - 1] += GROW * step[b] * GROW
    return k, l, (m_const, m)


def swap_pairs(count, kind):
    if kind == 0:
        return [(i, i ^ 1) for i in range(count)]
    return [(i, (i + 1) % count if i % 2 else (i - 1) % count) for i in range(count)]


def swaps(count):
    return {1: 0, 2: 1}.get(count, 2)


def exchange(payloads, axis):
    count = lax.axis_size(axis)
    assert count == 1 or count % 2 == 0
    return [lax.ppermute(p, axis, swap_pairs(count, kind)) for kind, p in enumerate(payloads)]


class Side:
    def __init__(self, axis, count):
        self.count = count
        self.index = lax.axis_index(axis)
        self.odd = lax.rem(self.index, 2) == 1

    def outgoing(self, first, last):
        kinds = [jnp.where(self.odd, first, last), jnp.where(self.odd, last, first)]
        return kinds[: swaps(self.count)]

    def incoming(self, got):
        if self.count == 1:
            return None
        if self.count == 2:
            zero = jnp.zeros_like(got[0])
            return jnp.where(self.odd, got[0], zero), jnp.where(self.odd, zero, got[0])
        a, b = got
        zero = jnp.zeros_like(a)
        before = jnp.where(self.index > 0, jnp.where(self.odd, a, b), zero)
        after = jnp.where(self.index < self.count - 1, jnp.where(self.odd, b, a), zero)
        return before, after


def grid_iota(ny):
    row = lax.broadcasted_iota(jnp.int32, (ny, LANES), 0)
    lane = lax.broadcasted_iota(jnp.int32, (ny, LANES), 1)
    return row, lane


def pack_z(acc, value, x, lane):
    return jnp.where(lane // 2 == x, pltpu.roll(value, lax.rem(2 * x + 1, LANES), 1), acc)


class Faces:
    def __init__(self, dims, counts, own, got):
        self.nx, self.ny = dims
        self.sides = [Side(a, n) for a, n in zip(AXES, counts)]
        self.mine = own
        a, b = swaps(counts[0]), swaps(counts[1])
        self.got = (got[:a], got[a : a + b], got[a + b :])

    def _part(self, axis, f):
        rows = self.nx if axis == 1 else self.ny
        return pl.ds(f * rows, rows)

    def near(self, axis, f):
        part = [r[self._part(axis, f), :] for r in self.got[axis]]
        before, after = self.sides[axis].incoming(part)
        if axis < 2:
            return before, after
        lane = lax.broadcasted_iota(jnp.int32, before.shape, 1)
        return jnp.where(lax.rem(lane, 2) == 0, before, after)

    def own(self, axis, f):
        if axis < 2:
            return [self.mine[axis][side, self._part(axis, f), :] for side in (0, 1)]
        return turn_z(self.mine[2][self._part(2, f), :])


def turn_z(pack):
    lane = lax.broadcasted_iota(jnp.int32, pack.shape, 1)
    even = lax.rem(lane, 2) == 0
    return jnp.where(even, pltpu.roll(pack, LANES - 1, 1), pltpu.roll(pack, 1, 1))


class Own:
    def __init__(self, dims, counts, refs):
        self.nx, self.ny = dims
        self.counts = counts
        self.x, self.y, self.z = refs[:3]
        a = swaps(counts[0])
        self.out = (refs[3 : 3 + a], refs[3 + a :])

    def rows(self, f, x, value):
        self.y[0, pl.ds(f * self.nx + x, 1), :] = value[:1, :]
        self.y[1, pl.ds(f * self.nx + x, 1), :] = value[self.ny - 1 :, :]

    def finish(self, fields, packs):
        nx, ny = self.nx, self.ny
        for f, (ref, pack) in enumerate(zip(fields, packs)):
            part = pl.ds(f * ny, ny)
            self.x[0, part, :] = ref[pl.ds(0, ny), :]
            self.x[1, part, :] = ref[pl.ds((nx - 1) * ny, ny), :]
            self.z[part, :] = pack
        for axis, own in enumerate((self.x, self.y)):
            side = Side(AXES[axis], self.counts[axis])
            for o, v in zip(self.out[axis], side.outgoing(own[0], own[1])):
                o[...] = v


def own_shapes(dims, counts, fields):
    nx, ny = dims
    x, y = (fields * ny, LANES), (fields * nx, LANES)
    shapes = [(2, *x), (2, *y), x] + [x] * swaps(counts[0]) + [y] * swaps(counts[1])
    return [(v, F32) for v in shapes]


def send_faces(own, counts):
    a = swaps(counts[0])
    payloads = (own[3 : 3 + a], own[3 + a :], [own[2]] * swaps(counts[2]))
    got = []
    for payload, axis in zip(payloads, AXES):
        got += exchange(payload, axis)
    return got


def at_plane(x, nx, pair):
    return jnp.where(x == 0, pair[0], jnp.where(x == nx - 1, pair[1], 0.0))


def at_rows(x, ref, f, nx, row, ny):
    part = pl.ds(f * nx + x, 1)
    return jnp.where(row == 0, ref[0, part, :], jnp.where(row == ny - 1, ref[1, part, :], 0.0))


def ready_z(value):
    lane = lax.broadcasted_iota(jnp.int32, value.shape, 1)
    return jnp.where(lax.rem(lane, 2) == 0, value, pltpu.roll(value, LANES - 2, 1))


def unpack_z(value, x):
    return pltpu.roll(value, lax.rem(LANES - 2 * x, LANES), 1)


def half_flux(k, t, kn, tn):
    return 0.5 * (k + kn) * (tn - t)


def divergence(flux_up, axis, index):
    size = flux_up.shape[axis]
    flux_up = jnp.where(index == size - 1, 0.0, flux_up)
    return flux_up - pltpu.roll(flux_up, 1, axis)


def ahead(value, axis):
    return pltpu.roll(value, value.shape[axis] - 1, axis)


def neighbour_sum(value, axis, index):
    size = value.shape[axis]
    up = jnp.where(index == size - 1, 0.0, ahead(value, axis))
    return up + jnp.where(index == 0, 0.0, pltpu.roll(value, 1, axis))


def log1p_of(e, u, inv):
    return jnp.log(u) + (e - (u - 1.0)) * inv


def softplus_parts(v):
    e = jnp.exp(-jnp.abs(v))
    u = 1.0 + e
    inv = 1.0 / u
    soft = jnp.maximum(v, 0.0) + log1p_of(e, u, inv)
    return soft, jnp.where(v >= 0, inv, e * inv)


def prepare_kernel(dims, counts, bins, chunks, *refs):
    nx, ny = dims
    c_hbm, t_hbm, s_hbm = refs[:3]
    k_ref, l_ref, m_ref, t_ref, s_ref = refs[3:8]
    own = Own(dims, counts, refs[8:-2])
    c_ref, sems = refs[-2:]
    rows = nx * ny // chunks
    copies = [
        pltpu.make_async_copy(t_hbm, t_ref, sems.at[chunks]),
        pltpu.make_async_copy(s_hbm, s_ref, sems.at[chunks + 1]),
    ]
    for j in range(chunks):
        part = pl.ds(j * rows, rows)
        copies.append(pltpu.make_async_copy(c_hbm.at[:, part, :], c_ref.at[:, part, :], sems.at[j]))
    for copy in copies:
        copy.start()
    copies[0].wait()
    copies[1].wait()
    _, lane = grid_iota(ny)
    weights = functional_weights(bins)

    def plane(x, accs):
        here = pl.ds(x * ny, ny)
        c = [c_ref[b, here, :] for b in range(bins)]
        values = []
        for const, per_bin in weights:
            total = None
            for b in range(bins):
                if per_bin[b] != 0.0:
                    term = float(per_bin[b]) * c[b]
                    total = term if total is None else total + term
            values.append(float(const) + total)
        k_ref[here, :], l_ref[here, :], m_ref[here, :] = values
        faces = (t_ref[here, :], s_ref[here, :], values[0])
        for f, v in enumerate(faces):
            own.rows(f, x, v)
        return tuple(pack_z(a, v, x, lane) for a, v in zip(accs, faces))

    accs = tuple(jnp.zeros((ny, LANES), F32) for _ in range(3))
    planes = nx // chunks
    for j in range(chunks):
        copies[2 + j].wait()
        accs = lax.fori_loop(j * planes, (j + 1) * planes, plane, accs, unroll=8)
    own.finish((t_ref, s_ref, k_ref), accs)


def first_inner_kernel(dims, unroll, *refs):
    nx, ny = dims
    t_ref, s_ref, k_ref, l_ref, m_ref, g_ref = refs[:6]
    t1, s1, h0, k1, l1, w0, v0, kpack = refs[6:]
    row, lane = grid_iota(ny)

    def plane(x, carry):
        t, s, k, s_prev, flux_prev, acc = carry
        here = pl.ds(x * ny, ny)
        then = pl.ds(jnp.minimum(x + 1, nx - 1) * ny, ny)
        tn, sn, kn = t_ref[then, :], s_ref[then, :], k_ref[then, :]
        flux = half_flux(k, t, kn, tn)
        heat = (flux - flux_prev) + divergence(
            half_flux(k, t, ahead(k, 0), ahead(t, 0)), 0, row
        )
        heat = heat + divergence(half_flux(k, t, ahead(k, 1), ahead(t, 1)), 1, lane)
        s_next = jnp.where(x == nx - 1, 0.0, sn)
        diff = (s_prev + s_next) + neighbour_sum(s, 0, row)
        diff = diff + neighbour_sum(s, 1, lane) - 6.0 * s
        g, l, m = g_ref[here, :], l_ref[here, :], m_ref[here, :]
        soft, _ = softplus_parts(SOLIDIFY_POINT - LOWERING_COEF * s - t)
        w, v = soft * l, soft * m
        frost = g * w
        t1[here, :] = t + WARMTH_ADVANCE * heat + HIDDEN_WARMTH * frost
        s1[here, :] = s + STEP_SOLUTE * diff + REJECT * frost
        h0[here, :] = heat
        new_k = k + frost
        k1[here, :] = new_k
        l1[here, :], w0[here, :], v0[here, :] = l + g * v, w, v
        return tn, sn, kn, s, flux, pack_z(acc, new_k, x, lane)

    top = pl.ds(0, ny)
    zero = jnp.zeros((ny, LANES), F32)
    carry = (t_ref[top, :], s_ref[top, :], k_ref[top, :], zero, zero, zero)
    kpack[...] = lax.fori_loop(0, nx, plane, carry, unroll=unroll)[-1]


def first_edge_kernel(dims, counts, unroll, *refs):
    nx, ny = dims
    ngot = sum(swaps(n) for n in counts)
    tp_ref, sp_ref, hp_ref, k1_ref, kpack_ref = refs[:5]
    faces = Faces(dims, counts, refs[5:8], refs[8 : 8 + ngot])
    t1, s1, h0 = refs[8 + ngot : 11 + ngot]
    own = Own(dims, counts, refs[11 + ngot : -1])
    rows_ref = refs[-1]
    row, lane = grid_iota(ny)
    edge = (lane == 0) | (lane == LANES - 1)

    def flux_in(axis):
        tn, sn, kn = [faces.near(axis, f) for f in range(3)]
        to, ko = faces.own(axis, 0), faces.own(axis, 2)
        if axis == 2:
            return half_flux(ko, to, kn, tn), sn
        return [half_flux(*v) for v in zip(ko, to, kn, tn)], sn

    heat_x, sugar_x = flux_in(0)
    heat_y, sugar_y = flux_in(1)
    for side in (0, 1):
        rows_ref[side, pl.ds(0, nx), :] = heat_y[side]
        rows_ref[side, pl.ds(nx, nx), :] = sugar_y[side]
    heat_z, sugar_z = flux_in(2)
    in_heat, in_sugar = ready_z(heat_z), ready_z(sugar_z)

    def plane(x, accs):
        here = pl.ds(x * ny, ny)
        heat = at_plane(x, nx, heat_x) + at_rows(x, rows_ref, 0, nx, row, ny)
        diff = at_plane(x, nx, sugar_x) + at_rows(x, rows_ref, 1, nx, row, ny)
        some_t = tp_ref[here, :] + WARMTH_ADVANCE * heat
        some_s = sp_ref[here, :] + STEP_SOLUTE * diff
        some_h = hp_ref[here, :] + heat
        heat = jnp.where(edge, unpack_z(in_heat, x), 0.0)
        diff = jnp.where(edge, unpack_z(in_sugar, x), 0.0)
        new_t = some_t + WARMTH_ADVANCE * heat
        new_s = some_s + STEP_SOLUTE * diff
        new_h = some_h + heat
        t1[here, :], s1[here, :], h0[here, :] = new_t, new_s, new_h
        for f, v in enumerate((new_t, new_s, k1_ref[here, :], new_h)):
            own.rows(f, x, v)
        return tuple(pack_z(a, v, x, lane) for a, v in zip(accs, (some_t, some_s, some_h)))

    accs = tuple(jnp.zeros((ny, LANES), F32) for _ in range(3))
    accs = lax.fori_loop(0, nx, plane, accs, unroll=unroll)
    heat_z, sugar_z = turn_z(heat_z), turn_z(sugar_z)
    packs = (
        accs[0] + WARMTH_ADVANCE * heat_z,
        accs[1] + STEP_SOLUTE * sugar_z,
        kpack_ref[...],
        accs[2] + heat_z,
    )
    own.finish((t1, s1, k1_ref, h0), packs)


def second_inner_kernel(dims, unroll, *refs):
    nx, ny = dims
    t_ref, s_ref, k_ref, h_ref, l_ref, g_ref, r_ref = refs[:7]
    mt_ref, ms_ref, inner_ref, soft_ref, slope_ref = refs[7:]
    row, lane = grid_iota(ny)

    def plane(x, carry):
        t, s, k, h, s_prev, flux_prev, other_prev = carry
        here = pl.ds(x * ny, ny)
        then = pl.ds(jnp.minimum(x + 1, nx - 1) * ny, ny)
        tn, sn, kn, hn = t_ref[then, :], s_ref[then, :], k_ref[then, :], h_ref[then, :]
        both = 0.5 * (k + kn)
        flux, other = both * (tn - t), both * (hn - h)
        heat, again = flux - flux_prev, other - other_prev
        for axis, index in ((0, row), (1, lane)):
            both = 0.5 * (k + ahead(k, axis))
            heat = heat + divergence(both * (ahead(t, axis) - t), axis, index)
            again = again + divergence(both * (ahead(h, axis) - h), axis, index)
        s_next = jnp.where(x == nx - 1, 0.0, sn)
        diff = (s_prev + s_next) + neighbour_sum(s, 0, row)
        diff = diff + neighbour_sum(s, 1, lane) - 6.0 * s
        g, l = g_ref[here, :], l_ref[here, :]
        soft, slope = softplus_parts(SOLIDIFY_POINT - LOWERING_COEF * s - t)
        frost = g * soft * l
        mt_ref[here, :] = (
            t + WARMTH_ADVANCE * heat + HIDDEN_WARMTH * frost - r_ref[0, here, :].astype(F32)
        )
        ms_ref[here, :] = s + STEP_SOLUTE * diff + REJECT * frost - r_ref[1, here, :].astype(F32)
        inner_ref[here, :] = heat + WARMTH_ADVANCE * again
        soft_ref[here, :], slope_ref[here, :] = soft, slope
        return tn, sn, kn, hn, s, flux, other

    top = pl.ds(0, ny)
    zero = jnp.zeros((ny, LANES), F32)
    start = [r[top, :] for r in (t_ref, s_ref, k_ref, h_ref)]
    lax.fori_loop(0, nx, plane, (*start, zero, zero, zero), unroll=unroll)


def second_edge_kernel(dims, counts, unroll, *refs):
    nx, ny = dims
    ngot = sum(swaps(n) for n in counts)
    h_ref, l_ref, w_ref, v_ref, g_ref = refs[:5]
    mtp_ref, msp_ref, inner_ref, soft_ref, slope_ref = refs[5:10]
    faces = Faces(dims, counts, refs[10:13], refs[13 : 13 + ngot])
    mt_ref, ms_ref, sense_ref, sums_ref = refs[13 + ngot : 17 + ngot]
    meet = refs[17 + ngot : 20 + ngot]
    own = Own(dims, counts, refs[20 + ngot : -1])
    rows_ref = refs[-1]
    row, lane = grid_iota(ny)
    edge = (lane == 0) | (lane == LANES - 1)

    def flux_in(axis):
        tn, sn, kn, hn = [faces.near(axis, f) for f in range(4)]
        to, ko, ho = [faces.own(axis, f) for f in (0, 2, 3)]
        if axis == 2:
            meet[2][...] = (0.5 * ko + to) + (0.5 * kn - tn)
            return half_flux(ko, to, kn, tn), sn, half_flux(ko, ho, kn, hn)
        for side in (0, 1):
            meet[axis][side] = (0.5 * ko[side] + to[side]) + (0.5 * kn[side] - tn[side])
        heat = [half_flux(*v) for v in zip(ko, to, kn, tn)]
        return heat, sn, [half_flux(*v) for v in zip(ko, ho, kn, hn)]

    heat_x, sugar_x, again_x = flux_in(0)
    for f, pair in enumerate(flux_in(1)):
        for side in (0, 1):
            rows_ref[side, pl.ds(f * nx, nx), :] = pair[side]
    heat_z, sugar_z, again_z = flux_in(2)
    in_heat, in_sugar = ready_z(heat_z), ready_z(sugar_z)

    def plane(x, carry):
        accs, misfit, part = carry
        here = pl.ds(x * ny, ny)
        heat = at_plane(x, nx, heat_x) + at_rows(x, rows_ref, 0, nx, row, ny)
        diff = at_plane(x, nx, sugar_x) + at_rows(x, rows_ref, 1, nx, row, ny)
        some_t = mtp_ref[here, :] + WARMTH_ADVANCE * heat
        some_s = msp_ref[here, :] + STEP_SOLUTE * diff
        heat_in = jnp.where(edge, unpack_z(in_heat, x), 0.0)
        diff = jnp.where(edge, unpack_z(in_sugar, x), 0.0)
        heat = heat + heat_in
        again = at_plane(x, nx, again_x) + at_rows(x, rows_ref, 2, nx, row, ny)
        mt = some_t + WARMTH_ADVANCE * heat_in
        ms = some_s + STEP_SOLUTE * diff
        h, l, soft, g = h_ref[here, :], l_ref[here, :], soft_ref[here, :], g_ref[here, :]
        pull = HIDDEN_WARMTH * mt + REJECT * ms
        by_speed = pull * l
        below = by_speed * g * slope_ref[here, :]
        part_t = mt - below
        pull_0 = HIDDEN_WARMTH * part_t + REJECT * (ms - LOWERING_COEF * below)
        mt_ref[here, :], ms_ref[here, :] = mt, ms
        sense_ref[here, :] = (
            by_speed * soft + pull_0 * w_ref[here, :] + g * soft * pull * v_ref[here, :]
        )
        misfit = misfit + (mt * mt + ms * ms)
        inner = inner_ref[here, :] + heat + WARMTH_ADVANCE * again
        part = part + (mt * inner + part_t * h)
        for f, v in enumerate((mt, ms)):
            own.rows(f, x, v)
        accs = tuple(pack_z(a, z, x, lane) for a, z in zip(accs, (some_t, some_s)))
        return accs, misfit, part

    zero = jnp.zeros((ny, LANES), F32)
    accs, misfit, part = lax.fori_loop(
        0, nx, plane, ((zero, zero), zero, zero), unroll=unroll
    )
    packs = (
        accs[0] + WARMTH_ADVANCE * turn_z(heat_z),
        accs[1] + STEP_SOLUTE * turn_z(sugar_z),
    )
    own.finish((mt_ref, ms_ref), packs)
    part = part + WARMTH_ADVANCE * turn_z(packs[0]) * again_z
    lane_row = lax.broadcasted_iota(jnp.int32, (1, LANES), 1)
    line = jnp.where(lane_row == 0, 0.5 * jnp.sum(misfit), 0.0)
    line = jnp.where(lane_row == 1, WARMTH_ADVANCE * jnp.sum(part), line)
    sums_ref[...] = jnp.broadcast_to(line, sums_ref.shape)


FLUX_WEIGHT = 0.5 * WARMTH_ADVANCE
SUGAR_WEIGHT = REJECT * STEP_SOLUTE


def crossing(k, t, mt, kn, tn, mtn, msn):
    return FLUX_WEIGHT * (mtn - mt) * (0.5 * (k + kn) + (t - tn)) + SUGAR_WEIGHT * msn


def third_inner_kernel(dims, unroll, *refs):
    nx, ny = dims
    t_ref, k_ref, mt_ref, ms_ref, w_ref, sense_ref = refs[:6]
    out_ref = refs[6]
    row, lane = grid_iota(ny)

    def plane(x, carry):
        t, k, mt, ms, from_prev = carry
        here = pl.ds(x * ny, ny)
        then = pl.ds(jnp.minimum(x + 1, nx - 1) * ny, ny)
        tn, kn, mtn, msn = [r[then, :] for r in (t_ref, k_ref, mt_ref, ms_ref)]
        total = from_prev - (6.0 * SUGAR_WEIGHT) * ms
        total = total + jnp.where(x == nx - 1, 0.0, crossing(k, t, mt, kn, tn, mtn, msn))
        to_next = crossing(kn, tn, mtn, k, t, mt, ms)
        for axis, index in ((0, row), (1, lane)):
            size = ny if axis == 0 else LANES
            ta, ka, mta, msa = [ahead(v, axis) for v in (t, k, mt, ms)]
            up = crossing(k, t, mt, ka, ta, mta, msa)
            down = crossing(ka, ta, mta, k, t, mt, ms)
            total = total + jnp.where(index == size - 1, 0.0, up)
            total = total + jnp.where(index == 0, 0.0, pltpu.roll(down, 1, axis))
        out_ref[here, :] = sense_ref[here, :] + w_ref[here, :] * total
        return tn, kn, mtn, msn, to_next

    top = pl.ds(0, ny)
    start = [r[top, :] for r in (t_ref, k_ref, mt_ref, ms_ref)]
    lax.fori_loop(0, nx, plane, (*start, jnp.zeros((ny, LANES), F32)), unroll=unroll)


def finish_kernel(dims, counts, cells, unroll, *refs):
    nx, ny = dims
    ngot = sum(swaps(n) for n in counts)
    w_ref, sense_ref, sums_ref = refs[:3]
    meet = refs[3:6]
    faces = Faces(dims, counts, refs[6:9], refs[9 : 9 + ngot])
    out_ref, misfit_ref, gradient_ref, rows_ref = refs[9 + ngot :]
    row, lane = grid_iota(ny)
    edge = (lane == 0) | (lane == LANES - 1)

    def into(axis):
        own, near, sugar = faces.own(axis, 0), faces.near(axis, 0), faces.near(axis, 1)
        if axis == 2:
            return FLUX_WEIGHT * (near - own) * meet[2][...] + SUGAR_WEIGHT * sugar
        return [
            FLUX_WEIGHT * (near[side] - own[side]) * meet[axis][side] + SUGAR_WEIGHT * sugar[side]
            for side in (0, 1)
        ]

    into_x, into_y, into_z = into(0), into(1), ready_z(into(2))
    rows_ref[0], rows_ref[1] = into_y

    def plane(x, _):
        here = pl.ds(x * ny, ny)
        value = jnp.where(edge, unpack_z(into_z, x), 0.0) + at_plane(x, nx, into_x)
        value = value + at_rows(x, rows_ref, 0, nx, row, ny)
        out_ref[here, :] = sense_ref[here, :] + w_ref[here, :] * value
        return 0

    lax.fori_loop(0, nx, plane, 0, unroll=unroll)
    sums = sums_ref[...]
    which = lax.broadcasted_iota(jnp.int32, sums.shape, 1)
    misfit_ref[0, 0] = jnp.sum(jnp.where(which == 0, sums, 0.0)) / cells
    gradient_ref[0, 0] = jnp.sum(jnp.where(which == 1, sums, 0.0)) / cells


VM = pl.BlockSpec(memory_space=pltpu.VMEM)
SM = pl.BlockSpec(memory_space=pltpu.SMEM)


def call(kernel, out, args, name, scratch=(), in_specs=None, out_specs=None, vmem=32, flops=0):
    size = sum(int(np.prod(a.shape)) * a.dtype.itemsize for a in args)
    return pl.pallas_call(
        kernel,
        out_shape=[jax.ShapeDtypeStruct(s, d) for s, d in out],
        in_specs=in_specs or [VM] * len(args),
        out_specs=out_specs or [VM] * len(out),
        scratch_shapes=list(scratch),
        name=name,
        cost_estimate=pl.CostEstimate(flops=flops, bytes_accessed=size, transcendentals=0),
        compiler_params=pltpu.CompilerParams(vmem_limit_bytes=vmem << 20),
    )(*args)


def per_device(counts, warmth, sugar, population, coefficient, sensors):
    nx, ny, nz = warmth.shape
    assert nz == LANES and 2 * nx <= LANES
    bins = population.shape[0]
    dims = (nx, ny)
    cells = nx * ny
    t, s, g = [v.reshape(cells, nz) for v in (warmth, sugar, coefficient)]
    c = population.reshape(bins, cells, nz)
    r = sensors.reshape(2, cells, nz)
    field = ((cells, nz), F32)
    hbm = pl.BlockSpec(memory_space=pl.ANY)
    work = cells * nz * 100

    chunks = 8
    res = call(
        functools.partial(prepare_kernel, dims, counts, bins, chunks),
        [field] * 5 + own_shapes(dims, counts, 3),
        (c, t, s),
        "prepare",
        [pltpu.VMEM((bins, cells, nz), F32), pltpu.SemaphoreType.DMA((chunks + 2,))],
        in_specs=[hbm] * 3,
        vmem=51,
    )
    k, l, m, t, s = res[:5]
    own = res[5:]
    got = send_faces(own, counts)
    pack = ((ny, nz), F32)
    tp, sp, hp, k1, l1, w, v, kpack = call(
        functools.partial(first_inner_kernel, dims, 8),
        [field] * 7 + [pack],
        (t, s, k, l, m, g),
        "first_inner",
        flops=work,
    )
    res = call(
        functools.partial(first_edge_kernel, dims, counts, 32),
        [field] * 3 + own_shapes(dims, counts, 4),
        (tp, sp, hp, k1, kpack, *own[:3], *got),
        "first_edge",
        [pltpu.VMEM((2, 2 * nx, nz), F32)],
    )
    t1, s1, h0 = res[:3]
    own1 = res[3:]
    got1 = send_faces(own1, counts)
    inner = call(
        functools.partial(second_inner_kernel, dims, 8),
        [field] * 5,
        (t1, s1, k1, h0, l1, g, r),
        "second_inner",
        flops=work,
    )
    devices = int(np.prod(counts))
    line = ((devices, LANES), F32)
    meet_shapes = own_shapes(dims, counts, 1)[:3]
    res = call(
        functools.partial(second_edge_kernel, dims, counts, 32),
        [field] * 3 + [line] + meet_shapes + own_shapes(dims, counts, 2),
        (h0, l1, w, v, g, *inner, *own1[:3], *got1),
        "second_edge",
        [pltpu.VMEM((2, 3 * nx, nz), F32)],
    )
    mt, ms, sense, sums = res[:4]
    meet, own2 = res[4:7], res[7:]
    got2 = send_faces(own2, counts)
    sums = lax.all_to_all(sums, AXES, 0, 0, tiled=True)
    (sense,) = call(
        functools.partial(third_inner_kernel, dims, 8),
        [field],
        (t1, k1, mt, ms, w, sense),
        "third_inner",
        flops=work,
    )
    sens, misfit, gradient = call(
        functools.partial(finish_kernel, dims, counts, float(cells * nz * devices), 64),
        [field, ((1, 1), F32), ((1, 1), F32)],
        (w, sense, sums, *meet, *own2[:3], *got2),
        "finish",
        [pltpu.VMEM((2, nx, nz), F32)],
        out_specs=[VM, SM, SM],
    )
    return sens.reshape(nx, ny, nz), misfit.reshape(()), gradient.reshape(())


def solution(mesh):
    counts = tuple(mesh.shape[a] for a in AXES)
    placed = (
        P("gx", "gy", "gz"),
        P("gx", "gy", "gz"),
        P(None, "gx", "gy", "gz"),
        P("gx", "gy", "gz"),
        P(None, "gx", "gy", "gz"),
    )
    return jax.shard_map(
        functools.partial(per_device, counts),
        mesh=mesh,
        in_specs=placed,
        out_specs=(P("gx", "gy", "gz"), P(), P()),
        check_vma=False,
    )
```

```python
import functools

import jax
import jax.numpy as jnp
import numpy as np
from jax import lax
from jax.experimental import pallas as pl
from jax.experimental.pallas import tpu as pltpu
from jax.sharding import PartitionSpec as P

F32 = jnp.float32
AXES = ("gx", "gy", "gz")

SOLIDIFY_POINT = 0.5
LOWERING_COEF = 0.5
GROW = 0.3
NUCLEATE = 0.2
VOLUME = 0.005
WARMTH_ADVANCE = 0.08
STEP_SOLUTE = 0.1
HIDDEN_WARMTH = 0.5
REJECT = 0.3
LANES = 128


def volumes(bin_count):
    rank = np.arange(bin_count, dtype=np.float64) + 1.0
    return VOLUME * rank * rank


def functional_weights(bin_count):
    vol = volumes(bin_count)
    step = vol[1:] - vol[:-1]
    k = (1.0, vol)
    l = (NUCLEATE * vol[0], np.concatenate([GROW * step, [0.0]]))
    m_const = GROW * step[0] * NUCLEATE
    m = np.zeros(bin_count)
    for b in range(bin_count - 1):
        m[b] -= GROW * step[b] * GROW
        if b >= 1:
            m[b - 1] += GROW * step[b] * GROW
    return k, l, (m_const, m)


SPARE = {"gx": 0, "gz": 0, "gy": 2}


def swap_pairs(counts, axis, kind):
    pairs = []
    for at in np.ndindex(*counts):
        to = list(at)
        i = at[axis]
        to[axis] = i ^ 1 if kind == 0 else (i + 1 if i % 2 else i - 1)
        if not 0 <= to[axis] < counts[axis]:
            to[axis] = i
            spare = SPARE[AXES[axis]]
            if spare == axis:
                to[axis] = counts[axis] - 1 - i
            else:
                to[spare] = at[spare] ^ 1
        pairs.append(tuple(int(np.ravel_multi_index(v, counts)) for v in (at, to)))
    return pairs


def swaps(count):
    return {1: 0, 2: 1}.get(count, 2)


def exchange(payloads, counts, axis):
    assert counts[axis] == 1 or counts[axis] % 2 == 0
    return [
        lax.ppermute(p, AXES, swap_pairs(counts, axis, kind)) for kind, p in enumerate(payloads)
    ]


class Side:
    def __init__(self, axis, count):
        self.count = count
        self.index = lax.axis_index(axis)
        self.odd = lax.rem(self.index, 2) == 1

    def outgoing(self, first, last):
        kinds = [jnp.where(self.odd, first, last), jnp.where(self.odd, last, first)]
        return kinds[: swaps(self.count)]

    def incoming(self, got):
        if self.count == 1:
            return None
        if self.count == 2:
            zero = jnp.zeros_like(got[0])
            return jnp.where(self.odd, got[0], zero), jnp.where(self.odd, zero, got[0])
        a, b = got
        zero = jnp.zeros_like(a)
        before = jnp.where(self.index > 0, jnp.where(self.odd, a, b), zero)
        after = jnp.where(self.index < self.count - 1, jnp.where(self.odd, b, a), zero)
        return before, after


def grid_iota(ny):
    row = lax.broadcasted_iota(jnp.int32, (ny, LANES), 0)
    lane = lax.broadcasted_iota(jnp.int32, (ny, LANES), 1)
    return row, lane


def pack_z(acc, value, x, lane):
    return jnp.where(lane // 2 == x, pltpu.roll(value, lax.rem(2 * x + 1, LANES), 1), acc)


class Faces:
    def __init__(self, dims, counts, own, got):
        self.nx, self.ny = dims
        self.sides = [Side(a, n) for a, n in zip(AXES, counts)]
        self.mine = own
        a, b = swaps(counts[0]), swaps(counts[1])
        self.got = (got[:a], got[a : a + b], got[a + b :])

    def _part(self, axis, f):
        rows = self.nx if axis == 1 else self.ny
        return pl.ds(f * rows, rows)

    def near(self, axis, f):
        part = [r[self._part(axis, f), :] for r in self.got[axis]]
        before, after = self.sides[axis].incoming(part)
        if axis < 2:
            return before, after
        lane = lax.broadcasted_iota(jnp.int32, before.shape, 1)
        return jnp.where(lax.rem(lane, 2) == 0, before, after)

    def own(self, axis, f):
        if axis < 2:
            return [self.mine[axis][side, self._part(axis, f), :] for side in (0, 1)]
        return turn_z(self.mine[2][self._part(2, f), :])


def turn_z(pack):
    lane = lax.broadcasted_iota(jnp.int32, pack.shape, 1)
    even = lax.rem(lane, 2) == 0
    return jnp.where(even, pltpu.roll(pack, LANES - 1, 1), pltpu.roll(pack, 1, 1))


class Own:
    def __init__(self, dims, counts, refs, scratch=None):
        self.nx, self.ny = dims
        self.counts = counts
        self.x, self.y = scratch or refs[:2]
        self.z, *out = refs if scratch else refs[2:]
        a = swaps(counts[0])
        self.out = (out[:a], out[a:])

    def rows(self, f, x, value):
        self.y[0, pl.ds(f * self.nx + x, 1), :] = value[:1, :]
        self.y[1, pl.ds(f * self.nx + x, 1), :] = value[self.ny - 1 :, :]

    def finish(self, fields, packs):
        nx, ny = self.nx, self.ny
        for f, (ref, pack) in enumerate(zip(fields, packs)):
            part = pl.ds(f * ny, ny)
            self.x[0, part, :] = ref[pl.ds(0, ny), :]
            self.x[1, part, :] = ref[pl.ds((nx - 1) * ny, ny), :]
            self.z[part, :] = pack
        for axis, own in enumerate((self.x, self.y)):
            side = Side(AXES[axis], self.counts[axis])
            for o, v in zip(self.out[axis], side.outgoing(own[0], own[1])):
                o[...] = v


def own_shapes(dims, counts, fields):
    nx, ny = dims
    x, y = (fields * ny, LANES), (fields * nx, LANES)
    shapes = [(2, *x), (2, *y), x] + [x] * swaps(counts[0]) + [y] * swaps(counts[1])
    return [(v, F32) for v in shapes]


def send_faces(own, counts):
    a = swaps(counts[0])
    payloads = (own[3 : 3 + a], own[3 + a :], [own[2]] * swaps(counts[2]))
    got = []
    for axis, payload in enumerate(payloads):
        got += exchange(payload, counts, axis)
    return got


def at_plane(x, nx, pair):
    return jnp.where(x == 0, pair[0], jnp.where(x == nx - 1, pair[1], 0.0))


def at_rows(x, ref, f, nx, row, ny):
    part = pl.ds(f * nx + x, 1)
    return jnp.where(row == 0, ref[0, part, :], jnp.where(row == ny - 1, ref[1, part, :], 0.0))


def ready_z(value):
    lane = lax.broadcasted_iota(jnp.int32, value.shape, 1)
    return jnp.where(lax.rem(lane, 2) == 0, value, pltpu.roll(value, LANES - 2, 1))


def unpack_z(value, x):
    return pltpu.roll(value, lax.rem(LANES - 2 * x, LANES), 1)


def half_flux(k, t, kn, tn):
    return 0.5 * (k + kn) * (tn - t)


def divergence(flux_up, axis, index):
    size = flux_up.shape[axis]
    flux_up = jnp.where(index == size - 1, 0.0, flux_up)
    return flux_up - pltpu.roll(flux_up, 1, axis)


def ahead(value, axis):
    return pltpu.roll(value, value.shape[axis] - 1, axis)


def neighbour_sum(value, axis, index):
    size = value.shape[axis]
    up = jnp.where(index == size - 1, 0.0, ahead(value, axis))
    return up + jnp.where(index == 0, 0.0, pltpu.roll(value, 1, axis))


def log1p_of(e, u, inv):
    return jnp.log(u) + (e - (u - 1.0)) * inv


def softplus_parts(v):
    e = jnp.exp(-jnp.abs(v))
    u = 1.0 + e
    inv = 1.0 / u
    soft = jnp.maximum(v, 0.0) + log1p_of(e, u, inv)
    return soft, jnp.where(v >= 0, inv, e * inv)


def prepare_kernel(dims, counts, bins, chunks, *refs):
    nx, ny = dims
    c_hbm, t_hbm, s_hbm = refs[:3]
    k_ref, l_ref, m_ref, t_ref, s_ref = refs[3:8]
    own = Own(dims, counts, refs[8:-2])
    c_ref, sems = refs[-2:]
    rows = nx * ny // chunks
    copies = [
        pltpu.make_async_copy(t_hbm, t_ref, sems.at[chunks]),
        pltpu.make_async_copy(s_hbm, s_ref, sems.at[chunks + 1]),
    ]
    for j in range(chunks):
        part = pl.ds(j * rows, rows)
        copies.append(pltpu.make_async_copy(c_hbm.at[:, part, :], c_ref.at[:, part, :], sems.at[j]))
    for copy in copies:
        copy.start()
    copies[0].wait()
    copies[1].wait()
    _, lane = grid_iota(ny)
    weights = functional_weights(bins)

    def plane(x, accs):
        here = pl.ds(x * ny, ny)
        c = [c_ref[b, here, :] for b in range(bins)]
        values = []
        for const, per_bin in weights:
            total = None
            for b in range(bins):
                if per_bin[b] != 0.0:
                    term = float(per_bin[b]) * c[b]
                    total = term if total is None else total + term
            values.append(float(const) + total)
        k_ref[here, :], l_ref[here, :], m_ref[here, :] = values
        faces = (t_ref[here, :], s_ref[here, :], values[0])
        for f, v in enumerate(faces):
            own.rows(f, x, v)
        return tuple(pack_z(a, v, x, lane) for a, v in zip(accs, faces))

    accs = tuple(jnp.zeros((ny, LANES), F32) for _ in range(3))
    planes = nx // chunks
    for j in range(chunks):
        copies[2 + j].wait()
        accs = lax.fori_loop(j * planes, (j + 1) * planes, plane, accs, unroll=8)
    own.finish((t_ref, s_ref, k_ref), accs)


def first_inner_kernel(dims, unroll, *refs):
    nx, ny = dims
    t_ref, s_ref, k_ref, l_ref, m_ref, g_ref = refs[:6]
    t1, s1, h0, k1, l1, w0, v0, kpack = refs[6:]
    row, lane = grid_iota(ny)

    def plane(x, carry):
        t, s, k, s_prev, flux_prev, acc = carry
        here = pl.ds(x * ny, ny)
        then = pl.ds(jnp.minimum(x + 1, nx - 1) * ny, ny)
        tn, sn, kn = t_ref[then, :], s_ref[then, :], k_ref[then, :]
        flux = half_flux(k, t, kn, tn)
        heat = (flux - flux_prev) + divergence(
            half_flux(k, t, ahead(k, 0), ahead(t, 0)), 0, row
        )
        heat = heat + divergence(half_flux(k, t, ahead(k, 1), ahead(t, 1)), 1, lane)
        s_next = jnp.where(x == nx - 1, 0.0, sn)
        diff = (s_prev + s_next) + neighbour_sum(s, 0, row)
        diff = diff + neighbour_sum(s, 1, lane) - 6.0 * s
        g, l, m = g_ref[here, :], l_ref[here, :], m_ref[here, :]
        soft, _ = softplus_parts(SOLIDIFY_POINT - LOWERING_COEF * s - t)
        w, v = soft * l, soft * m
        frost = g * w
        t1[here, :] = t + WARMTH_ADVANCE * heat + HIDDEN_WARMTH * frost
        s1[here, :] = s + STEP_SOLUTE * diff + REJECT * frost
        h0[here, :] = heat
        new_k = k + frost
        k1[here, :] = new_k
        l1[here, :], w0[here, :], v0[here, :] = l + g * v, w, v
        return tn, sn, kn, s, flux, pack_z(acc, new_k, x, lane)

    top = pl.ds(0, ny)
    zero = jnp.zeros((ny, LANES), F32)
    carry = (t_ref[top, :], s_ref[top, :], k_ref[top, :], zero, zero, zero)
    kpack[...] = lax.fori_loop(0, nx, plane, carry, unroll=unroll)[-1]


def first_edge_kernel(dims, counts, unroll, *refs):
    nx, ny = dims
    ngot = sum(swaps(n) for n in counts)
    tp_ref, sp_ref, hp_ref, k1_ref, kpack_ref = refs[:5]
    faces = Faces(dims, counts, refs[5:8], refs[8 : 8 + ngot])
    t1, s1, h0 = refs[8 + ngot : 11 + ngot]
    own = Own(dims, counts, refs[11 + ngot : -1])
    rows_ref = refs[-1]
    row, lane = grid_iota(ny)
    edge = (lane == 0) | (lane == LANES - 1)

    def flux_in(axis):
        tn, sn, kn = [faces.near(axis, f) for f in range(3)]
        to, ko = faces.own(axis, 0), faces.own(axis, 2)
        if axis == 2:
            return half_flux(ko, to, kn, tn), sn
        return [half_flux(*v) for v in zip(ko, to, kn, tn)], sn

    heat_x, sugar_x = flux_in(0)
    heat_y, sugar_y = flux_in(1)
    for side in (0, 1):
        rows_ref[side, pl.ds(0, nx), :] = heat_y[side]
        rows_ref[side, pl.ds(nx, nx), :] = sugar_y[side]
    heat_z, sugar_z = flux_in(2)
    in_heat, in_sugar = ready_z(heat_z), ready_z(sugar_z)

    def plane(x, accs):
        here = pl.ds(x * ny, ny)
        heat = at_plane(x, nx, heat_x) + at_rows(x, rows_ref, 0, nx, row, ny)
        diff = at_plane(x, nx, sugar_x) + at_rows(x, rows_ref, 1, nx, row, ny)
        some_t = tp_ref[here, :] + WARMTH_ADVANCE * heat
        some_s = sp_ref[here, :] + STEP_SOLUTE * diff
        some_h = hp_ref[here, :] + heat
        heat = jnp.where(edge, unpack_z(in_heat, x), 0.0)
        diff = jnp.where(edge, unpack_z(in_sugar, x), 0.0)
        new_t = some_t + WARMTH_ADVANCE * heat
        new_s = some_s + STEP_SOLUTE * diff
        new_h = some_h + heat
        t1[here, :], s1[here, :], h0[here, :] = new_t, new_s, new_h
        for f, v in enumerate((new_t, new_s, k1_ref[here, :], new_h)):
            own.rows(f, x, v)
        return tuple(pack_z(a, v, x, lane) for a, v in zip(accs, (some_t, some_s, some_h)))

    accs = tuple(jnp.zeros((ny, LANES), F32) for _ in range(3))
    accs = lax.fori_loop(0, nx, plane, accs, unroll=unroll)
    heat_z, sugar_z = turn_z(heat_z), turn_z(sugar_z)
    packs = (
        accs[0] + WARMTH_ADVANCE * heat_z,
        accs[1] + STEP_SOLUTE * sugar_z,
        kpack_ref[...],
        accs[2] + heat_z,
    )
    own.finish((t1, s1, k1_ref, h0), packs)


def second_inner_kernel(dims, unroll, *refs):
    nx, ny = dims
    t_ref, s_ref, k_ref, h_ref, l_ref, g_ref, r_ref = refs[:7]
    mt_ref, ms_ref, inner_ref, soft_ref, slope_ref = refs[7:]
    row, lane = grid_iota(ny)

    def plane(x, carry):
        t, s, k, h, s_prev, flux_prev, other_prev = carry
        here = pl.ds(x * ny, ny)
        then = pl.ds(jnp.minimum(x + 1, nx - 1) * ny, ny)
        tn, sn, kn, hn = t_ref[then, :], s_ref[then, :], k_ref[then, :], h_ref[then, :]
        both = 0.5 * (k + kn)
        flux, other = both * (tn - t), both * (hn - h)
        heat, again = flux - flux_prev, other - other_prev
        for axis, index in ((0, row), (1, lane)):
            both = 0.5 * (k + ahead(k, axis))
            heat = heat + divergence(both * (ahead(t, axis) - t), axis, index)
            again = again + divergence(both * (ahead(h, axis) - h), axis, index)
        s_next = jnp.where(x == nx - 1, 0.0, sn)
        diff = (s_prev + s_next) + neighbour_sum(s, 0, row)
        diff = diff + neighbour_sum(s, 1, lane) - 6.0 * s
        g, l = g_ref[here, :], l_ref[here, :]
        soft, slope = softplus_parts(SOLIDIFY_POINT - LOWERING_COEF * s - t)
        frost = g * soft * l
        mt_ref[here, :] = (
            t + WARMTH_ADVANCE * heat + HIDDEN_WARMTH * frost - r_ref[0, here, :].astype(F32)
        )
        ms_ref[here, :] = s + STEP_SOLUTE * diff + REJECT * frost - r_ref[1, here, :].astype(F32)
        inner_ref[here, :] = heat + WARMTH_ADVANCE * again
        soft_ref[here, :], slope_ref[here, :] = soft, slope
        return tn, sn, kn, hn, s, flux, other

    top = pl.ds(0, ny)
    zero = jnp.zeros((ny, LANES), F32)
    start = [r[top, :] for r in (t_ref, s_ref, k_ref, h_ref)]
    lax.fori_loop(0, nx, plane, (*start, zero, zero, zero), unroll=unroll)


def second_edge_kernel(dims, counts, unroll, *refs):
    nx, ny = dims
    ngot = sum(swaps(n) for n in counts)
    h_ref, l_ref, w_ref, v_ref, g_ref = refs[:5]
    mtp_ref, msp_ref, inner_ref, soft_ref, slope_ref = refs[5:10]
    faces = Faces(dims, counts, refs[10:13], refs[13 : 13 + ngot])
    mt_ref, ms_ref, sense_ref, sums_ref = refs[13 + ngot : 17 + ngot]
    meet = refs[17 + ngot : 20 + ngot]
    own = Own(dims, counts, refs[20 + ngot : -3], refs[-2:])
    rows_ref = refs[-3]
    row, lane = grid_iota(ny)
    edge = (lane == 0) | (lane == LANES - 1)

    def flux_in(axis):
        tn, sn, kn, hn = [faces.near(axis, f) for f in range(4)]
        to, ko, ho = [faces.own(axis, f) for f in (0, 2, 3)]
        if axis == 2:
            meet[2][...] = (0.5 * ko + to) + (0.5 * kn - tn)
            return half_flux(ko, to, kn, tn), sn, half_flux(ko, ho, kn, hn)
        for side in (0, 1):
            meet[axis][side] = (0.5 * ko[side] + to[side]) + (0.5 * kn[side] - tn[side])
        heat = [half_flux(*v) for v in zip(ko, to, kn, tn)]
        return heat, sn, [half_flux(*v) for v in zip(ko, ho, kn, hn)]

    heat_x, sugar_x, again_x = flux_in(0)
    for f, pair in enumerate(flux_in(1)):
        for side in (0, 1):
            rows_ref[side, pl.ds(f * nx, nx), :] = pair[side]
    heat_z, sugar_z, again_z = flux_in(2)
    in_heat, in_sugar = ready_z(heat_z), ready_z(sugar_z)

    def plane(x, carry):
        accs, misfit, part = carry
        here = pl.ds(x * ny, ny)
        heat = at_plane(x, nx, heat_x) + at_rows(x, rows_ref, 0, nx, row, ny)
        diff = at_plane(x, nx, sugar_x) + at_rows(x, rows_ref, 1, nx, row, ny)
        some_t = mtp_ref[here, :] + WARMTH_ADVANCE * heat
        some_s = msp_ref[here, :] + STEP_SOLUTE * diff
        heat_in = jnp.where(edge, unpack_z(in_heat, x), 0.0)
        diff = jnp.where(edge, unpack_z(in_sugar, x), 0.0)
        heat = heat + heat_in
        again = at_plane(x, nx, again_x) + at_rows(x, rows_ref, 2, nx, row, ny)
        mt = some_t + WARMTH_ADVANCE * heat_in
        ms = some_s + STEP_SOLUTE * diff
        h, l, soft, g = h_ref[here, :], l_ref[here, :], soft_ref[here, :], g_ref[here, :]
        pull = HIDDEN_WARMTH * mt + REJECT * ms
        by_speed = pull * l
        below = by_speed * g * slope_ref[here, :]
        part_t = mt - below
        pull_0 = HIDDEN_WARMTH * part_t + REJECT * (ms - LOWERING_COEF * below)
        mt_ref[here, :], ms_ref[here, :] = mt, ms
        sense_ref[here, :] = (
            by_speed * soft + pull_0 * w_ref[here, :] + g * soft * pull * v_ref[here, :]
        )
        misfit = misfit + (mt * mt + ms * ms)
        inner = inner_ref[here, :] + heat + WARMTH_ADVANCE * again
        part = part + (mt * inner + part_t * h)
        for f, v in enumerate((mt, ms)):
            own.rows(f, x, v)
        accs = tuple(pack_z(a, z, x, lane) for a, z in zip(accs, (some_t, some_s)))
        return accs, misfit, part

    zero = jnp.zeros((ny, LANES), F32)
    accs, misfit, part = lax.fori_loop(
        0, nx, plane, ((zero, zero), zero, zero), unroll=unroll
    )
    packs = (
        accs[0] + WARMTH_ADVANCE * turn_z(heat_z),
        accs[1] + STEP_SOLUTE * turn_z(sugar_z),
    )
    own.finish((mt_ref, ms_ref), packs)
    part = part + WARMTH_ADVANCE * turn_z(packs[0]) * again_z
    lane_row = lax.broadcasted_iota(jnp.int32, (1, LANES), 1)
    line = jnp.where(lane_row == 0, 0.5 * jnp.sum(misfit), 0.0)
    line = jnp.where(lane_row == 1, WARMTH_ADVANCE * jnp.sum(part), line)
    sums_ref[...] = jnp.broadcast_to(line, sums_ref.shape)


FLUX_WEIGHT = 0.5 * WARMTH_ADVANCE
SUGAR_WEIGHT = REJECT * STEP_SOLUTE


def crossing(k, t, mt, kn, tn, mtn, msn):
    return FLUX_WEIGHT * (mtn - mt) * (0.5 * (k + kn) + (t - tn)) + SUGAR_WEIGHT * msn


def third_inner_kernel(dims, unroll, *refs):
    nx, ny = dims
    t_ref, k_ref, mt_ref, ms_ref, w_ref, sense_ref = refs[:6]
    out_ref, x_ref, y_ref = refs[6:]
    row, lane = grid_iota(ny)
    x_ref[0], x_ref[1] = mt_ref[pl.ds(0, ny), :], mt_ref[pl.ds((nx - 1) * ny, ny), :]

    def plane(x, carry):
        t, k, mt, ms, from_prev = carry
        here = pl.ds(x * ny, ny)
        then = pl.ds(jnp.minimum(x + 1, nx - 1) * ny, ny)
        tn, kn, mtn, msn = [r[then, :] for r in (t_ref, k_ref, mt_ref, ms_ref)]
        y_ref[0, pl.ds(x, 1), :], y_ref[1, pl.ds(x, 1), :] = mt[:1, :], mt[ny - 1 :, :]
        total = from_prev - (6.0 * SUGAR_WEIGHT) * ms
        total = total + jnp.where(x == nx - 1, 0.0, crossing(k, t, mt, kn, tn, mtn, msn))
        to_next = crossing(kn, tn, mtn, k, t, mt, ms)
        for axis, index in ((0, row), (1, lane)):
            size = ny if axis == 0 else LANES
            ta, ka, mta, msa = [ahead(v, axis) for v in (t, k, mt, ms)]
            up = crossing(k, t, mt, ka, ta, mta, msa)
            down = crossing(ka, ta, mta, k, t, mt, ms)
            total = total + jnp.where(index == size - 1, 0.0, up)
            total = total + jnp.where(index == 0, 0.0, pltpu.roll(down, 1, axis))
        out_ref[here, :] = sense_ref[here, :] + w_ref[here, :] * total
        return tn, kn, mtn, msn, to_next

    top = pl.ds(0, ny)
    start = [r[top, :] for r in (t_ref, k_ref, mt_ref, ms_ref)]
    lax.fori_loop(0, nx, plane, (*start, jnp.zeros((ny, LANES), F32)), unroll=unroll)


def finish_kernel(dims, counts, cells, unroll, *refs):
    nx, ny = dims
    ngot = sum(swaps(n) for n in counts)
    w_ref, sense_ref, sums_ref = refs[:3]
    meet = refs[3:6]
    faces = Faces(dims, counts, refs[6:9], refs[9 : 9 + ngot])
    out_ref, misfit_ref, gradient_ref, rows_ref = refs[9 + ngot :]
    row, lane = grid_iota(ny)
    edge = (lane == 0) | (lane == LANES - 1)

    def into(axis):
        own, near, sugar = faces.own(axis, 0), faces.near(axis, 0), faces.near(axis, 1)
        if axis == 2:
            return FLUX_WEIGHT * (near - own) * meet[2][...] + SUGAR_WEIGHT * sugar
        return [
            FLUX_WEIGHT * (near[side] - own[side]) * meet[axis][side] + SUGAR_WEIGHT * sugar[side]
            for side in (0, 1)
        ]

    into_x, into_y, into_z = into(0), into(1), ready_z(into(2))
    rows_ref[0], rows_ref[1] = into_y

    def plane(x, _):
        here = pl.ds(x * ny, ny)
        value = jnp.where(edge, unpack_z(into_z, x), 0.0) + at_plane(x, nx, into_x)
        value = value + at_rows(x, rows_ref, 0, nx, row, ny)
        out_ref[here, :] = sense_ref[here, :] + w_ref[here, :] * value
        return 0

    lax.fori_loop(0, nx, plane, 0, unroll=unroll)
    sums = sums_ref[...]
    which = lax.broadcasted_iota(jnp.int32, sums.shape, 1)
    misfit_ref[0, 0] = jnp.sum(jnp.where(which == 0, sums, 0.0)) / cells
    gradient_ref[0, 0] = jnp.sum(jnp.where(which == 1, sums, 0.0)) / cells


VM = pl.BlockSpec(memory_space=pltpu.VMEM)
SM = pl.BlockSpec(memory_space=pltpu.SMEM)


def call(kernel, out, args, name, scratch=(), in_specs=None, out_specs=None, vmem=32, flops=0, aliases={}):
    size = sum(int(np.prod(a.shape)) * a.dtype.itemsize for a in args)
    return pl.pallas_call(
        kernel,
        out_shape=[jax.ShapeDtypeStruct(s, d) for s, d in out],
        in_specs=in_specs or [VM] * len(args),
        out_specs=out_specs or [VM] * len(out),
        scratch_shapes=list(scratch),
        name=name,
        input_output_aliases=aliases,
        cost_estimate=pl.CostEstimate(flops=flops, bytes_accessed=size, transcendentals=0),
        compiler_params=pltpu.CompilerParams(vmem_limit_bytes=vmem << 20),
    )(*args)


def per_device(counts, warmth, sugar, population, coefficient, sensors):
    nx, ny, nz = warmth.shape
    assert nz == LANES and 2 * nx <= LANES
    bins = population.shape[0]
    dims = (nx, ny)
    cells = nx * ny
    t, s, g = [v.reshape(cells, nz) for v in (warmth, sugar, coefficient)]
    c = population.reshape(bins, cells, nz)
    r = sensors.reshape(2, cells, nz)
    field = ((cells, nz), F32)
    hbm = pl.BlockSpec(memory_space=pl.ANY)
    work = cells * nz * 100

    chunks = 8
    res = call(
        functools.partial(prepare_kernel, dims, counts, bins, chunks),
        [field] * 5 + own_shapes(dims, counts, 3),
        (c, t, s),
        "prepare",
        [pltpu.VMEM((bins, cells, nz), F32), pltpu.SemaphoreType.DMA((chunks + 2,))],
        in_specs=[hbm] * 3,
        vmem=51,
    )
    k, l, m, t, s = res[:5]
    own = res[5:]
    got = send_faces(own, counts)
    pack = ((ny, nz), F32)
    tp, sp, hp, k1, l1, w, v, kpack = call(
        functools.partial(first_inner_kernel, dims, 8),
        [field] * 7 + [pack],
        (t, s, k, l, m, g),
        "first_inner",
        flops=work,
    )
    res = call(
        functools.partial(first_edge_kernel, dims, counts, 64),
        [field] * 3 + own_shapes(dims, counts, 4),
        (tp, sp, hp, k1, kpack, *own[:3], *got),
        "first_edge",
        [pltpu.VMEM((2, 2 * nx, nz), F32)],
    )
    t1, s1, h0 = res[:3]
    own1 = res[3:]
    got1 = send_faces(own1, counts)
    inner = call(
        functools.partial(second_inner_kernel, dims, 8),
        [field] * 5,
        (t1, s1, k1, h0, l1, g, r),
        "second_inner",
        flops=work,
    )
    devices = int(np.prod(counts))
    line = ((devices, LANES), F32)
    meet_shapes = own_shapes(dims, counts, 1)[:3]
    res = call(
        functools.partial(second_edge_kernel, dims, counts, 64),
        [field] * 3 + [line] + meet_shapes + own_shapes(dims, counts, 2)[2:],
        (h0, l1, w, v, g, *inner, *own1[:3], *got1),
        "second_edge",
        [pltpu.VMEM(v, F32) for v in ((2, 3 * nx, nz), (2, 2 * ny, nz), (2, 2 * nx, nz))],
    )
    mt, ms, sense, sums = res[:4]
    meet, sent = res[4:7], res[7:]
    got2 = send_faces((None, None, *sent), counts)
    sums = lax.all_to_all(sums, AXES, 0, 0, tiled=True)
    sense, *kept = call(
        functools.partial(third_inner_kernel, dims, 16),
        [field] + meet_shapes[:2],
        (t1, k1, mt, ms, w, sense),
        "third_inner",
        aliases={5: 0},
        flops=work,
    )
    sens, misfit, gradient = call(
        functools.partial(finish_kernel, dims, counts, float(cells * nz * devices), 64),
        [field, ((1, 1), F32), ((1, 1), F32)],
        (w, sense, sums, *meet, *kept, sent[0], *got2),
        "finish",
        [pltpu.VMEM((2, nx, nz), F32)],
        out_specs=[VM, SM, SM],
    )
    return sens.reshape(nx, ny, nz), misfit.reshape(()), gradient.reshape(())


def solution(mesh):
    counts = tuple(mesh.shape[a] for a in AXES)
    placed = (
        P("gx", "gy", "gz"),
        P("gx", "gy", "gz"),
        P(None, "gx", "gy", "gz"),
        P("gx", "gy", "gz"),
        P(None, "gx", "gy", "gz"),
    )
    return jax.shard_map(
        functools.partial(per_device, counts),
        mesh=mesh,
        in_specs=placed,
        out_specs=(P("gx", "gy", "gz"), P(), P()),
        check_vma=False,
    )
```

```python
import functools

import jax
import jax.numpy as jnp
import numpy as np
from jax import lax
from jax.experimental import pallas as pl
from jax.experimental.pallas import tpu as pltpu
from jax.sharding import PartitionSpec as P

F32 = jnp.float32
AXES = ("gx", "gy", "gz")

SOLIDIFY_POINT = 0.5
LOWERING_COEF = 0.5
GROW = 0.3
NUCLEATE = 0.2
VOLUME = 0.005
WARMTH_ADVANCE = 0.08
STEP_SOLUTE = 0.1
HIDDEN_WARMTH = 0.5
REJECT = 0.3
LANES = 128


def volumes(bin_count):
    rank = np.arange(bin_count, dtype=np.float64) + 1.0
    return VOLUME * rank * rank


def functional_weights(bin_count):
    vol = volumes(bin_count)
    step = vol[1:] - vol[:-1]
    k = (1.0, vol)
    l = (NUCLEATE * vol[0], np.concatenate([GROW * step, [0.0]]))
    m_const = GROW * step[0] * NUCLEATE
    m = np.zeros(bin_count)
    for b in range(bin_count - 1):
        m[b] -= GROW * step[b] * GROW
        if b >= 1:
            m[b - 1] += GROW * step[b] * GROW
    return k, l, (m_const, m)


SPARE = {"gx": 0, "gz": 0, "gy": 2}


def swap_pairs(counts, axis, kind):
    pairs = []
    for at in np.ndindex(*counts):
        to = list(at)
        i = at[axis]
        to[axis] = i ^ 1 if kind == 0 else (i + 1 if i % 2 else i - 1)
        if not 0 <= to[axis] < counts[axis]:
            to[axis] = i
            spare = SPARE[AXES[axis]]
            if spare == axis:
                to[axis] = counts[axis] - 1 - i
            else:
                to[spare] = at[spare] ^ 1
        pairs.append(tuple(int(np.ravel_multi_index(v, counts)) for v in (at, to)))
    return pairs


def swaps(count):
    return {1: 0, 2: 1}.get(count, 2)


def exchange(payloads, counts, axis):
    assert counts[axis] == 1 or counts[axis] % 2 == 0
    return [
        lax.ppermute(p, AXES, swap_pairs(counts, axis, kind)) for kind, p in enumerate(payloads)
    ]


class Side:
    def __init__(self, axis, count):
        self.count = count
        self.index = lax.axis_index(axis)
        self.odd = lax.rem(self.index, 2) == 1

    def outgoing(self, first, last):
        kinds = [jnp.where(self.odd, first, last), jnp.where(self.odd, last, first)]
        return kinds[: swaps(self.count)]

    def incoming(self, got):
        if self.count == 1:
            return None
        if self.count == 2:
            zero = jnp.zeros_like(got[0])
            return jnp.where(self.odd, got[0], zero), jnp.where(self.odd, zero, got[0])
        a, b = got
        zero = jnp.zeros_like(a)
        before = jnp.where(self.index > 0, jnp.where(self.odd, a, b), zero)
        after = jnp.where(self.index < self.count - 1, jnp.where(self.odd, b, a), zero)
        return before, after


def grid_iota(ny):
    row = lax.broadcasted_iota(jnp.int32, (ny, LANES), 0)
    lane = lax.broadcasted_iota(jnp.int32, (ny, LANES), 1)
    return row, lane


def pack_z(acc, value, x, lane):
    return jnp.where(lane // 2 == x, pltpu.roll(value, lax.rem(2 * x + 1, LANES), 1), acc)


class Faces:
    def __init__(self, dims, counts, own, got):
        self.nx, self.ny = dims
        self.sides = [Side(a, n) for a, n in zip(AXES, counts)]
        self.mine = own
        a, b = swaps(counts[0]), swaps(counts[1])
        self.got = (got[:a], got[a : a + b], got[a + b :])

    def _part(self, axis, f):
        rows = self.nx if axis == 1 else self.ny
        return pl.ds(f * rows, rows)

    def near(self, axis, f):
        part = [r[self._part(axis, f), :] for r in self.got[axis]]
        before, after = self.sides[axis].incoming(part)
        if axis < 2:
            return before, after
        lane = lax.broadcasted_iota(jnp.int32, before.shape, 1)
        return jnp.where(lax.rem(lane, 2) == 0, before, after)

    def own(self, axis, f):
        if axis < 2:
            return [self.mine[axis][side, self._part(axis, f), :] for side in (0, 1)]
        return turn_z(self.mine[2][self._part(2, f), :])


def turn_z(pack):
    lane = lax.broadcasted_iota(jnp.int32, pack.shape, 1)
    even = lax.rem(lane, 2) == 0
    return jnp.where(even, pltpu.roll(pack, LANES - 1, 1), pltpu.roll(pack, 1, 1))


class Own:
    def __init__(self, dims, counts, refs, scratch=None):
        self.nx, self.ny = dims
        self.counts = counts
        self.x, self.y = scratch or refs[:2]
        self.z, *out = refs if scratch else refs[2:]
        a = swaps(counts[0])
        self.out = (out[:a], out[a:])

    def rows(self, f, x, value):
        self.y[0, pl.ds(f * self.nx + x, 1), :] = value[:1, :]
        self.y[1, pl.ds(f * self.nx + x, 1), :] = value[self.ny - 1 :, :]

    def finish(self, fields, packs):
        nx, ny = self.nx, self.ny
        for f, (ref, pack) in enumerate(zip(fields, packs)):
            part = pl.ds(f * ny, ny)
            self.x[0, part, :] = ref[pl.ds(0, ny), :]
            self.x[1, part, :] = ref[pl.ds((nx - 1) * ny, ny), :]
            self.z[part, :] = pack
        for axis, own in enumerate((self.x, self.y)):
            side = Side(AXES[axis], self.counts[axis])
            for o, v in zip(self.out[axis], side.outgoing(own[0], own[1])):
                o[...] = v


def own_shapes(dims, counts, fields):
    nx, ny = dims
    x, y = (fields * ny, LANES), (fields * nx, LANES)
    shapes = [(2, *x), (2, *y), x] + [x] * swaps(counts[0]) + [y] * swaps(counts[1])
    return [(v, F32) for v in shapes]


def send_faces(own, counts):
    a = swaps(counts[0])
    payloads = (own[3 : 3 + a], own[3 + a :], [own[2]] * swaps(counts[2]))
    got = []
    for axis, payload in enumerate(payloads):
        got += exchange(payload, counts, axis)
    return got


def at_plane(x, nx, pair):
    return jnp.where(x == 0, pair[0], jnp.where(x == nx - 1, pair[1], 0.0))


def at_rows(x, ref, f, nx, row, ny):
    part = pl.ds(f * nx + x, 1)
    first, last = ref[0, part, :], ref[1, part, :]
    if ny < 16:
        return jnp.where(row == 0, first, jnp.where(row == ny - 1, last, 0.0))
    parts = [jnp.where(row[:8] == 0, first, 0.0), jnp.where(row[:8] == 7, last, 0.0)]
    if ny > 16:
        parts.insert(1, jnp.zeros((ny - 16, LANES), F32))
    return jnp.concatenate(parts, axis=0)


def pack_edges(pair_x, pair_y, nx, ny):
    _, lane = grid_iota(ny)
    acc = jnp.zeros((ny, LANES), F32)
    for side, x in ((0, 0), (1, nx - 1)):
        acc = acc + pack_z(jnp.zeros_like(acc), pair_x[side], x, lane)
    x, lane = grid_iota(nx)
    row, _ = grid_iota(ny)
    for side, y in ((0, 0), (1, ny - 1)):
        moved = pltpu.roll(pair_y[side], 1, 1, stride=2, stride_axis=0)
        line = jnp.sum(jnp.where(lane // 2 == x, moved, 0.0), axis=0, keepdims=True)
        acc = acc + jnp.where(row == y, line, 0.0)
    return acc


def ready_z(value):
    lane = lax.broadcasted_iota(jnp.int32, value.shape, 1)
    return jnp.where(lax.rem(lane, 2) == 0, value, pltpu.roll(value, LANES - 2, 1))


def unpack_z(value, x):
    return pltpu.roll(value, lax.rem(LANES - 2 * x, LANES), 1)


def half_flux(k, t, kn, tn):
    return 0.5 * (k + kn) * (tn - t)


def divergence(flux_up, axis, index):
    size = flux_up.shape[axis]
    flux_up = jnp.where(index == size - 1, 0.0, flux_up)
    return flux_up - pltpu.roll(flux_up, 1, axis)


def ahead(value, axis):
    return pltpu.roll(value, value.shape[axis] - 1, axis)


def neighbour_sum(value, axis, index):
    size = value.shape[axis]
    up = jnp.where(index == size - 1, 0.0, ahead(value, axis))
    return up + jnp.where(index == 0, 0.0, pltpu.roll(value, 1, axis))


def log1p_of(e, u, inv):
    return jnp.log(u) + (e - (u - 1.0)) * inv


def softplus_parts(v):
    e = jnp.exp(-jnp.abs(v))
    u = 1.0 + e
    inv = 1.0 / u
    soft = jnp.maximum(v, 0.0) + log1p_of(e, u, inv)
    return soft, jnp.where(v >= 0, inv, e * inv)


def prepare_kernel(dims, counts, bins, chunks, *refs):
    nx, ny = dims
    c_hbm, t_hbm, s_hbm = refs[:3]
    k_ref, l_ref, m_ref, t_ref, s_ref = refs[3:8]
    own = Own(dims, counts, refs[8:-2])
    c_ref, sems = refs[-2:]
    rows = nx * ny // chunks
    copies = [
        pltpu.make_async_copy(t_hbm, t_ref, sems.at[chunks]),
        pltpu.make_async_copy(s_hbm, s_ref, sems.at[chunks + 1]),
    ]
    for j in range(chunks):
        part = pl.ds(j * rows, rows)
        copies.append(pltpu.make_async_copy(c_hbm.at[:, part, :], c_ref.at[:, part, :], sems.at[j]))
    for copy in copies:
        copy.start()
    copies[0].wait()
    copies[1].wait()
    _, lane = grid_iota(ny)
    weights = functional_weights(bins)

    def plane(x, accs):
        here = pl.ds(x * ny, ny)
        c = [c_ref[b, here, :] for b in range(bins)]
        values = []
        for const, per_bin in weights:
            total = None
            for b in range(bins):
                if per_bin[b] != 0.0:
                    term = float(per_bin[b]) * c[b]
                    total = term if total is None else total + term
            values.append(float(const) + total)
        k_ref[here, :], l_ref[here, :], m_ref[here, :] = values
        faces = (t_ref[here, :], s_ref[here, :], values[0])
        for f, v in enumerate(faces):
            own.rows(f, x, v)
        return tuple(pack_z(a, v, x, lane) for a, v in zip(accs, faces))

    accs = tuple(jnp.zeros((ny, LANES), F32) for _ in range(3))
    planes = nx // chunks
    for j in range(chunks):
        copies[2 + j].wait()
        accs = lax.fori_loop(j * planes, (j + 1) * planes, plane, accs, unroll=8)
    own.finish((t_ref, s_ref, k_ref), accs)


def first_inner_kernel(dims, unroll, *refs):
    nx, ny = dims
    t_ref, s_ref, k_ref, l_ref, m_ref, g_ref = refs[:6]
    t1, s1, h0, k1, l1, w0, v0, packs = refs[6:]
    row, lane = grid_iota(ny)

    def plane(x, carry):
        t, s, k, s_prev, flux_prev, accs = carry
        here = pl.ds(x * ny, ny)
        then = pl.ds(jnp.minimum(x + 1, nx - 1) * ny, ny)
        tn, sn, kn = t_ref[then, :], s_ref[then, :], k_ref[then, :]
        flux = half_flux(k, t, kn, tn)
        heat = (flux - flux_prev) + divergence(
            half_flux(k, t, ahead(k, 0), ahead(t, 0)), 0, row
        )
        heat = heat + divergence(half_flux(k, t, ahead(k, 1), ahead(t, 1)), 1, lane)
        s_next = jnp.where(x == nx - 1, 0.0, sn)
        diff = (s_prev + s_next) + neighbour_sum(s, 0, row)
        diff = diff + neighbour_sum(s, 1, lane) - 6.0 * s
        g, l, m = g_ref[here, :], l_ref[here, :], m_ref[here, :]
        soft, _ = softplus_parts(SOLIDIFY_POINT - LOWERING_COEF * s - t)
        w, v = soft * l, soft * m
        frost = g * w
        new_t = t + WARMTH_ADVANCE * heat + HIDDEN_WARMTH * frost
        new_s = s + STEP_SOLUTE * diff + REJECT * frost
        new_k = k + frost
        t1[here, :], s1[here, :], h0[here, :], k1[here, :] = new_t, new_s, heat, new_k
        l1[here, :], w0[here, :], v0[here, :] = l + g * v, w, v
        accs = tuple(pack_z(a, z, x, lane) for a, z in zip(accs, (new_t, new_s, new_k, heat)))
        return tn, sn, kn, s, flux, accs

    top = pl.ds(0, ny)
    zero = jnp.zeros((ny, LANES), F32)
    carry = (t_ref[top, :], s_ref[top, :], k_ref[top, :], zero, zero, (zero,) * 4)
    for f, acc in enumerate(lax.fori_loop(0, nx, plane, carry, unroll=unroll)[-1]):
        packs[pl.ds(f * ny, ny), :] = acc


def first_edge_kernel(dims, counts, unroll, *refs):
    nx, ny = dims
    ngot = sum(swaps(n) for n in counts)
    tp_ref, sp_ref, hp_ref, k1_ref, packs_ref = refs[:5]
    faces = Faces(dims, counts, refs[5:8], refs[8 : 8 + ngot])
    t1, s1, h0 = refs[8 + ngot : 11 + ngot]
    own = Own(dims, counts, refs[11 + ngot : -1])
    rows_ref = refs[-1]
    row, lane = grid_iota(ny)
    edge = (lane == 0) | (lane == LANES - 1)

    def flux_in(axis):
        tn, sn, kn = [faces.near(axis, f) for f in range(3)]
        to, ko = faces.own(axis, 0), faces.own(axis, 2)
        if axis == 2:
            return half_flux(ko, to, kn, tn), sn
        return [half_flux(*v) for v in zip(ko, to, kn, tn)], sn

    heat_x, sugar_x = flux_in(0)
    heat_y, sugar_y = flux_in(1)
    for side in (0, 1):
        rows_ref[side, pl.ds(0, nx), :] = heat_y[side]
        rows_ref[side, pl.ds(nx, nx), :] = sugar_y[side]
    heat_z, sugar_z = flux_in(2)
    in_heat, in_sugar = ready_z(heat_z), ready_z(sugar_z)

    def plane(x, _):
        here = pl.ds(x * ny, ny)
        heat = at_plane(x, nx, heat_x) + at_rows(x, rows_ref, 0, nx, row, ny)
        diff = at_plane(x, nx, sugar_x) + at_rows(x, rows_ref, 1, nx, row, ny)
        some_t = tp_ref[here, :] + WARMTH_ADVANCE * heat
        some_s = sp_ref[here, :] + STEP_SOLUTE * diff
        some_h = hp_ref[here, :] + heat
        heat = jnp.where(edge, unpack_z(in_heat, x), 0.0)
        diff = jnp.where(edge, unpack_z(in_sugar, x), 0.0)
        new_t = some_t + WARMTH_ADVANCE * heat
        new_s = some_s + STEP_SOLUTE * diff
        new_h = some_h + heat
        t1[here, :], s1[here, :], h0[here, :] = new_t, new_s, new_h
        for f, v in enumerate((new_t, new_s, k1_ref[here, :], new_h)):
            own.rows(f, x, v)
        return 0

    lax.fori_loop(0, nx, plane, 0, unroll=unroll)
    heat = turn_z(heat_z) + pack_edges(heat_x, heat_y, nx, ny)
    sugar = turn_z(sugar_z) + pack_edges(sugar_x, sugar_y, nx, ny)
    packs = [packs_ref[pl.ds(f * ny, ny), :] for f in range(4)]
    packs[0] = packs[0] + WARMTH_ADVANCE * heat
    packs[1] = packs[1] + STEP_SOLUTE * sugar
    packs[3] = packs[3] + heat
    own.finish((t1, s1, k1_ref, h0), packs)


def second_inner_kernel(dims, unroll, *refs):
    nx, ny = dims
    t_ref, s_ref, k_ref, h_ref, l_ref, w_ref, v_ref, g_ref, r_ref = refs[:9]
    mt_ref, ms_ref, by_pull_ref, with_miss_ref, with_pull_ref = refs[9:]
    row, lane = grid_iota(ny)

    def plane(x, carry):
        t, s, k, h, s_prev, flux_prev, other_prev = carry
        here = pl.ds(x * ny, ny)
        then = pl.ds(jnp.minimum(x + 1, nx - 1) * ny, ny)
        tn, sn, kn, hn = t_ref[then, :], s_ref[then, :], k_ref[then, :], h_ref[then, :]
        both = 0.5 * (k + kn)
        flux, other = both * (tn - t), both * (hn - h)
        heat, again = flux - flux_prev, other - other_prev
        for axis, index in ((0, row), (1, lane)):
            both = 0.5 * (k + ahead(k, axis))
            heat = heat + divergence(both * (ahead(t, axis) - t), axis, index)
            again = again + divergence(both * (ahead(h, axis) - h), axis, index)
        s_next = jnp.where(x == nx - 1, 0.0, sn)
        diff = (s_prev + s_next) + neighbour_sum(s, 0, row)
        diff = diff + neighbour_sum(s, 1, lane) - 6.0 * s
        g, l = g_ref[here, :], l_ref[here, :]
        soft, slope = softplus_parts(SOLIDIFY_POINT - LOWERING_COEF * s - t)
        frost = g * soft * l
        mt_ref[here, :] = (
            t + WARMTH_ADVANCE * heat + HIDDEN_WARMTH * frost - r_ref[0, here, :].astype(F32)
        )
        ms_ref[here, :] = s + STEP_SOLUTE * diff + REJECT * frost - r_ref[1, here, :].astype(F32)
        below = g * l * slope
        by_pull_ref[here, :] = soft * (l + g * v_ref[here, :]) + w_ref[here, :] * (
            1.0 - (HIDDEN_WARMTH + REJECT * LOWERING_COEF) * below
        )
        with_miss_ref[here, :] = heat + WARMTH_ADVANCE * again + h
        with_pull_ref[here, :] = below * h
        return tn, sn, kn, hn, s, flux, other

    top = pl.ds(0, ny)
    zero = jnp.zeros((ny, LANES), F32)
    start = [r[top, :] for r in (t_ref, s_ref, k_ref, h_ref)]
    lax.fori_loop(0, nx, plane, (*start, zero, zero, zero), unroll=unroll)


def second_edge_kernel(dims, counts, unroll, *refs):
    nx, ny = dims
    ngot = sum(swaps(n) for n in counts)
    mtp_ref, msp_ref, with_miss_ref, with_pull_ref = refs[:4]
    faces = Faces(dims, counts, refs[4:7], refs[7 : 7 + ngot])
    mt_ref, ms_ref, sums_ref = refs[7 + ngot : 10 + ngot]
    meet = refs[10 + ngot : 13 + ngot]
    own = Own(dims, counts, refs[13 + ngot : -3], refs[-2:])
    rows_ref = refs[-3]
    row, lane = grid_iota(ny)
    edge = (lane == 0) | (lane == LANES - 1)

    def flux_in(axis):
        tn, sn, kn, hn = [faces.near(axis, f) for f in range(4)]
        to, ko, ho = [faces.own(axis, f) for f in (0, 2, 3)]
        if axis == 2:
            meet[2][...] = (0.5 * ko + to) + (0.5 * kn - tn)
            return half_flux(ko, to, kn, tn), sn, half_flux(ko, ho, kn, hn)
        for side in (0, 1):
            meet[axis][side] = (0.5 * ko[side] + to[side]) + (0.5 * kn[side] - tn[side])
        heat = [half_flux(*v) for v in zip(ko, to, kn, tn)]
        return heat, sn, [half_flux(*v) for v in zip(ko, ho, kn, hn)]

    heat_x, sugar_x, again_x = flux_in(0)
    heat_y, sugar_y, again_y = flux_in(1)
    for side in (0, 1):
        rows_ref[side, pl.ds(0, nx), :] = heat_y[side]
        rows_ref[side, pl.ds(nx, nx), :] = sugar_y[side]
    heat_z, sugar_z, again_z = flux_in(2)
    in_heat, in_sugar = ready_z(heat_z), ready_z(sugar_z)

    def plane(x, carry):
        accs, misfit, part = carry
        here = pl.ds(x * ny, ny)
        heat = at_plane(x, nx, heat_x) + at_rows(x, rows_ref, 0, nx, row, ny)
        diff = at_plane(x, nx, sugar_x) + at_rows(x, rows_ref, 1, nx, row, ny)
        some_t = mtp_ref[here, :] + WARMTH_ADVANCE * heat
        some_s = msp_ref[here, :] + STEP_SOLUTE * diff
        heat = jnp.where(edge, unpack_z(in_heat, x), 0.0)
        diff = jnp.where(edge, unpack_z(in_sugar, x), 0.0)
        mt = some_t + WARMTH_ADVANCE * heat
        ms = some_s + STEP_SOLUTE * diff
        mt_ref[here, :], ms_ref[here, :] = mt, ms
        misfit = misfit + (mt * mt + ms * ms)
        pull = HIDDEN_WARMTH * mt + REJECT * ms
        part = part + (mt * with_miss_ref[here, :] - pull * with_pull_ref[here, :])
        for f, v in enumerate((mt, ms)):
            own.rows(f, x, v)
        accs = tuple(pack_z(a, z, x, lane) for a, z in zip(accs, (some_t, some_s)))
        return accs, misfit, part

    zero = jnp.zeros((ny, LANES), F32)
    accs, misfit, part = lax.fori_loop(
        0, nx, plane, ((zero, zero), zero, zero), unroll=unroll
    )
    packs = (
        accs[0] + WARMTH_ADVANCE * turn_z(heat_z),
        accs[1] + STEP_SOLUTE * turn_z(sugar_z),
    )
    own.finish((mt_ref, ms_ref), packs)
    part = part + turn_z(packs[0]) * (heat_z + WARMTH_ADVANCE * again_z)
    rows = None
    for side in (0, 1):
        part = part + own.x[side, pl.ds(0, ny), :] * (
            heat_x[side] + WARMTH_ADVANCE * again_x[side]
        )
        line = own.y[side, pl.ds(0, nx), :] * (heat_y[side] + WARMTH_ADVANCE * again_y[side])
        rows = line if rows is None else rows + line
    for first in range(0, nx, ny):
        part = part + rows[first : first + ny]
    lane_row = lax.broadcasted_iota(jnp.int32, (1, LANES), 1)
    line = jnp.where(lane_row == 0, 0.5 * jnp.sum(misfit), 0.0)
    line = jnp.where(lane_row == 1, WARMTH_ADVANCE * jnp.sum(part), line)
    sums_ref[...] = jnp.broadcast_to(line, sums_ref.shape)


FLUX_WEIGHT = 0.5 * WARMTH_ADVANCE
SUGAR_WEIGHT = REJECT * STEP_SOLUTE


def crossing(k, t, mt, kn, tn, mtn, msn):
    return FLUX_WEIGHT * (mtn - mt) * (0.5 * (k + kn) + (t - tn)) + SUGAR_WEIGHT * msn


def third_inner_kernel(dims, unroll, *refs):
    nx, ny = dims
    t_ref, k_ref, mt_ref, ms_ref, w_ref, by_pull_ref = refs[:6]
    out_ref, x_ref, y_ref = refs[6:]
    row, lane = grid_iota(ny)
    x_ref[0], x_ref[1] = mt_ref[pl.ds(0, ny), :], mt_ref[pl.ds((nx - 1) * ny, ny), :]

    def plane(x, carry):
        t, k, mt, ms, from_prev = carry
        here = pl.ds(x * ny, ny)
        then = pl.ds(jnp.minimum(x + 1, nx - 1) * ny, ny)
        tn, kn, mtn, msn = [r[then, :] for r in (t_ref, k_ref, mt_ref, ms_ref)]
        y_ref[0, pl.ds(x, 1), :], y_ref[1, pl.ds(x, 1), :] = mt[:1, :], mt[ny - 1 :, :]
        total = from_prev - (6.0 * SUGAR_WEIGHT) * ms
        total = total + jnp.where(x == nx - 1, 0.0, crossing(k, t, mt, kn, tn, mtn, msn))
        to_next = crossing(kn, tn, mtn, k, t, mt, ms)
        for axis, index in ((0, row), (1, lane)):
            size = ny if axis == 0 else LANES
            ta, ka, mta, msa = [ahead(v, axis) for v in (t, k, mt, ms)]
            up = crossing(k, t, mt, ka, ta, mta, msa)
            down = crossing(ka, ta, mta, k, t, mt, ms)
            total = total + jnp.where(index == size - 1, 0.0, up)
            total = total + jnp.where(index == 0, 0.0, pltpu.roll(down, 1, axis))
        pull = HIDDEN_WARMTH * mt + REJECT * ms
        out_ref[here, :] = by_pull_ref[here, :] * pull + w_ref[here, :] * total
        return tn, kn, mtn, msn, to_next

    top = pl.ds(0, ny)
    start = [r[top, :] for r in (t_ref, k_ref, mt_ref, ms_ref)]
    lax.fori_loop(0, nx, plane, (*start, jnp.zeros((ny, LANES), F32)), unroll=unroll)


def finish_kernel(dims, counts, unroll, *refs):
    nx, ny = dims
    ngot = sum(swaps(n) for n in counts)
    w_ref, sense_ref = refs[:2]
    meet = refs[2:5]
    faces = Faces(dims, counts, refs[5:8], refs[8 : 8 + ngot])
    out_ref, rows_ref = refs[8 + ngot :]
    row, lane = grid_iota(ny)
    edge = (lane == 0) | (lane == LANES - 1)

    def into(axis):
        own, near, sugar = faces.own(axis, 0), faces.near(axis, 0), faces.near(axis, 1)
        if axis == 2:
            return FLUX_WEIGHT * (near - own) * meet[2][...] + SUGAR_WEIGHT * sugar
        return [
            FLUX_WEIGHT * (near[side] - own[side]) * meet[axis][side] + SUGAR_WEIGHT * sugar[side]
            for side in (0, 1)
        ]

    into_x, into_y, into_z = into(0), into(1), ready_z(into(2))
    rows_ref[0], rows_ref[1] = into_y

    def plane(x, _):
        here = pl.ds(x * ny, ny)
        value = jnp.where(edge, unpack_z(into_z, x), 0.0) + at_plane(x, nx, into_x)
        value = value + at_rows(x, rows_ref, 0, nx, row, ny)
        out_ref[here, :] = sense_ref[here, :] + w_ref[here, :] * value
        return 0

    lax.fori_loop(0, nx, plane, 0, unroll=unroll)


def totals_kernel(cells, sums_ref, misfit_ref, gradient_ref):
    sums = sums_ref[...]
    which = lax.broadcasted_iota(jnp.int32, sums.shape, 1)
    misfit_ref[0, 0] = jnp.sum(jnp.where(which == 0, sums, 0.0)) / cells
    gradient_ref[0, 0] = jnp.sum(jnp.where(which == 1, sums, 0.0)) / cells


VM = pl.BlockSpec(memory_space=pltpu.VMEM)
SM = pl.BlockSpec(memory_space=pltpu.SMEM)


def call(kernel, out, args, name, scratch=(), in_specs=None, out_specs=None, vmem=32, flops=0, aliases={}):
    size = sum(int(np.prod(a.shape)) * a.dtype.itemsize for a in args)
    return pl.pallas_call(
        kernel,
        out_shape=[jax.ShapeDtypeStruct(s, d) for s, d in out],
        in_specs=in_specs or [VM] * len(args),
        out_specs=out_specs or [VM] * len(out),
        scratch_shapes=list(scratch),
        name=name,
        input_output_aliases=aliases,
        cost_estimate=pl.CostEstimate(flops=flops, bytes_accessed=size, transcendentals=0),
        compiler_params=pltpu.CompilerParams(vmem_limit_bytes=vmem << 20),
    )(*args)


def per_device(counts, warmth, sugar, population, coefficient, sensors):
    nx, ny, nz = warmth.shape
    assert nz == LANES and 2 * nx <= LANES
    bins = population.shape[0]
    dims = (nx, ny)
    cells = nx * ny
    t, s, g = [v.reshape(cells, nz) for v in (warmth, sugar, coefficient)]
    c = population.reshape(bins, cells, nz)
    r = sensors.reshape(2, cells, nz)
    field = ((cells, nz), F32)
    hbm = pl.BlockSpec(memory_space=pl.ANY)
    work = cells * nz * 100

    chunks = 8
    res = call(
        functools.partial(prepare_kernel, dims, counts, bins, chunks),
        [field] * 5 + own_shapes(dims, counts, 3),
        (c, t, s),
        "prepare",
        [pltpu.VMEM((bins, cells, nz), F32), pltpu.SemaphoreType.DMA((chunks + 2,))],
        in_specs=[hbm] * 3,
        vmem=51,
    )
    k, l, m, t, s = res[:5]
    own = res[5:]
    got = send_faces(own, counts)
    pack = ((4 * ny, nz), F32)
    tp, sp, hp, k1, l1, w, v, packs = call(
        functools.partial(first_inner_kernel, dims, 8),
        [field] * 7 + [pack],
        (t, s, k, l, m, g),
        "first_inner",
        flops=work,
    )
    res = call(
        functools.partial(first_edge_kernel, dims, counts, 64),
        [field] * 3 + own_shapes(dims, counts, 4),
        (tp, sp, hp, k1, packs, *own[:3], *got),
        "first_edge",
        [pltpu.VMEM((2, 2 * nx, nz), F32)],
    )
    t1, s1, h0 = res[:3]
    own1 = res[3:]
    got1 = send_faces(own1, counts)
    mtp, msp, by_pull, *inner = call(
        functools.partial(second_inner_kernel, dims, 8),
        [field] * 5,
        (t1, s1, k1, h0, l1, w, v, g, r),
        "second_inner",
        flops=work,
    )
    devices = int(np.prod(counts))
    line = ((devices, LANES), F32)
    meet_shapes = own_shapes(dims, counts, 1)[:3]
    res = call(
        functools.partial(second_edge_kernel, dims, counts, 64),
        [field] * 2 + [line] + meet_shapes + own_shapes(dims, counts, 2)[2:],
        (mtp, msp, *inner, *own1[:3], *got1),
        "second_edge",
        [pltpu.VMEM(v, F32) for v in ((2, 2 * nx, nz), (2, 2 * ny, nz), (2, 2 * nx, nz))],
    )
    mt, ms, sums = res[:3]
    meet, sent = res[3:6], res[6:]
    got2 = send_faces((None, None, *sent), counts)
    sums = lax.all_to_all(sums, AXES, 0, 0, tiled=True)
    sense, *kept = call(
        functools.partial(third_inner_kernel, dims, 16),
        [field] + meet_shapes[:2],
        (t1, k1, mt, ms, w, by_pull),
        "third_inner",
        aliases={5: 0},
        flops=work,
    )
    (sens,) = call(
        functools.partial(finish_kernel, dims, counts, 64),
        [field],
        (w, sense, *meet, *kept, sent[0], *got2),
        "finish",
        [pltpu.VMEM((2, nx, nz), F32)],
        flops=work,
    )
    sums, sens = lax.optimization_barrier((sums, sens))
    misfit, gradient = call(
        functools.partial(totals_kernel, float(cells * nz * devices)),
        [((1, 1), F32), ((1, 1), F32)],
        (sums,),
        "totals",
        out_specs=[SM, SM],
    )
    return sens.reshape(nx, ny, nz), misfit.reshape(()), gradient.reshape(())


def solution(mesh):
    counts = tuple(mesh.shape[a] for a in AXES)
    placed = (
        P("gx", "gy", "gz"),
        P("gx", "gy", "gz"),
        P(None, "gx", "gy", "gz"),
        P("gx", "gy", "gz"),
        P(None, "gx", "gy", "gz"),
    )
    return jax.shard_map(
        functools.partial(per_device, counts),
        mesh=mesh,
        in_specs=placed,
        out_specs=(P("gx", "gy", "gz"), P(), P()),
        check_vma=False,
    )
```

```python
import functools

import jax
import jax.numpy as jnp
import numpy as np
from jax import lax
from jax.experimental import pallas as pl
from jax.experimental.pallas import tpu as pltpu
from jax.sharding import PartitionSpec as P

F32 = jnp.float32
AXES = ("gx", "gy", "gz")

SOLIDIFY_POINT = 0.5
LOWERING_COEF = 0.5
GROW = 0.3
NUCLEATE = 0.2
VOLUME = 0.005
WARMTH_ADVANCE = 0.08
STEP_SOLUTE = 0.1
HIDDEN_WARMTH = 0.5
REJECT = 0.3
LANES = 128


def volumes(bin_count):
    rank = np.arange(bin_count, dtype=np.float64) + 1.0
    return VOLUME * rank * rank


def functional_weights(bin_count):
    vol = volumes(bin_count)
    step = vol[1:] - vol[:-1]
    k = (1.0, vol)
    l = (NUCLEATE * vol[0], np.concatenate([GROW * step, [0.0]]))
    m_const = GROW * step[0] * NUCLEATE
    m = np.zeros(bin_count)
    for b in range(bin_count - 1):
        m[b] -= GROW * step[b] * GROW
        if b >= 1:
            m[b - 1] += GROW * step[b] * GROW
    return k, l, (m_const, m)


SPARE = {"gx": 0, "gz": 0, "gy": 2}


def swap_pairs(counts, axis, kind):
    pairs = []
    for at in np.ndindex(*counts):
        to = list(at)
        i = at[axis]
        to[axis] = i ^ 1 if kind == 0 else (i + 1 if i % 2 else i - 1)
        if not 0 <= to[axis] < counts[axis]:
            to[axis] = i
            spare = SPARE[AXES[axis]]
            if spare == axis:
                to[axis] = counts[axis] - 1 - i
            else:
                to[spare] = at[spare] ^ 1
        pairs.append(tuple(int(np.ravel_multi_index(v, counts)) for v in (at, to)))
    return pairs


def swaps(count):
    return {1: 0, 2: 1}.get(count, 2)


def exchange(payloads, counts, axis):
    assert counts[axis] == 1 or counts[axis] % 2 == 0
    return [
        lax.ppermute(p, AXES, swap_pairs(counts, axis, kind)) for kind, p in enumerate(payloads)
    ]


class Side:
    def __init__(self, axis, count):
        self.count = count
        self.index = lax.axis_index(axis)
        self.odd = lax.rem(self.index, 2) == 1

    def outgoing(self, first, last):
        kinds = [jnp.where(self.odd, first, last), jnp.where(self.odd, last, first)]
        return kinds[: swaps(self.count)]

    def incoming(self, got):
        if self.count == 1:
            return None
        if self.count == 2:
            zero = jnp.zeros_like(got[0])
            return jnp.where(self.odd, got[0], zero), jnp.where(self.odd, zero, got[0])
        a, b = got
        zero = jnp.zeros_like(a)
        before = jnp.where(self.index > 0, jnp.where(self.odd, a, b), zero)
        after = jnp.where(self.index < self.count - 1, jnp.where(self.odd, b, a), zero)
        return before, after


def grid_iota(ny):
    row = lax.broadcasted_iota(jnp.int32, (ny, LANES), 0)
    lane = lax.broadcasted_iota(jnp.int32, (ny, LANES), 1)
    return row, lane


def pack_z(acc, value, x, lane):
    return jnp.where(lane // 2 == x, pltpu.roll(value, lax.rem(2 * x + 1, LANES), 1), acc)


class Faces:
    def __init__(self, dims, counts, own, got):
        self.nx, self.ny = dims
        self.sides = [Side(a, n) for a, n in zip(AXES, counts)]
        self.mine = own
        a, b = swaps(counts[0]), swaps(counts[1])
        self.got = (got[:a], got[a : a + b], got[a + b :])

    def _part(self, axis, f):
        rows = self.nx if axis == 1 else self.ny
        return pl.ds(f * rows, rows)

    def near(self, axis, f):
        part = [r[self._part(axis, f), :] for r in self.got[axis]]
        before, after = self.sides[axis].incoming(part)
        if axis < 2:
            return before, after
        lane = lax.broadcasted_iota(jnp.int32, before.shape, 1)
        return jnp.where(lax.rem(lane, 2) == 0, before, after)

    def own(self, axis, f):
        if axis < 2:
            return [self.mine[axis][side, self._part(axis, f), :] for side in (0, 1)]
        return turn_z(self.mine[2][self._part(2, f), :])


def turn_z(pack):
    lane = lax.broadcasted_iota(jnp.int32, pack.shape, 1)
    even = lax.rem(lane, 2) == 0
    return jnp.where(even, pltpu.roll(pack, LANES - 1, 1), pltpu.roll(pack, 1, 1))


class Own:
    def __init__(self, dims, counts, refs, scratch=None):
        self.nx, self.ny = dims
        self.counts = counts
        self.x, self.y = scratch or refs[:2]
        self.z, *out = refs if scratch else refs[2:]
        a = swaps(counts[0])
        self.out = (out[:a], out[a:])

    def rows(self, f, x, value):
        self.y[0, pl.ds(f * self.nx + x, 1), :] = value[:1, :]
        self.y[1, pl.ds(f * self.nx + x, 1), :] = value[self.ny - 1 :, :]

    def finish(self, fields, packs):
        nx, ny = self.nx, self.ny
        for f, (ref, pack) in enumerate(zip(fields, packs)):
            part = pl.ds(f * ny, ny)
            self.x[0, part, :] = ref[pl.ds(0, ny), :]
            self.x[1, part, :] = ref[pl.ds((nx - 1) * ny, ny), :]
            self.z[part, :] = pack
        for axis, own in enumerate((self.x, self.y)):
            side = Side(AXES[axis], self.counts[axis])
            for o, v in zip(self.out[axis], side.outgoing(own[0], own[1])):
                o[...] = v


def choose_kernel(counts, rows_ref, *outs):
    for o, v in zip(outs, Side(AXES[1], counts[1]).outgoing(rows_ref[0], rows_ref[1])):
        o[...] = v


def own_shapes(dims, counts, fields):
    nx, ny = dims
    x, y = (fields * ny, LANES), (fields * nx, LANES)
    shapes = [(2, *x), (2, *y), x] + [x] * swaps(counts[0]) + [y] * swaps(counts[1])
    return [(v, F32) for v in shapes]


def send_faces(own, counts):
    a = swaps(counts[0])
    payloads = (own[3 : 3 + a], own[3 + a :], [own[2]] * swaps(counts[2]))
    got = []
    for axis, payload in enumerate(payloads):
        got += exchange(payload, counts, axis)
    return got


def at_plane(x, nx, pair):
    return jnp.where(x == 0, pair[0], jnp.where(x == nx - 1, pair[1], 0.0))


def at_rows(x, ref, f, nx, row, ny):
    part = pl.ds(f * nx + x, 1)
    first, last = ref[0, part, :], ref[1, part, :]
    if ny < 16:
        return jnp.where(row == 0, first, jnp.where(row == ny - 1, last, 0.0))
    parts = [jnp.where(row[:8] == 0, first, 0.0), jnp.where(row[:8] == 7, last, 0.0)]
    if ny > 16:
        parts.insert(1, jnp.zeros((ny - 16, LANES), F32))
    return jnp.concatenate(parts, axis=0)


def pack_edges(pair_x, pair_y, nx, ny):
    _, lane = grid_iota(ny)
    acc = jnp.zeros((ny, LANES), F32)
    for side, x in ((0, 0), (1, nx - 1)):
        acc = acc + pack_z(jnp.zeros_like(acc), pair_x[side], x, lane)
    x, lane = grid_iota(nx)
    row, _ = grid_iota(ny)
    for side, y in ((0, 0), (1, ny - 1)):
        moved = pltpu.roll(pair_y[side], 1, 1, stride=2, stride_axis=0)
        line = jnp.sum(jnp.where(lane // 2 == x, moved, 0.0), axis=0, keepdims=True)
        acc = acc + jnp.where(row == y, line, 0.0)
    return acc


def ready_z(value):
    lane = lax.broadcasted_iota(jnp.int32, value.shape, 1)
    return jnp.where(lax.rem(lane, 2) == 0, value, pltpu.roll(value, LANES - 2, 1))


def unpack_z(value, x):
    return pltpu.roll(value, lax.rem(LANES - 2 * x, LANES), 1)


def half_flux(k, t, kn, tn):
    return 0.5 * (k + kn) * (tn - t)


def behind(value, axis):
    return pltpu.roll(value, 1, axis)


def divergence(k, fields, axis, index):
    last = index == k.shape[axis] - 1
    up, down = 0.5 * (k + ahead(k, axis)), 0.5 * (k + behind(k, axis))
    up, down = jnp.where(last, 0.0, up), jnp.where(index == 0, 0.0, down)
    return [up * (ahead(v, axis) - v) + down * (behind(v, axis) - v) for v in fields]


def ahead(value, axis):
    return pltpu.roll(value, value.shape[axis] - 1, axis)


def neighbour_sum(value, axis, index):
    size = value.shape[axis]
    up = jnp.where(index == size - 1, 0.0, ahead(value, axis))
    return up + jnp.where(index == 0, 0.0, pltpu.roll(value, 1, axis))


def log1p_of(e, u, inv):
    return jnp.log(u) + (e - (u - 1.0)) * inv


def softplus_parts(v):
    e = jnp.exp(-jnp.abs(v))
    u = 1.0 + e
    inv = 1.0 / u
    soft = jnp.maximum(v, 0.0) + log1p_of(e, u, inv)
    return soft, jnp.where(v >= 0, inv, e * inv)


def prepare_kernel(dims, counts, bins, chunks, *refs):
    nx, ny = dims
    c_hbm, t_hbm, s_hbm = refs[:3]
    k_ref, l_ref, m_ref, t_ref, s_ref = refs[3:8]
    own = Own(dims, counts, refs[8:-2])
    c_ref, sems = refs[-2:]
    rows = nx * ny // chunks
    copies = [
        pltpu.make_async_copy(t_hbm, t_ref, sems.at[chunks]),
        pltpu.make_async_copy(s_hbm, s_ref, sems.at[chunks + 1]),
    ]
    for j in range(chunks):
        part = pl.ds(j * rows, rows)
        copies.append(pltpu.make_async_copy(c_hbm.at[:, part, :], c_ref.at[:, part, :], sems.at[j]))
    for copy in copies:
        copy.start()
    copies[0].wait()
    copies[1].wait()
    _, lane = grid_iota(ny)
    weights = functional_weights(bins)

    def plane(x, accs):
        here = pl.ds(x * ny, ny)
        c = [c_ref[b, here, :] for b in range(bins)]
        values = []
        for const, per_bin in weights:
            total = None
            for b in range(bins):
                if per_bin[b] != 0.0:
                    term = float(per_bin[b]) * c[b]
                    total = term if total is None else total + term
            values.append(float(const) + total)
        k_ref[here, :], l_ref[here, :], m_ref[here, :] = values
        faces = (t_ref[here, :], s_ref[here, :], values[0])
        for f, v in enumerate(faces):
            own.rows(f, x, v)
        return tuple(pack_z(a, v, x, lane) for a, v in zip(accs, faces))

    accs = tuple(jnp.zeros((ny, LANES), F32) for _ in range(3))
    planes = nx // chunks
    for j in range(chunks):
        copies[2 + j].wait()
        accs = lax.fori_loop(j * planes, (j + 1) * planes, plane, accs, unroll=8)
    own.finish((t_ref, s_ref, k_ref), accs)


def first_inner_kernel(dims, unroll, *refs):
    nx, ny = dims
    t_ref, s_ref, k_ref, l_ref, m_ref, g_ref = refs[:6]
    t1, s1, h0, k1, l1, w0, v0, packs = refs[6:]
    row, lane = grid_iota(ny)

    def plane(x, carry):
        t, s, k, s_prev, flux_prev = carry
        here = pl.ds(x * ny, ny)
        then = pl.ds(jnp.minimum(x + 1, nx - 1) * ny, ny)
        tn, sn, kn = t_ref[then, :], s_ref[then, :], k_ref[then, :]
        flux = half_flux(k, t, kn, tn)
        heat = flux - flux_prev
        for axis, index in ((0, row), (1, lane)):
            heat = heat + divergence(k, (t,), axis, index)[0]
        s_next = jnp.where(x == nx - 1, 0.0, sn)
        diff = (s_prev + s_next) + neighbour_sum(s, 0, row)
        diff = diff + neighbour_sum(s, 1, lane) - 6.0 * s
        g, l, m = g_ref[here, :], l_ref[here, :], m_ref[here, :]
        soft, _ = softplus_parts(SOLIDIFY_POINT - LOWERING_COEF * s - t)
        w, v = soft * l, soft * m
        frost = g * w
        new_t = t + WARMTH_ADVANCE * heat + HIDDEN_WARMTH * frost
        new_s = s + STEP_SOLUTE * diff + REJECT * frost
        new_k = k + frost
        t1[here, :], s1[here, :], h0[here, :], k1[here, :] = new_t, new_s, heat, new_k
        l1[here, :], w0[here, :], v0[here, :] = l + g * v, w, v
        return tn, sn, kn, s, flux

    top = pl.ds(0, ny)
    zero = jnp.zeros((ny, LANES), F32)
    carry = (t_ref[top, :], s_ref[top, :], k_ref[top, :], zero, zero)
    lax.fori_loop(0, nx, plane, carry, unroll=unroll)
    fields = (t1, s1, k1, h0)

    def pack(x, accs):
        here = pl.ds(x * ny, ny)
        return tuple(pack_z(a, r[here, :], x, lane) for a, r in zip(accs, fields))

    for f, acc in enumerate(lax.fori_loop(0, nx, pack, (zero,) * 4, unroll=64)):
        packs[pl.ds(f * ny, ny), :] = acc


def first_edge_kernel(dims, counts, unroll, *refs):
    nx, ny = dims
    ngot = sum(swaps(n) for n in counts)
    tp_ref, sp_ref, hp_ref, k1_ref, packs_ref = refs[:5]
    faces = Faces(dims, counts, refs[5:8], refs[8 : 8 + ngot])
    t1, s1, h0 = refs[8 + ngot : 11 + ngot]
    own = Own(dims, counts, refs[11 + ngot : -1])
    rows_ref = refs[-1]
    row, lane = grid_iota(ny)
    edge = (lane == 0) | (lane == LANES - 1)

    def flux_in(axis):
        tn, sn, kn = [faces.near(axis, f) for f in range(3)]
        to, ko = faces.own(axis, 0), faces.own(axis, 2)
        if axis == 2:
            return half_flux(ko, to, kn, tn), sn
        return [half_flux(*v) for v in zip(ko, to, kn, tn)], sn

    heat_x, sugar_x = flux_in(0)
    heat_y, sugar_y = flux_in(1)
    for side in (0, 1):
        rows_ref[side, pl.ds(0, nx), :] = heat_y[side]
        rows_ref[side, pl.ds(nx, nx), :] = sugar_y[side]
    heat_z, sugar_z = flux_in(2)
    in_heat, in_sugar = ready_z(heat_z), ready_z(sugar_z)

    def plane(x, _):
        here = pl.ds(x * ny, ny)
        heat = at_plane(x, nx, heat_x) + at_rows(x, rows_ref, 0, nx, row, ny)
        diff = at_plane(x, nx, sugar_x) + at_rows(x, rows_ref, 1, nx, row, ny)
        some_t = tp_ref[here, :] + WARMTH_ADVANCE * heat
        some_s = sp_ref[here, :] + STEP_SOLUTE * diff
        some_h = hp_ref[here, :] + heat
        heat = jnp.where(edge, unpack_z(in_heat, x), 0.0)
        diff = jnp.where(edge, unpack_z(in_sugar, x), 0.0)
        new_t = some_t + WARMTH_ADVANCE * heat
        new_s = some_s + STEP_SOLUTE * diff
        new_h = some_h + heat
        t1[here, :], s1[here, :], h0[here, :] = new_t, new_s, new_h
        for f, v in enumerate((new_t, new_s, k1_ref[here, :], new_h)):
            own.rows(f, x, v)
        return 0

    lax.fori_loop(0, nx, plane, 0, unroll=unroll)
    heat = turn_z(heat_z) + pack_edges(heat_x, heat_y, nx, ny)
    sugar = turn_z(sugar_z) + pack_edges(sugar_x, sugar_y, nx, ny)
    packs = [packs_ref[pl.ds(f * ny, ny), :] for f in range(4)]
    packs[0] = packs[0] + WARMTH_ADVANCE * heat
    packs[1] = packs[1] + STEP_SOLUTE * sugar
    packs[3] = packs[3] + heat
    own.finish((t1, s1, k1_ref, h0), packs)


def second_inner_kernel(dims, unroll, *refs):
    nx, ny = dims
    t_ref, s_ref, k_ref, h_ref, l_ref, w_ref, v_ref, g_ref, r_ref = refs[:9]
    mt_ref, ms_ref, by_pull_ref, with_miss_ref, with_pull_ref = refs[9:]
    row, lane = grid_iota(ny)

    def plane(x, carry):
        t, s, k, h, s_prev, flux_prev, other_prev = carry
        here = pl.ds(x * ny, ny)
        then = pl.ds(jnp.minimum(x + 1, nx - 1) * ny, ny)
        tn, sn, kn, hn = t_ref[then, :], s_ref[then, :], k_ref[then, :], h_ref[then, :]
        both = 0.5 * (k + kn)
        flux, other = both * (tn - t), both * (hn - h)
        heat, again = flux - flux_prev, other - other_prev
        for axis, index in ((0, row), (1, lane)):
            more, other_more = divergence(k, (t, h), axis, index)
            heat, again = heat + more, again + other_more
        s_next = jnp.where(x == nx - 1, 0.0, sn)
        diff = (s_prev + s_next) + neighbour_sum(s, 0, row)
        diff = diff + neighbour_sum(s, 1, lane) - 6.0 * s
        g, l = g_ref[here, :], l_ref[here, :]
        soft, slope = softplus_parts(SOLIDIFY_POINT - LOWERING_COEF * s - t)
        frost = g * soft * l
        mt_ref[here, :] = (
            t + WARMTH_ADVANCE * heat + HIDDEN_WARMTH * frost - r_ref[0, here, :].astype(F32)
        )
        ms_ref[here, :] = s + STEP_SOLUTE * diff + REJECT * frost - r_ref[1, here, :].astype(F32)
        below = g * l * slope
        by_pull_ref[here, :] = soft * (l + g * v_ref[here, :]) + w_ref[here, :] * (
            1.0 - (HIDDEN_WARMTH + REJECT * LOWERING_COEF) * below
        )
        with_miss_ref[here, :] = heat + WARMTH_ADVANCE * again + h
        with_pull_ref[here, :] = below * h
        return tn, sn, kn, hn, s, flux, other

    top = pl.ds(0, ny)
    zero = jnp.zeros((ny, LANES), F32)
    start = [r[top, :] for r in (t_ref, s_ref, k_ref, h_ref)]
    lax.fori_loop(0, nx, plane, (*start, zero, zero, zero), unroll=unroll)


def second_edge_kernel(dims, counts, unroll, *refs):
    nx, ny = dims
    ngot = sum(swaps(n) for n in counts)
    mtp_ref, msp_ref, with_miss_ref, with_pull_ref = refs[:4]
    faces = Faces(dims, counts, refs[4:7], refs[7 : 7 + ngot])
    mt_ref, ms_ref, sums_ref = refs[7 + ngot : 10 + ngot]
    meet = refs[10 + ngot : 13 + ngot]
    own = Own(dims, counts, refs[13 + ngot : -3], (refs[-1], refs[-3]))
    rows_ref = refs[-2]
    row, lane = grid_iota(ny)
    edge = (lane == 0) | (lane == LANES - 1)

    def flux_in(axis):
        tn, sn, kn, hn = [faces.near(axis, f) for f in range(4)]
        to, ko, ho = [faces.own(axis, f) for f in (0, 2, 3)]
        if axis == 2:
            meet[2][...] = (0.5 * ko + to) + (0.5 * kn - tn)
            return half_flux(ko, to, kn, tn), sn, half_flux(ko, ho, kn, hn)
        for side in (0, 1):
            meet[axis][side] = (0.5 * ko[side] + to[side]) + (0.5 * kn[side] - tn[side])
        heat = [half_flux(*v) for v in zip(ko, to, kn, tn)]
        return heat, sn, [half_flux(*v) for v in zip(ko, ho, kn, hn)]

    heat_x, sugar_x, again_x = flux_in(0)
    heat_y, sugar_y, again_y = flux_in(1)
    for side in (0, 1):
        rows_ref[side, pl.ds(0, nx), :] = heat_y[side]
        rows_ref[side, pl.ds(nx, nx), :] = sugar_y[side]
    heat_z, sugar_z, again_z = flux_in(2)
    in_heat, in_sugar = ready_z(heat_z), ready_z(sugar_z)

    def plane(x, carry):
        accs, misfit, part = carry
        here = pl.ds(x * ny, ny)
        heat = at_plane(x, nx, heat_x) + at_rows(x, rows_ref, 0, nx, row, ny)
        diff = at_plane(x, nx, sugar_x) + at_rows(x, rows_ref, 1, nx, row, ny)
        some_t = mtp_ref[here, :] + WARMTH_ADVANCE * heat
        some_s = msp_ref[here, :] + STEP_SOLUTE * diff
        heat = jnp.where(edge, unpack_z(in_heat, x), 0.0)
        diff = jnp.where(edge, unpack_z(in_sugar, x), 0.0)
        mt = some_t + WARMTH_ADVANCE * heat
        ms = some_s + STEP_SOLUTE * diff
        mt_ref[here, :], ms_ref[here, :] = mt, ms
        misfit = misfit + (mt * mt + ms * ms)
        pull = HIDDEN_WARMTH * mt + REJECT * ms
        part = part + (mt * with_miss_ref[here, :] - pull * with_pull_ref[here, :])
        for f, v in enumerate((mt, ms)):
            own.rows(f, x, v)
        accs = tuple(pack_z(a, z, x, lane) for a, z in zip(accs, (some_t, some_s)))
        return accs, misfit, part

    zero = jnp.zeros((ny, LANES), F32)
    accs, misfit, part = lax.fori_loop(
        0, nx, plane, ((zero, zero), zero, zero), unroll=unroll
    )
    packs = (
        accs[0] + WARMTH_ADVANCE * turn_z(heat_z),
        accs[1] + STEP_SOLUTE * turn_z(sugar_z),
    )
    own.finish((mt_ref, ms_ref), packs)
    part = part + turn_z(packs[0]) * (heat_z + WARMTH_ADVANCE * again_z)
    rows = None
    for side in (0, 1):
        part = part + own.x[side, pl.ds(0, ny), :] * (
            heat_x[side] + WARMTH_ADVANCE * again_x[side]
        )
        line = own.y[side, pl.ds(0, nx), :] * (heat_y[side] + WARMTH_ADVANCE * again_y[side])
        rows = line if rows is None else rows + line
    for first in range(0, nx, ny):
        part = part + rows[first : first + ny]
    lane_row = lax.broadcasted_iota(jnp.int32, (1, LANES), 1)
    line = jnp.where(lane_row == 0, 0.5 * jnp.sum(misfit), 0.0)
    line = jnp.where(lane_row == 1, WARMTH_ADVANCE * jnp.sum(part), line)
    sums_ref[...] = jnp.broadcast_to(line, sums_ref.shape)


FLUX_WEIGHT = 0.5 * WARMTH_ADVANCE
SUGAR_WEIGHT = REJECT * STEP_SOLUTE


def crossing(k, t, mt, kn, tn, mtn, msn):
    return FLUX_WEIGHT * (mtn - mt) * (0.5 * (k + kn) + (t - tn)) + SUGAR_WEIGHT * msn


def third_inner_kernel(dims, unroll, *refs):
    nx, ny = dims
    t_ref, k_ref, mt_ref, ms_ref, w_ref, by_pull_ref = refs[:6]
    out_ref, x_ref, y_ref = refs[6:]
    row, lane = grid_iota(ny)
    x_ref[0], x_ref[1] = mt_ref[pl.ds(0, ny), :], mt_ref[pl.ds((nx - 1) * ny, ny), :]

    def plane(x, carry):
        t, k, mt, ms, from_prev = carry
        here = pl.ds(x * ny, ny)
        then = pl.ds(jnp.minimum(x + 1, nx - 1) * ny, ny)
        tn, kn, mtn, msn = [r[then, :] for r in (t_ref, k_ref, mt_ref, ms_ref)]
        y_ref[0, pl.ds(x, 1), :], y_ref[1, pl.ds(x, 1), :] = mt[:1, :], mt[ny - 1 :, :]
        total = from_prev - (6.0 * SUGAR_WEIGHT) * ms
        total = total + jnp.where(x == nx - 1, 0.0, crossing(k, t, mt, kn, tn, mtn, msn))
        to_next = crossing(kn, tn, mtn, k, t, mt, ms)
        for axis, index in ((0, row), (1, lane)):
            size = ny if axis == 0 else LANES
            ta, ka, mta, msa = [ahead(v, axis) for v in (t, k, mt, ms)]
            up = crossing(k, t, mt, ka, ta, mta, msa)
            down = crossing(ka, ta, mta, k, t, mt, ms)
            total = total + jnp.where(index == size - 1, 0.0, up)
            total = total + jnp.where(index == 0, 0.0, pltpu.roll(down, 1, axis))
        pull = HIDDEN_WARMTH * mt + REJECT * ms
        out_ref[here, :] = by_pull_ref[here, :] * pull + w_ref[here, :] * total
        return tn, kn, mtn, msn, to_next

    top = pl.ds(0, ny)
    start = [r[top, :] for r in (t_ref, k_ref, mt_ref, ms_ref)]
    lax.fori_loop(0, nx, plane, (*start, jnp.zeros((ny, LANES), F32)), unroll=unroll)


def finish_kernel(dims, counts, unroll, *refs):
    nx, ny = dims
    ngot = sum(swaps(n) for n in counts)
    w_ref, sense_ref = refs[:2]
    meet = refs[2:5]
    faces = Faces(dims, counts, refs[5:8], refs[8 : 8 + ngot])
    out_ref, rows_ref = refs[8 + ngot :]
    row, lane = grid_iota(ny)
    edge = (lane == 0) | (lane == LANES - 1)

    def into(axis):
        own, near, sugar = faces.own(axis, 0), faces.near(axis, 0), faces.near(axis, 1)
        if axis == 2:
            return FLUX_WEIGHT * (near - own) * meet[2][...] + SUGAR_WEIGHT * sugar
        return [
            FLUX_WEIGHT * (near[side] - own[side]) * meet[axis][side] + SUGAR_WEIGHT * sugar[side]
            for side in (0, 1)
        ]

    into_x, into_y, into_z = into(0), into(1), ready_z(into(2))
    rows_ref[0], rows_ref[1] = into_y

    def plane(x, _):
        here = pl.ds(x * ny, ny)
        value = jnp.where(edge, unpack_z(into_z, x), 0.0) + at_plane(x, nx, into_x)
        value = value + at_rows(x, rows_ref, 0, nx, row, ny)
        out_ref[here, :] = sense_ref[here, :] + w_ref[here, :] * value
        return 0

    lax.fori_loop(0, nx, plane, 0, unroll=unroll)


def totals_kernel(cells, sums_ref, misfit_ref, gradient_ref):
    sums = sums_ref[...]
    which = lax.broadcasted_iota(jnp.int32, sums.shape, 1)
    misfit_ref[0, 0] = jnp.sum(jnp.where(which == 0, sums, 0.0)) / cells
    gradient_ref[0, 0] = jnp.sum(jnp.where(which == 1, sums, 0.0)) / cells


VM = pl.BlockSpec(memory_space=pltpu.VMEM)
SM = pl.BlockSpec(memory_space=pltpu.SMEM)


def call(kernel, out, args, name, scratch=(), in_specs=None, out_specs=None, vmem=32, flops=0, aliases={}):
    size = sum(int(np.prod(a.shape)) * a.dtype.itemsize for a in args)
    return pl.pallas_call(
        kernel,
        out_shape=[jax.ShapeDtypeStruct(s, d) for s, d in out],
        in_specs=in_specs or [VM] * len(args),
        out_specs=out_specs or [VM] * len(out),
        scratch_shapes=list(scratch),
        name=name,
        input_output_aliases=aliases,
        cost_estimate=pl.CostEstimate(flops=flops, bytes_accessed=size, transcendentals=0),
        compiler_params=pltpu.CompilerParams(vmem_limit_bytes=vmem << 20),
    )(*args)


def per_device(counts, warmth, sugar, population, coefficient, sensors):
    nx, ny, nz = warmth.shape
    assert nz == LANES and 2 * nx <= LANES
    bins = population.shape[0]
    dims = (nx, ny)
    cells = nx * ny
    t, s, g = [v.reshape(cells, nz) for v in (warmth, sugar, coefficient)]
    c = population.reshape(bins, cells, nz)
    r = sensors.reshape(2, cells, nz)
    field = ((cells, nz), F32)
    hbm = pl.BlockSpec(memory_space=pl.ANY)
    work = cells * nz * 100

    chunks = 8
    res = call(
        functools.partial(prepare_kernel, dims, counts, bins, chunks),
        [field] * 5 + own_shapes(dims, counts, 3),
        (c, t, s),
        "prepare",
        [pltpu.VMEM((bins, cells, nz), F32), pltpu.SemaphoreType.DMA((chunks + 2,))],
        in_specs=[hbm] * 3,
        vmem=51,
    )
    k, l, m, t, s = res[:5]
    own = res[5:]
    got = send_faces(own, counts)
    pack = ((4 * ny, nz), F32)
    tp, sp, hp, k1, l1, w, v, packs = call(
        functools.partial(first_inner_kernel, dims, 8),
        [field] * 7 + [pack],
        (t, s, k, l, m, g),
        "first_inner",
        flops=work,
    )
    res = call(
        functools.partial(first_edge_kernel, dims, counts, 64),
        [field] * 3 + own_shapes(dims, counts, 4),
        (tp, sp, hp, k1, packs, *own[:3], *got),
        "first_edge",
        [pltpu.VMEM((2, 2 * nx, nz), F32)],
    )
    t1, s1, h0 = res[:3]
    own1 = res[3:]
    got1 = send_faces(own1, counts)
    mtp, msp, by_pull, *inner = call(
        functools.partial(second_inner_kernel, dims, 8),
        [field] * 5,
        (t1, s1, k1, h0, l1, w, v, g, r),
        "second_inner",
        flops=work,
    )
    devices = int(np.prod(counts))
    line = ((devices, LANES), F32)
    meet_shapes = own_shapes(dims, counts, 1)[:3]
    second_own = own_shapes(dims, counts, 2)
    second_own = second_own[2 : 3 + swaps(counts[0])] + [second_own[1]]
    res = call(
        functools.partial(second_edge_kernel, dims, counts, 64),
        [field] * 2 + [line] + meet_shapes + second_own,
        (mtp, msp, *inner, *own1[:3], *got1),
        "second_edge",
        [pltpu.VMEM(v, F32) for v in ((2, 2 * nx, nz), (2, 2 * ny, nz))],
    )
    mt, ms, sums = res[:3]
    meet, sent = res[3:6], list(res[6:])
    sums = lax.all_to_all(sums, AXES, 0, 0, tiled=True)
    a = swaps(counts[0])
    sent[1 + a :] = call(
        functools.partial(choose_kernel, counts),
        own_shapes(dims, counts, 2)[3 + a :],
        (sent[1 + a],),
        "choose",
    )
    got2 = send_faces((None, None, *sent), counts)
    sense, *kept = call(
        functools.partial(third_inner_kernel, dims, 16),
        [field] + meet_shapes[:2],
        (t1, k1, mt, ms, w, by_pull),
        "third_inner",
        aliases={5: 0},
        flops=work,
    )
    (sens,) = call(
        functools.partial(finish_kernel, dims, counts, 64),
        [field],
        (w, sense, *meet, *kept, sent[0], *got2),
        "finish",
        [pltpu.VMEM((2, nx, nz), F32)],
        flops=work,
    )
    sums, sens = lax.optimization_barrier((sums, sens))
    misfit, gradient = call(
        functools.partial(totals_kernel, float(cells * nz * devices)),
        [((1, 1), F32), ((1, 1), F32)],
        (sums,),
        "totals",
        out_specs=[SM, SM],
    )
    return sens.reshape(nx, ny, nz), misfit.reshape(()), gradient.reshape(())


def solution(mesh):
    counts = tuple(mesh.shape[a] for a in AXES)
    placed = (
        P("gx", "gy", "gz"),
        P("gx", "gy", "gz"),
        P(None, "gx", "gy", "gz"),
        P("gx", "gy", "gz"),
        P(None, "gx", "gy", "gz"),
    )
    return jax.shard_map(
        functools.partial(per_device, counts),
        mesh=mesh,
        in_specs=placed,
        out_specs=(P("gx", "gy", "gz"), P(), P()),
        check_vma=False,
    )
```

```python
import functools

import jax
import jax.numpy as jnp
import numpy as np
from jax import lax
from jax.experimental import pallas as pl
from jax.experimental.pallas import tpu as pltpu
from jax.sharding import PartitionSpec as P

F32 = jnp.float32
AXES = ("gx", "gy", "gz")

SOLIDIFY_POINT = 0.5
LOWERING_COEF = 0.5
GROW = 0.3
NUCLEATE = 0.2
VOLUME = 0.005
WARMTH_ADVANCE = 0.08
STEP_SOLUTE = 0.1
HIDDEN_WARMTH = 0.5
REJECT = 0.3
LANES = 128


def volumes(bin_count):
    rank = np.arange(bin_count, dtype=np.float64) + 1.0
    return VOLUME * rank * rank


def functional_weights(bin_count):
    vol = volumes(bin_count)
    step = vol[1:] - vol[:-1]
    k = (1.0, vol)
    l = (NUCLEATE * vol[0], np.concatenate([GROW * step, [0.0]]))
    m_const = GROW * step[0] * NUCLEATE
    m = np.zeros(bin_count)
    for b in range(bin_count - 1):
        m[b] -= GROW * step[b] * GROW
        if b >= 1:
            m[b - 1] += GROW * step[b] * GROW
    return k, l, (m_const, m)


SPARE = {"gx": 0, "gz": 0, "gy": 2}


def swap_pairs(counts, axis, kind):
    pairs = []
    for at in np.ndindex(*counts):
        to = list(at)
        i = at[axis]
        to[axis] = i ^ 1 if kind == 0 else (i + 1 if i % 2 else i - 1)
        if not 0 <= to[axis] < counts[axis]:
            to[axis] = i
            spare = SPARE[AXES[axis]]
            if spare == axis:
                to[axis] = counts[axis] - 1 - i
            else:
                to[spare] = at[spare] ^ 1
        pairs.append(tuple(int(np.ravel_multi_index(v, counts)) for v in (at, to)))
    return pairs


def swaps(count):
    return {1: 0, 2: 1}.get(count, 2)


def exchange(payloads, counts, axis):
    assert counts[axis] == 1 or counts[axis] % 2 == 0
    return [
        lax.ppermute(p, AXES, swap_pairs(counts, axis, kind)) for kind, p in enumerate(payloads)
    ]


class Side:
    def __init__(self, axis, count):
        self.count = count
        self.index = lax.axis_index(axis)
        self.odd = lax.rem(self.index, 2) == 1

    def outgoing(self, first, last):
        kinds = [jnp.where(self.odd, first, last), jnp.where(self.odd, last, first)]
        return kinds[: swaps(self.count)]

    def incoming(self, got):
        if self.count == 1:
            return None
        if self.count == 2:
            zero = jnp.zeros_like(got[0])
            return jnp.where(self.odd, got[0], zero), jnp.where(self.odd, zero, got[0])
        a, b = got
        zero = jnp.zeros_like(a)
        before = jnp.where(self.index > 0, jnp.where(self.odd, a, b), zero)
        after = jnp.where(self.index < self.count - 1, jnp.where(self.odd, b, a), zero)
        return before, after


def grid_iota(ny):
    row = lax.broadcasted_iota(jnp.int32, (ny, LANES), 0)
    lane = lax.broadcasted_iota(jnp.int32, (ny, LANES), 1)
    return row, lane


def pack_z(acc, value, x, lane):
    return jnp.where(lane // 2 == x, pltpu.roll(value, lax.rem(2 * x + 1, LANES), 1), acc)


class Faces:
    def __init__(self, dims, counts, own, got):
        self.nx, self.ny = dims
        self.sides = [Side(a, n) for a, n in zip(AXES, counts)]
        self.mine = own
        a, b = swaps(counts[0]), swaps(counts[1])
        self.got = (got[:a], got[a : a + b], got[a + b :])

    def _part(self, axis, f):
        rows = self.nx if axis == 1 else self.ny
        return pl.ds(f * rows, rows)

    def near(self, axis, f):
        part = [r[self._part(axis, f), :] for r in self.got[axis]]
        before, after = self.sides[axis].incoming(part)
        if axis < 2:
            return before, after
        lane = lax.broadcasted_iota(jnp.int32, before.shape, 1)
        return jnp.where(lax.rem(lane, 2) == 0, before, after)

    def own(self, axis, f):
        if axis < 2:
            return [self.mine[axis][side, self._part(axis, f), :] for side in (0, 1)]
        return turn_z(self.mine[2][self._part(2, f), :])


def turn_z(pack):
    lane = lax.broadcasted_iota(jnp.int32, pack.shape, 1)
    even = lax.rem(lane, 2) == 0
    return jnp.where(even, pltpu.roll(pack, LANES - 1, 1), pltpu.roll(pack, 1, 1))


class Own:
    def __init__(self, dims, counts, refs, scratch=None):
        self.nx, self.ny = dims
        self.counts = counts
        self.x, self.y = scratch or refs[:2]
        self.z, *out = refs if scratch else refs[2:]
        a = swaps(counts[0])
        self.out = (out[:a], out[a:])

    def rows(self, f, x, value):
        self.y[0, pl.ds(f * self.nx + x, 1), :] = value[:1, :]
        self.y[1, pl.ds(f * self.nx + x, 1), :] = value[self.ny - 1 :, :]

    def finish(self, fields, packs):
        nx, ny = self.nx, self.ny
        for f, (ref, pack) in enumerate(zip(fields, packs)):
            part = pl.ds(f * ny, ny)
            self.x[0, part, :] = ref[pl.ds(0, ny), :]
            self.x[1, part, :] = ref[pl.ds((nx - 1) * ny, ny), :]
            self.z[part, :] = pack
        for axis, own in enumerate((self.x, self.y)):
            side = Side(AXES[axis], self.counts[axis])
            for o, v in zip(self.out[axis], side.outgoing(own[0], own[1])):
                o[...] = v


def choose_kernel(counts, rows_ref, *outs):
    for o, v in zip(outs, Side(AXES[1], counts[1]).outgoing(rows_ref[0], rows_ref[1])):
        o[...] = v


def own_shapes(dims, counts, fields):
    nx, ny = dims
    x, y = (fields * ny, LANES), (fields * nx, LANES)
    shapes = [(2, *x), (2, *y), x] + [x] * swaps(counts[0]) + [y] * swaps(counts[1])
    return [(v, F32) for v in shapes]


def send_faces(own, counts):
    a = swaps(counts[0])
    payloads = (own[3 : 3 + a], own[3 + a :], [own[2]] * swaps(counts[2]))
    got = []
    for axis, payload in enumerate(payloads):
        got += exchange(payload, counts, axis)
    return got


def at_plane(x, nx, pair):
    return jnp.where(x == 0, pair[0], jnp.where(x == nx - 1, pair[1], 0.0))


def at_rows(x, ref, f, nx, row, ny):
    part = pl.ds(f * nx + x, 1)
    first, last = ref[0, part, :], ref[1, part, :]
    if ny < 16:
        return jnp.where(row == 0, first, jnp.where(row == ny - 1, last, 0.0))
    parts = [jnp.where(row[:8] == 0, first, 0.0), jnp.where(row[:8] == 7, last, 0.0)]
    if ny > 16:
        parts.insert(1, jnp.zeros((ny - 16, LANES), F32))
    return jnp.concatenate(parts, axis=0)


def pack_edges(pair_x, pair_y, nx, ny):
    _, lane = grid_iota(ny)
    acc = jnp.zeros((ny, LANES), F32)
    for side, x in ((0, 0), (1, nx - 1)):
        acc = acc + pack_z(jnp.zeros_like(acc), pair_x[side], x, lane)
    x, lane = grid_iota(nx)
    row, _ = grid_iota(ny)
    for side, y in ((0, 0), (1, ny - 1)):
        moved = pltpu.roll(pair_y[side], 1, 1, stride=2, stride_axis=0)
        line = jnp.sum(jnp.where(lane // 2 == x, moved, 0.0), axis=0, keepdims=True)
        acc = acc + jnp.where(row == y, line, 0.0)
    return acc


def ready_z(value):
    lane = lax.broadcasted_iota(jnp.int32, value.shape, 1)
    return jnp.where(lax.rem(lane, 2) == 0, value, pltpu.roll(value, LANES - 2, 1))


def unpack_z(value, x):
    return pltpu.roll(value, lax.rem(LANES - 2 * x, LANES), 1)


def half_flux(k, t, kn, tn):
    return 0.5 * (k + kn) * (tn - t)


def behind(value, axis):
    return pltpu.roll(value, 1, axis)


def divergence(k, fields, axis, index):
    last = index == k.shape[axis] - 1
    up, down = 0.5 * (k + ahead(k, axis)), 0.5 * (k + behind(k, axis))
    up, down = jnp.where(last, 0.0, up), jnp.where(index == 0, 0.0, down)
    return [up * (ahead(v, axis) - v) + down * (behind(v, axis) - v) for v in fields]


def ahead(value, axis):
    return pltpu.roll(value, value.shape[axis] - 1, axis)


def neighbour_sum(value, axis, index):
    size = value.shape[axis]
    up = jnp.where(index == size - 1, 0.0, ahead(value, axis))
    return up + jnp.where(index == 0, 0.0, pltpu.roll(value, 1, axis))


def log1p_of(e, u, inv):
    return jnp.log(u) + (e - (u - 1.0)) * inv


def softplus_parts(v):
    e = jnp.exp(-jnp.abs(v))
    u = 1.0 + e
    inv = 1.0 / u
    soft = jnp.maximum(v, 0.0) + log1p_of(e, u, inv)
    return soft, jnp.where(v >= 0, inv, e * inv)


def prepare_kernel(dims, counts, bins, chunks, *refs):
    nx, ny = dims
    c_hbm, t_hbm, s_hbm = refs[:3]
    k_ref, l_ref, m_ref, t_ref, s_ref = refs[3:8]
    own = Own(dims, counts, refs[8:-2])
    c_ref, sems = refs[-2:]
    copies = [
        pltpu.make_async_copy(t_hbm, t_ref, sems.at[chunks]),
        pltpu.make_async_copy(s_hbm, s_ref, sems.at[chunks + 1]),
    ]
    ends = [nx * i // 16 for i in (0, 2, 6, 10, 14, 16)]
    for j in range(chunks):
        part = pl.ds(ends[j] * ny, (ends[j + 1] - ends[j]) * ny)
        copies.append(pltpu.make_async_copy(c_hbm.at[:, part, :], c_ref.at[:, part, :], sems.at[j]))
    for copy in copies:
        copy.start()
    copies[0].wait()
    copies[1].wait()
    _, lane = grid_iota(ny)
    weights = functional_weights(bins)

    def plane(x, accs):
        here = pl.ds(x * ny, ny)
        c = [c_ref[b, here, :] for b in range(bins)]
        values = []
        for const, per_bin in weights:
            total = None
            for b in range(bins):
                if per_bin[b] != 0.0:
                    term = float(per_bin[b]) * c[b]
                    total = term if total is None else total + term
            values.append(float(const) + total)
        k_ref[here, :], l_ref[here, :], m_ref[here, :] = values
        faces = (t_ref[here, :], s_ref[here, :], values[0])
        for f, v in enumerate(faces):
            own.rows(f, x, v)
        return tuple(pack_z(a, v, x, lane) for a, v in zip(accs, faces))

    accs = tuple(jnp.zeros((ny, LANES), F32) for _ in range(3))
    for j in range(chunks):
        copies[2 + j].wait()
        accs = lax.fori_loop(ends[j], ends[j + 1], plane, accs, unroll=min(8, ends[j + 1] - ends[j]))
    own.finish((t_ref, s_ref, k_ref), accs)


def first_inner_kernel(dims, unroll, *refs):
    nx, ny = dims
    t_ref, s_ref, k_ref, l_ref, m_ref, g_ref = refs[:6]
    t1, s1, h0, k1, l1, w0, v0, packs = refs[6:]
    row, lane = grid_iota(ny)

    def plane(x, carry):
        t, s, k, s_prev, flux_prev = carry
        here = pl.ds(x * ny, ny)
        then = pl.ds(jnp.minimum(x + 1, nx - 1) * ny, ny)
        tn, sn, kn = t_ref[then, :], s_ref[then, :], k_ref[then, :]
        flux = half_flux(k, t, kn, tn)
        heat = flux - flux_prev
        for axis, index in ((0, row), (1, lane)):
            heat = heat + divergence(k, (t,), axis, index)[0]
        s_next = jnp.where(x == nx - 1, 0.0, sn)
        diff = (s_prev + s_next) + neighbour_sum(s, 0, row)
        diff = diff + neighbour_sum(s, 1, lane) - 6.0 * s
        g, l, m = g_ref[here, :], l_ref[here, :], m_ref[here, :]
        soft, _ = softplus_parts(SOLIDIFY_POINT - LOWERING_COEF * s - t)
        w, v = soft * l, soft * m
        frost = g * w
        new_t = t + WARMTH_ADVANCE * heat + HIDDEN_WARMTH * frost
        new_s = s + STEP_SOLUTE * diff + REJECT * frost
        new_k = k + frost
        t1[here, :], s1[here, :], h0[here, :], k1[here, :] = new_t, new_s, heat, new_k
        l1[here, :], w0[here, :], v0[here, :] = l + g * v, w, v
        return tn, sn, kn, s, flux

    top = pl.ds(0, ny)
    zero = jnp.zeros((ny, LANES), F32)
    carry = (t_ref[top, :], s_ref[top, :], k_ref[top, :], zero, zero)
    lax.fori_loop(0, nx, plane, carry, unroll=unroll)
    fields = (t1, s1, k1, h0)

    def pack(x, accs):
        here = pl.ds(x * ny, ny)
        return tuple(pack_z(a, r[here, :], x, lane) for a, r in zip(accs, fields))

    for f, acc in enumerate(lax.fori_loop(0, nx, pack, (zero,) * 4, unroll=64)):
        packs[pl.ds(f * ny, ny), :] = acc


def first_edge_kernel(dims, counts, unroll, *refs):
    nx, ny = dims
    ngot = sum(swaps(n) for n in counts)
    tp_ref, sp_ref, hp_ref, k1_ref, packs_ref = refs[:5]
    faces = Faces(dims, counts, refs[5:8], refs[8 : 8 + ngot])
    t1, s1, h0 = refs[8 + ngot : 11 + ngot]
    own = Own(dims, counts, refs[11 + ngot : -1])
    rows_ref = refs[-1]
    row, lane = grid_iota(ny)
    edge = (lane == 0) | (lane == LANES - 1)

    def flux_in(axis):
        tn, sn, kn = [faces.near(axis, f) for f in range(3)]
        to, ko = faces.own(axis, 0), faces.own(axis, 2)
        if axis == 2:
            return half_flux(ko, to, kn, tn), sn
        return [half_flux(*v) for v in zip(ko, to, kn, tn)], sn

    heat_x, sugar_x = flux_in(0)
    heat_y, sugar_y = flux_in(1)
    for side in (0, 1):
        rows_ref[side, pl.ds(0, nx), :] = heat_y[side]
        rows_ref[side, pl.ds(nx, nx), :] = sugar_y[side]
    heat_z, sugar_z = flux_in(2)
    in_heat, in_sugar = ready_z(heat_z), ready_z(sugar_z)

    def plane(x, _):
        here = pl.ds(x * ny, ny)
        heat = at_plane(x, nx, heat_x) + at_rows(x, rows_ref, 0, nx, row, ny)
        diff = at_plane(x, nx, sugar_x) + at_rows(x, rows_ref, 1, nx, row, ny)
        some_t = tp_ref[here, :] + WARMTH_ADVANCE * heat
        some_s = sp_ref[here, :] + STEP_SOLUTE * diff
        some_h = hp_ref[here, :] + heat
        heat = jnp.where(edge, unpack_z(in_heat, x), 0.0)
        diff = jnp.where(edge, unpack_z(in_sugar, x), 0.0)
        new_t = some_t + WARMTH_ADVANCE * heat
        new_s = some_s + STEP_SOLUTE * diff
        new_h = some_h + heat
        t1[here, :], s1[here, :], h0[here, :] = new_t, new_s, new_h
        for f, v in enumerate((new_t, new_s, k1_ref[here, :], new_h)):
            own.rows(f, x, v)
        return 0

    lax.fori_loop(0, nx, plane, 0, unroll=unroll)
    heat = turn_z(heat_z) + pack_edges(heat_x, heat_y, nx, ny)
    sugar = turn_z(sugar_z) + pack_edges(sugar_x, sugar_y, nx, ny)
    packs = [packs_ref[pl.ds(f * ny, ny), :] for f in range(4)]
    packs[0] = packs[0] + WARMTH_ADVANCE * heat
    packs[1] = packs[1] + STEP_SOLUTE * sugar
    packs[3] = packs[3] + heat
    own.finish((t1, s1, k1_ref, h0), packs)


def second_inner_kernel(dims, unroll, *refs):
    nx, ny = dims
    t_ref, s_ref, k_ref, h_ref, l_ref, w_ref, v_ref, g_ref, r_ref = refs[:9]
    mt_ref, ms_ref, by_pull_ref, with_miss_ref, with_pull_ref = refs[9:]
    row, lane = grid_iota(ny)

    def plane(x, carry):
        t, s, k, h, s_prev, flux_prev, other_prev = carry
        here = pl.ds(x * ny, ny)
        then = pl.ds(jnp.minimum(x + 1, nx - 1) * ny, ny)
        tn, sn, kn, hn = t_ref[then, :], s_ref[then, :], k_ref[then, :], h_ref[then, :]
        both = 0.5 * (k + kn)
        flux, other = both * (tn - t), both * (hn - h)
        heat, again = flux - flux_prev, other - other_prev
        for axis, index in ((0, row), (1, lane)):
            more, other_more = divergence(k, (t, h), axis, index)
            heat, again = heat + more, again + other_more
        s_next = jnp.where(x == nx - 1, 0.0, sn)
        diff = (s_prev + s_next) + neighbour_sum(s, 0, row)
        diff = diff + neighbour_sum(s, 1, lane) - 6.0 * s
        g, l = g_ref[here, :], l_ref[here, :]
        soft, slope = softplus_parts(SOLIDIFY_POINT - LOWERING_COEF * s - t)
        frost = g * soft * l
        mt_ref[here, :] = (
            t + WARMTH_ADVANCE * heat + HIDDEN_WARMTH * frost - r_ref[0, here, :].astype(F32)
        )
        ms_ref[here, :] = s + STEP_SOLUTE * diff + REJECT * frost - r_ref[1, here, :].astype(F32)
        below = g * l * slope
        by_pull_ref[here, :] = soft * (l + g * v_ref[here, :]) + w_ref[here, :] * (
            1.0 - (HIDDEN_WARMTH + REJECT * LOWERING_COEF) * below
        )
        with_miss_ref[here, :] = heat + WARMTH_ADVANCE * again + h
        with_pull_ref[here, :] = below * h
        return tn, sn, kn, hn, s, flux, other

    top = pl.ds(0, ny)
    zero = jnp.zeros((ny, LANES), F32)
    start = [r[top, :] for r in (t_ref, s_ref, k_ref, h_ref)]
    lax.fori_loop(0, nx, plane, (*start, zero, zero, zero), unroll=unroll)


def second_edge_kernel(dims, counts, unroll, *refs):
    nx, ny = dims
    ngot = sum(swaps(n) for n in counts)
    mtp_ref, msp_ref, with_miss_ref, with_pull_ref = refs[:4]
    faces = Faces(dims, counts, refs[4:7], refs[7 : 7 + ngot])
    mt_ref, ms_ref, sums_ref = refs[7 + ngot : 10 + ngot]
    meet = refs[10 + ngot : 13 + ngot]
    own = Own(dims, counts, refs[13 + ngot : -3], (refs[-1], refs[-3]))
    rows_ref = refs[-2]
    row, lane = grid_iota(ny)
    edge = (lane == 0) | (lane == LANES - 1)

    def flux_in(axis):
        tn, sn, kn, hn = [faces.near(axis, f) for f in range(4)]
        to, ko, ho = [faces.own(axis, f) for f in (0, 2, 3)]
        if axis == 2:
            meet[2][...] = (0.5 * ko + to) + (0.5 * kn - tn)
            return half_flux(ko, to, kn, tn), sn, half_flux(ko, ho, kn, hn)
        for side in (0, 1):
            meet[axis][side] = (0.5 * ko[side] + to[side]) + (0.5 * kn[side] - tn[side])
        heat = [half_flux(*v) for v in zip(ko, to, kn, tn)]
        return heat, sn, [half_flux(*v) for v in zip(ko, ho, kn, hn)]

    heat_x, sugar_x, again_x = flux_in(0)
    heat_y, sugar_y, again_y = flux_in(1)
    for side in (0, 1):
        rows_ref[side, pl.ds(0, nx), :] = heat_y[side]
        rows_ref[side, pl.ds(nx, nx), :] = sugar_y[side]
    heat_z, sugar_z, again_z = flux_in(2)
    in_heat, in_sugar = ready_z(heat_z), ready_z(sugar_z)

    def plane(x, carry):
        accs, misfit, part = carry
        here = pl.ds(x * ny, ny)
        heat = at_plane(x, nx, heat_x) + at_rows(x, rows_ref, 0, nx, row, ny)
        diff = at_plane(x, nx, sugar_x) + at_rows(x, rows_ref, 1, nx, row, ny)
        some_t = mtp_ref[here, :] + WARMTH_ADVANCE * heat
        some_s = msp_ref[here, :] + STEP_SOLUTE * diff
        heat = jnp.where(edge, unpack_z(in_heat, x), 0.0)
        diff = jnp.where(edge, unpack_z(in_sugar, x), 0.0)
        mt = some_t + WARMTH_ADVANCE * heat
        ms = some_s + STEP_SOLUTE * diff
        mt_ref[here, :], ms_ref[here, :] = mt, ms
        misfit = misfit + (mt * mt + ms * ms)
        pull = HIDDEN_WARMTH * mt + REJECT * ms
        part = part + (mt * with_miss_ref[here, :] - pull * with_pull_ref[here, :])
        for f, v in enumerate((mt, ms)):
            own.rows(f, x, v)
        accs = tuple(pack_z(a, z, x, lane) for a, z in zip(accs, (some_t, some_s)))
        return accs, misfit, part

    zero = jnp.zeros((ny, LANES), F32)
    accs, misfit, part = lax.fori_loop(
        0, nx, plane, ((zero, zero), zero, zero), unroll=unroll
    )
    packs = (
        accs[0] + WARMTH_ADVANCE * turn_z(heat_z),
        accs[1] + STEP_SOLUTE * turn_z(sugar_z),
    )
    own.finish((mt_ref, ms_ref), packs)
    part = part + turn_z(packs[0]) * (heat_z + WARMTH_ADVANCE * again_z)
    rows = None
    for side in (0, 1):
        part = part + own.x[side, pl.ds(0, ny), :] * (
            heat_x[side] + WARMTH_ADVANCE * again_x[side]
        )
        line = own.y[side, pl.ds(0, nx), :] * (heat_y[side] + WARMTH_ADVANCE * again_y[side])
        rows = line if rows is None else rows + line
    for first in range(0, nx, ny):
        part = part + rows[first : first + ny]
    lane_row = lax.broadcasted_iota(jnp.int32, (1, LANES), 1)
    line = jnp.where(lane_row == 0, 0.5 * jnp.sum(misfit), 0.0)
    line = jnp.where(lane_row == 1, WARMTH_ADVANCE * jnp.sum(part), line)
    sums_ref[...] = jnp.broadcast_to(line, sums_ref.shape)


FLUX_WEIGHT = 0.5 * WARMTH_ADVANCE
SUGAR_WEIGHT = REJECT * STEP_SOLUTE


def crossing(k, t, mt, kn, tn, mtn, msn):
    return FLUX_WEIGHT * (mtn - mt) * (0.5 * (k + kn) + (t - tn)) + SUGAR_WEIGHT * msn


def third_inner_kernel(dims, unroll, *refs):
    nx, ny = dims
    t_ref, k_ref, mt_ref, ms_ref, w_ref, by_pull_ref = refs[:6]
    out_ref, x_ref, y_ref = refs[6:]
    row, lane = grid_iota(ny)
    x_ref[0], x_ref[1] = mt_ref[pl.ds(0, ny), :], mt_ref[pl.ds((nx - 1) * ny, ny), :]

    def plane(x, carry):
        t, k, mt, ms, from_prev = carry
        here = pl.ds(x * ny, ny)
        then = pl.ds(jnp.minimum(x + 1, nx - 1) * ny, ny)
        tn, kn, mtn, msn = [r[then, :] for r in (t_ref, k_ref, mt_ref, ms_ref)]
        y_ref[0, pl.ds(x, 1), :], y_ref[1, pl.ds(x, 1), :] = mt[:1, :], mt[ny - 1 :, :]
        total = from_prev - (6.0 * SUGAR_WEIGHT) * ms
        total = total + jnp.where(x == nx - 1, 0.0, crossing(k, t, mt, kn, tn, mtn, msn))
        to_next = crossing(kn, tn, mtn, k, t, mt, ms)
        for axis, index in ((0, row), (1, lane)):
            size = ny if axis == 0 else LANES
            ta, ka, mta, msa = [ahead(v, axis) for v in (t, k, mt, ms)]
            up = crossing(k, t, mt, ka, ta, mta, msa)
            down = crossing(ka, ta, mta, k, t, mt, ms)
            total = total + jnp.where(index == size - 1, 0.0, up)
            total = total + jnp.where(index == 0, 0.0, pltpu.roll(down, 1, axis))
        pull = HIDDEN_WARMTH * mt + REJECT * ms
        out_ref[here, :] = by_pull_ref[here, :] * pull + w_ref[here, :] * total
        return tn, kn, mtn, msn, to_next

    top = pl.ds(0, ny)
    start = [r[top, :] for r in (t_ref, k_ref, mt_ref, ms_ref)]
    lax.fori_loop(0, nx, plane, (*start, jnp.zeros((ny, LANES), F32)), unroll=unroll)


def finish_kernel(dims, counts, unroll, *refs):
    nx, ny = dims
    ngot = sum(swaps(n) for n in counts)
    w_ref, sense_ref = refs[:2]
    meet = refs[2:5]
    faces = Faces(dims, counts, refs[5:8], refs[8 : 8 + ngot])
    out_ref, rows_ref = refs[8 + ngot :]
    row, lane = grid_iota(ny)
    edge = (lane == 0) | (lane == LANES - 1)

    def into(axis):
        own, near, sugar = faces.own(axis, 0), faces.near(axis, 0), faces.near(axis, 1)
        if axis == 2:
            return FLUX_WEIGHT * (near - own) * meet[2][...] + SUGAR_WEIGHT * sugar
        return [
            FLUX_WEIGHT * (near[side] - own[side]) * meet[axis][side] + SUGAR_WEIGHT * sugar[side]
            for side in (0, 1)
        ]

    into_x, into_y, into_z = into(0), into(1), ready_z(into(2))
    rows_ref[0], rows_ref[1] = into_y

    def plane(x, _):
        here = pl.ds(x * ny, ny)
        value = jnp.where(edge, unpack_z(into_z, x), 0.0) + at_plane(x, nx, into_x)
        value = value + at_rows(x, rows_ref, 0, nx, row, ny)
        out_ref[here, :] = sense_ref[here, :] + w_ref[here, :] * value
        return 0

    lax.fori_loop(0, nx, plane, 0, unroll=unroll)


def totals_kernel(cells, sums_ref, misfit_ref, gradient_ref):
    sums = sums_ref[...]
    which = lax.broadcasted_iota(jnp.int32, sums.shape, 1)
    misfit_ref[0, 0] = jnp.sum(jnp.where(which == 0, sums, 0.0)) / cells
    gradient_ref[0, 0] = jnp.sum(jnp.where(which == 1, sums, 0.0)) / cells


VM = pl.BlockSpec(memory_space=pltpu.VMEM)
SM = pl.BlockSpec(memory_space=pltpu.SMEM)


def call(kernel, out, args, name, scratch=(), in_specs=None, out_specs=None, vmem=32, flops=0, aliases={}):
    size = sum(int(np.prod(a.shape)) * a.dtype.itemsize for a in args)
    return pl.pallas_call(
        kernel,
        out_shape=[jax.ShapeDtypeStruct(s, d) for s, d in out],
        in_specs=in_specs or [VM] * len(args),
        out_specs=out_specs or [VM] * len(out),
        scratch_shapes=list(scratch),
        name=name,
        input_output_aliases=aliases,
        cost_estimate=pl.CostEstimate(flops=flops, bytes_accessed=size, transcendentals=0),
        compiler_params=pltpu.CompilerParams(vmem_limit_bytes=vmem << 20),
    )(*args)


def per_device(counts, warmth, sugar, population, coefficient, sensors):
    nx, ny, nz = warmth.shape
    assert nz == LANES and 2 * nx <= LANES
    bins = population.shape[0]
    dims = (nx, ny)
    cells = nx * ny
    t, s, g = [v.reshape(cells, nz) for v in (warmth, sugar, coefficient)]
    c = population.reshape(bins, cells, nz)
    r = sensors.reshape(2, cells, nz)
    field = ((cells, nz), F32)
    hbm = pl.BlockSpec(memory_space=pl.ANY)
    work = cells * nz * 100

    chunks = 5
    res = call(
        functools.partial(prepare_kernel, dims, counts, bins, chunks),
        [field] * 5 + own_shapes(dims, counts, 3),
        (c, t, s),
        "prepare",
        [pltpu.VMEM((bins, cells, nz), F32), pltpu.SemaphoreType.DMA((chunks + 2,))],
        in_specs=[hbm] * 3,
        vmem=51,
    )
    k, l, m, t, s = res[:5]
    own = res[5:]
    got = send_faces(own, counts)
    pack = ((4 * ny, nz), F32)
    tp, sp, hp, k1, l1, w, v, packs = call(
        functools.partial(first_inner_kernel, dims, 8),
        [field] * 7 + [pack],
        (t, s, k, l, m, g),
        "first_inner",
        flops=work,
    )
    res = call(
        functools.partial(first_edge_kernel, dims, counts, 64),
        [field] * 3 + own_shapes(dims, counts, 4),
        (tp, sp, hp, k1, packs, *own[:3], *got),
        "first_edge",
        [pltpu.VMEM((2, 2 * nx, nz), F32)],
    )
    t1, s1, h0 = res[:3]
    own1 = res[3:]
    got1 = send_faces(own1, counts)
    mtp, msp, by_pull, *inner = call(
        functools.partial(second_inner_kernel, dims, 8),
        [field] * 5,
        (t1, s1, k1, h0, l1, w, v, g, r),
        "second_inner",
        flops=work,
    )
    devices = int(np.prod(counts))
    line = ((devices, LANES), F32)
    meet_shapes = own_shapes(dims, counts, 1)[:3]
    second_own = own_shapes(dims, counts, 2)
    second_own = second_own[2 : 3 + swaps(counts[0])] + [second_own[1]]
    res = call(
        functools.partial(second_edge_kernel, dims, counts, 64),
        [field] * 2 + [line] + meet_shapes + second_own,
        (mtp, msp, *inner, *own1[:3], *got1),
        "second_edge",
        [pltpu.VMEM(v, F32) for v in ((2, 2 * nx, nz), (2, 2 * ny, nz))],
    )
    mt, ms, sums = res[:3]
    meet, sent = res[3:6], list(res[6:])
    sums = lax.all_to_all(sums, AXES, 0, 0, tiled=True)
    a = swaps(counts[0])
    sent[1 + a :] = call(
        functools.partial(choose_kernel, counts),
        own_shapes(dims, counts, 2)[3 + a :],
        (sent[1 + a],),
        "choose",
    )
    got2 = send_faces((None, None, *sent), counts)
    sense, *kept = call(
        functools.partial(third_inner_kernel, dims, 16),
        [field] + meet_shapes[:2],
        (t1, k1, mt, ms, w, by_pull),
        "third_inner",
        aliases={5: 0},
        flops=work,
    )
    (sens,) = call(
        functools.partial(finish_kernel, dims, counts, 64),
        [field],
        (w, sense, *meet, *kept, sent[0], *got2),
        "finish",
        [pltpu.VMEM((2, nx, nz), F32)],
        flops=work,
    )
    sums, sens = lax.optimization_barrier((sums, sens))
    misfit, gradient = call(
        functools.partial(totals_kernel, float(cells * nz * devices)),
        [((1, 1), F32), ((1, 1), F32)],
        (sums,),
        "totals",
        out_specs=[SM, SM],
    )
    return sens.reshape(nx, ny, nz), misfit.reshape(()), gradient.reshape(())


def solution(mesh):
    counts = tuple(mesh.shape[a] for a in AXES)
    placed = (
        P("gx", "gy", "gz"),
        P("gx", "gy", "gz"),
        P(None, "gx", "gy", "gz"),
        P("gx", "gy", "gz"),
        P(None, "gx", "gy", "gz"),
    )
    return jax.shard_map(
        functools.partial(per_device, counts),
        mesh=mesh,
        in_specs=placed,
        out_specs=(P("gx", "gy", "gz"), P(), P()),
        check_vma=False,
    )
```

```python
import functools

import jax
import jax.numpy as jnp
import numpy as np
from jax import lax
from jax.experimental import pallas as pl
from jax.experimental.pallas import tpu as pltpu
from jax.sharding import PartitionSpec as P

F32 = jnp.float32
AXES = ("gx", "gy", "gz")

SOLIDIFY_POINT = 0.5
LOWERING_COEF = 0.5
GROW = 0.3
NUCLEATE = 0.2
VOLUME = 0.005
WARMTH_ADVANCE = 0.08
STEP_SOLUTE = 0.1
HIDDEN_WARMTH = 0.5
REJECT = 0.3
LANES = 128


def volumes(bin_count):
    rank = np.arange(bin_count, dtype=np.float64) + 1.0
    return VOLUME * rank * rank


def functional_weights(bin_count):
    vol = volumes(bin_count)
    step = vol[1:] - vol[:-1]
    k = (1.0, vol)
    l = (NUCLEATE * vol[0], np.concatenate([GROW * step, [0.0]]))
    m_const = GROW * step[0] * NUCLEATE
    m = np.zeros(bin_count)
    for b in range(bin_count - 1):
        m[b] -= GROW * step[b] * GROW
        if b >= 1:
            m[b - 1] += GROW * step[b] * GROW
    return k, l, (m_const, m)


SPARE = {"gx": 0, "gz": 0, "gy": 2}


def swap_pairs(counts, axis, kind):
    pairs = []
    for at in np.ndindex(*counts):
        to = list(at)
        i = at[axis]
        to[axis] = i ^ 1 if kind == 0 else (i + 1 if i % 2 else i - 1)
        if not 0 <= to[axis] < counts[axis]:
            to[axis] = i
            spare = SPARE[AXES[axis]]
            if spare == axis:
                to[axis] = counts[axis] - 1 - i
            else:
                to[spare] = at[spare] ^ 1
        pairs.append(tuple(int(np.ravel_multi_index(v, counts)) for v in (at, to)))
    return pairs


def swaps(count):
    return {1: 0, 2: 1}.get(count, 2)


def exchange(payloads, counts, axis):
    assert counts[axis] == 1 or counts[axis] % 2 == 0
    return [
        lax.ppermute(p, AXES, swap_pairs(counts, axis, kind)) for kind, p in enumerate(payloads)
    ]


class Side:
    def __init__(self, axis, count):
        self.count = count
        self.index = lax.axis_index(axis)
        self.odd = lax.rem(self.index, 2) == 1

    def outgoing(self, first, last):
        kinds = [jnp.where(self.odd, first, last), jnp.where(self.odd, last, first)]
        return kinds[: swaps(self.count)]

    def incoming(self, got):
        if self.count == 1:
            return None
        if self.count == 2:
            zero = jnp.zeros_like(got[0])
            return jnp.where(self.odd, got[0], zero), jnp.where(self.odd, zero, got[0])
        a, b = got
        zero = jnp.zeros_like(a)
        before = jnp.where(self.index > 0, jnp.where(self.odd, a, b), zero)
        after = jnp.where(self.index < self.count - 1, jnp.where(self.odd, b, a), zero)
        return before, after


def grid_iota(ny):
    row = lax.broadcasted_iota(jnp.int32, (ny, LANES), 0)
    lane = lax.broadcasted_iota(jnp.int32, (ny, LANES), 1)
    return row, lane


def pack_z(acc, value, x, lane):
    return jnp.where(lane // 2 == x, pltpu.roll(value, lax.rem(2 * x + 1, LANES), 1), acc)


class Faces:
    def __init__(self, dims, counts, own, got):
        self.nx, self.ny = dims
        self.sides = [Side(a, n) for a, n in zip(AXES, counts)]
        self.mine = own
        a, b = swaps(counts[0]), swaps(counts[1])
        self.got = (got[:a], got[a : a + b], got[a + b :])

    def _part(self, axis, f):
        rows = self.nx if axis == 1 else self.ny
        return pl.ds(f * rows, rows)

    def near(self, axis, f):
        part = [r[self._part(axis, f), :] for r in self.got[axis]]
        before, after = self.sides[axis].incoming(part)
        if axis < 2:
            return before, after
        lane = lax.broadcasted_iota(jnp.int32, before.shape, 1)
        return jnp.where(lax.rem(lane, 2) == 0, before, after)

    def own(self, axis, f):
        if axis < 2:
            return [self.mine[axis][side, self._part(axis, f), :] for side in (0, 1)]
        return turn_z(self.mine[2][self._part(2, f), :])


def turn_z(pack):
    lane = lax.broadcasted_iota(jnp.int32, pack.shape, 1)
    even = lax.rem(lane, 2) == 0
    return jnp.where(even, pltpu.roll(pack, LANES - 1, 1), pltpu.roll(pack, 1, 1))


class Own:
    def __init__(self, dims, counts, refs, scratch=None):
        self.nx, self.ny = dims
        self.counts = counts
        self.x, self.y = scratch or refs[:2]
        self.z, *out = refs if scratch else refs[2:]
        a = swaps(counts[0])
        self.out = (out[:a], out[a:])

    def rows(self, f, x, value):
        self.y[0, pl.ds(f * self.nx + x, 1), :] = value[:1, :]
        self.y[1, pl.ds(f * self.nx + x, 1), :] = value[self.ny - 1 :, :]

    def finish(self, fields, packs):
        nx, ny = self.nx, self.ny
        for f, (ref, pack) in enumerate(zip(fields, packs)):
            part = pl.ds(f * ny, ny)
            self.x[0, part, :] = ref[pl.ds(0, ny), :]
            self.x[1, part, :] = ref[pl.ds((nx - 1) * ny, ny), :]
            self.z[part, :] = pack
        for axis, own in enumerate((self.x, self.y)):
            side = Side(AXES[axis], self.counts[axis])
            for o, v in zip(self.out[axis], side.outgoing(own[0], own[1])):
                o[...] = v


def choose_kernel(counts, rows_ref, *outs):
    for o, v in zip(outs, Side(AXES[1], counts[1]).outgoing(rows_ref[0], rows_ref[1])):
        o[...] = v


def own_shapes(dims, counts, fields):
    nx, ny = dims
    x, y = (fields * ny, LANES), (fields * nx, LANES)
    shapes = [(2, *x), (2, *y), x] + [x] * swaps(counts[0]) + [y] * swaps(counts[1])
    return [(v, F32) for v in shapes]


def send_faces(own, counts):
    a = swaps(counts[0])
    payloads = (own[3 : 3 + a], own[3 + a :], [own[2]] * swaps(counts[2]))
    got = []
    for axis, payload in enumerate(payloads):
        got += exchange(payload, counts, axis)
    return got


def at_plane(x, nx, pair):
    return jnp.where(x == 0, pair[0], jnp.where(x == nx - 1, pair[1], 0.0))


def at_rows(x, ref, f, nx, row, ny):
    part = pl.ds(f * nx + x, 1)
    first, last = ref[0, part, :], ref[1, part, :]
    if ny < 16:
        return jnp.where(row == 0, first, jnp.where(row == ny - 1, last, 0.0))
    parts = [jnp.where(row[:8] == 0, first, 0.0), jnp.where(row[:8] == 7, last, 0.0)]
    if ny > 16:
        parts.insert(1, jnp.zeros((ny - 16, LANES), F32))
    return jnp.concatenate(parts, axis=0)


def pack_edges(pair_x, pair_y, nx, ny):
    _, lane = grid_iota(ny)
    acc = jnp.zeros((ny, LANES), F32)
    for side, x in ((0, 0), (1, nx - 1)):
        acc = acc + pack_z(jnp.zeros_like(acc), pair_x[side], x, lane)
    x, lane = grid_iota(nx)
    row, _ = grid_iota(ny)
    for side, y in ((0, 0), (1, ny - 1)):
        moved = pltpu.roll(pair_y[side], 1, 1, stride=2, stride_axis=0)
        line = jnp.sum(jnp.where(lane // 2 == x, moved, 0.0), axis=0, keepdims=True)
        acc = acc + jnp.where(row == y, line, 0.0)
    return acc


def ready_z(value):
    lane = lax.broadcasted_iota(jnp.int32, value.shape, 1)
    return jnp.where(lax.rem(lane, 2) == 0, value, pltpu.roll(value, LANES - 2, 1))


def unpack_z(value, x):
    return pltpu.roll(value, lax.rem(LANES - 2 * x, LANES), 1)


def half_flux(k, t, kn, tn):
    return 0.5 * (k + kn) * (tn - t)


def behind(value, axis):
    return pltpu.roll(value, 1, axis)


def divergence(k, fields, axis, index):
    last = index == k.shape[axis] - 1
    half = 0.5 * k
    up, down = half + ahead(half, axis), half + behind(half, axis)
    up, down = jnp.where(last, 0.0, up), jnp.where(index == 0, 0.0, down)
    return [up * (ahead(v, axis) - v) + down * (behind(v, axis) - v) for v in fields]


def ahead(value, axis):
    return pltpu.roll(value, value.shape[axis] - 1, axis)


def neighbour_sum(value, axis, index):
    size = value.shape[axis]
    up = jnp.where(index == size - 1, 0.0, ahead(value, axis))
    return up + jnp.where(index == 0, 0.0, pltpu.roll(value, 1, axis))


def log1p_of(e, u):
    return jnp.log(u) + (e - (u - 1.0))


def softplus_parts(v):
    e = jnp.exp(-jnp.abs(v))
    u = 1.0 + e
    inv = 1.0 / u
    soft = jnp.maximum(v, 0.0) + log1p_of(e, u)
    return soft, jnp.where(v >= 0, inv, e * inv)


def prepare_kernel(dims, counts, bins, chunks, *refs):
    nx, ny = dims
    c_hbm, t_hbm, s_hbm = refs[:3]
    k_ref, l_ref, m_ref, t_ref, s_ref = refs[3:8]
    own = Own(dims, counts, refs[8:-2])
    c_ref, sems = refs[-2:]
    rows = nx * ny // chunks
    copies = [
        pltpu.make_async_copy(t_hbm, t_ref, sems.at[chunks]),
        pltpu.make_async_copy(s_hbm, s_ref, sems.at[chunks + 1]),
    ]
    for j in range(chunks):
        part = pl.ds(j * rows, rows)
        copies.append(pltpu.make_async_copy(c_hbm.at[:, part, :], c_ref.at[:, part, :], sems.at[j]))
    for copy in copies:
        copy.start()
    copies[0].wait()
    copies[1].wait()
    _, lane = grid_iota(ny)
    weights = functional_weights(bins)

    def plane(x, accs):
        here = pl.ds(x * ny, ny)
        c = [c_ref[b, here, :] for b in range(bins)]
        values = []
        for const, per_bin in weights:
            total = None
            for b in range(bins):
                if per_bin[b] != 0.0:
                    term = float(per_bin[b]) * c[b]
                    total = term if total is None else total + term
            values.append(float(const) + total)
        k_ref[here, :], l_ref[here, :], m_ref[here, :] = values
        faces = (t_ref[here, :], s_ref[here, :], values[0])
        for f, v in enumerate(faces):
            own.rows(f, x, v)
        return tuple(pack_z(a, v, x, lane) for a, v in zip(accs, faces))

    accs = tuple(jnp.zeros((ny, LANES), F32) for _ in range(3))
    planes = nx // chunks
    for j in range(chunks):
        copies[2 + j].wait()
        accs = lax.fori_loop(j * planes, (j + 1) * planes, plane, accs, unroll=8)
    own.finish((t_ref, s_ref, k_ref), accs)


def first_inner_kernel(dims, unroll, *refs):
    nx, ny = dims
    t_ref, s_ref, k_ref, l_ref, m_ref, g_ref = refs[:6]
    t1, s1, h0, k1, l1, w0, v0, packs = refs[6:]
    row, lane = grid_iota(ny)

    def plane(x, carry):
        t, s, k, s_prev, flux_prev = carry
        here = pl.ds(x * ny, ny)
        then = pl.ds(jnp.minimum(x + 1, nx - 1) * ny, ny)
        tn, sn, kn = t_ref[then, :], s_ref[then, :], k_ref[then, :]
        flux = half_flux(k, t, kn, tn)
        heat = flux - flux_prev
        for axis, index in ((0, row), (1, lane)):
            heat = heat + divergence(k, (t,), axis, index)[0]
        s_next = jnp.where(x == nx - 1, 0.0, sn)
        diff = (s_prev + s_next) + neighbour_sum(s, 0, row)
        diff = diff + neighbour_sum(s, 1, lane) - 6.0 * s
        g, l, m = g_ref[here, :], l_ref[here, :], m_ref[here, :]
        soft, _ = softplus_parts(SOLIDIFY_POINT - LOWERING_COEF * s - t)
        w, v = soft * l, soft * m
        frost = g * w
        new_t = t + WARMTH_ADVANCE * heat + HIDDEN_WARMTH * frost
        new_s = s + STEP_SOLUTE * diff + REJECT * frost
        new_k = k + frost
        t1[here, :], s1[here, :], h0[here, :], k1[here, :] = new_t, new_s, heat, new_k
        l1[here, :], w0[here, :], v0[here, :] = l + g * v, w, v
        return tn, sn, kn, s, flux

    top = pl.ds(0, ny)
    zero = jnp.zeros((ny, LANES), F32)
    carry = (t_ref[top, :], s_ref[top, :], k_ref[top, :], zero, zero)
    lax.fori_loop(0, nx, plane, carry, unroll=unroll)
    fields = (t1, s1, k1, h0)

    def pack(x, accs):
        here = pl.ds(x * ny, ny)
        return tuple(pack_z(a, r[here, :], x, lane) for a, r in zip(accs, fields))

    for f, acc in enumerate(lax.fori_loop(0, nx, pack, (zero,) * 4, unroll=64)):
        packs[pl.ds(f * ny, ny), :] = acc


def first_edge_kernel(dims, counts, unroll, *refs):
    nx, ny = dims
    ngot = sum(swaps(n) for n in counts)
    tp_ref, sp_ref, hp_ref, k1_ref, packs_ref = refs[:5]
    faces = Faces(dims, counts, refs[5:8], refs[8 : 8 + ngot])
    t1, s1, h0 = refs[8 + ngot : 11 + ngot]
    own = Own(dims, counts, refs[11 + ngot : -1])
    rows_ref = refs[-1]
    row, lane = grid_iota(ny)
    edge = (lane == 0) | (lane == LANES - 1)

    def flux_in(axis):
        tn, sn, kn = [faces.near(axis, f) for f in range(3)]
        to, ko = faces.own(axis, 0), faces.own(axis, 2)
        if axis == 2:
            return half_flux(ko, to, kn, tn), sn
        return [half_flux(*v) for v in zip(ko, to, kn, tn)], sn

    heat_x, sugar_x = flux_in(0)
    heat_y, sugar_y = flux_in(1)
    for side in (0, 1):
        rows_ref[side, pl.ds(0, nx), :] = heat_y[side]
        rows_ref[side, pl.ds(nx, nx), :] = sugar_y[side]
    heat_z, sugar_z = flux_in(2)
    in_heat, in_sugar = ready_z(heat_z), ready_z(sugar_z)

    def plane(x, _):
        here = pl.ds(x * ny, ny)
        heat = at_plane(x, nx, heat_x) + at_rows(x, rows_ref, 0, nx, row, ny)
        diff = at_plane(x, nx, sugar_x) + at_rows(x, rows_ref, 1, nx, row, ny)
        some_t = tp_ref[here, :] + WARMTH_ADVANCE * heat
        some_s = sp_ref[here, :] + STEP_SOLUTE * diff
        some_h = hp_ref[here, :] + heat
        heat = jnp.where(edge, unpack_z(in_heat, x), 0.0)
        diff = jnp.where(edge, unpack_z(in_sugar, x), 0.0)
        new_t = some_t + WARMTH_ADVANCE * heat
        new_s = some_s + STEP_SOLUTE * diff
        new_h = some_h + heat
        t1[here, :], s1[here, :], h0[here, :] = new_t, new_s, new_h
        for f, v in enumerate((new_t, new_s, k1_ref[here, :], new_h)):
            own.rows(f, x, v)
        return 0

    lax.fori_loop(0, nx, plane, 0, unroll=unroll)
    heat = turn_z(heat_z) + pack_edges(heat_x, heat_y, nx, ny)
    sugar = turn_z(sugar_z) + pack_edges(sugar_x, sugar_y, nx, ny)
    packs = [packs_ref[pl.ds(f * ny, ny), :] for f in range(4)]
    packs[0] = packs[0] + WARMTH_ADVANCE * heat
    packs[1] = packs[1] + STEP_SOLUTE * sugar
    packs[3] = packs[3] + heat
    own.finish((t1, s1, k1_ref, h0), packs)


def second_inner_kernel(dims, unroll, *refs):
    nx, ny = dims
    t_ref, s_ref, k_ref, h_ref, l_ref, w_ref, v_ref, g_ref, r_ref = refs[:9]
    mt_ref, ms_ref, by_pull_ref, with_miss_ref, with_pull_ref = refs[9:]
    row, lane = grid_iota(ny)

    def plane(x, carry):
        t, s, k, h, s_prev, flux_prev, other_prev = carry
        here = pl.ds(x * ny, ny)
        then = pl.ds(jnp.minimum(x + 1, nx - 1) * ny, ny)
        tn, sn, kn, hn = t_ref[then, :], s_ref[then, :], k_ref[then, :], h_ref[then, :]
        both = 0.5 * (k + kn)
        flux, other = both * (tn - t), both * (hn - h)
        heat, again = flux - flux_prev, other - other_prev
        for axis, index in ((0, row), (1, lane)):
            more, other_more = divergence(k, (t, h), axis, index)
            heat, again = heat + more, again + other_more
        s_next = jnp.where(x == nx - 1, 0.0, sn)
        diff = (s_prev + s_next) + neighbour_sum(s, 0, row)
        diff = diff + neighbour_sum(s, 1, lane) - 6.0 * s
        g, l = g_ref[here, :], l_ref[here, :]
        soft, slope = softplus_parts(SOLIDIFY_POINT - LOWERING_COEF * s - t)
        frost = g * soft * l
        mt_ref[here, :] = (
            t + WARMTH_ADVANCE * heat + HIDDEN_WARMTH * frost - r_ref[0, here, :].astype(F32)
        )
        ms_ref[here, :] = s + STEP_SOLUTE * diff + REJECT * frost - r_ref[1, here, :].astype(F32)
        below = g * l * slope
        by_pull_ref[here, :] = soft * (l + g * v_ref[here, :]) + w_ref[here, :] * (
            1.0 - (HIDDEN_WARMTH + REJECT * LOWERING_COEF) * below
        )
        with_miss_ref[here, :] = heat + WARMTH_ADVANCE * again + h
        with_pull_ref[here, :] = below * h
        return tn, sn, kn, hn, s, flux, other

    top = pl.ds(0, ny)
    zero = jnp.zeros((ny, LANES), F32)
    start = [r[top, :] for r in (t_ref, s_ref, k_ref, h_ref)]
    lax.fori_loop(0, nx, plane, (*start, zero, zero, zero), unroll=unroll)


def second_edge_kernel(dims, counts, unroll, *refs):
    nx, ny = dims
    ngot = sum(swaps(n) for n in counts)
    mtp_ref, msp_ref, with_miss_ref, with_pull_ref = refs[:4]
    faces = Faces(dims, counts, refs[4:7], refs[7 : 7 + ngot])
    mt_ref, ms_ref, sums_ref = refs[7 + ngot : 10 + ngot]
    meet = refs[10 + ngot : 13 + ngot]
    own = Own(dims, counts, refs[13 + ngot : -3], (refs[-1], refs[-3]))
    rows_ref = refs[-2]
    row, lane = grid_iota(ny)
    edge = (lane == 0) | (lane == LANES - 1)

    def flux_in(axis):
        tn, sn, kn, hn = [faces.near(axis, f) for f in range(4)]
        to, ko, ho = [faces.own(axis, f) for f in (0, 2, 3)]
        if axis == 2:
            meet[2][...] = (0.5 * ko + to) + (0.5 * kn - tn)
            return half_flux(ko, to, kn, tn), sn, half_flux(ko, ho, kn, hn)
        for side in (0, 1):
            meet[axis][side] = (0.5 * ko[side] + to[side]) + (0.5 * kn[side] - tn[side])
        heat = [half_flux(*v) for v in zip(ko, to, kn, tn)]
        return heat, sn, [half_flux(*v) for v in zip(ko, ho, kn, hn)]

    heat_x, sugar_x, again_x = flux_in(0)
    heat_y, sugar_y, again_y = flux_in(1)
    for side in (0, 1):
        rows_ref[side, pl.ds(0, nx), :] = heat_y[side]
        rows_ref[side, pl.ds(nx, nx), :] = sugar_y[side]
    heat_z, sugar_z, again_z = flux_in(2)
    in_heat, in_sugar = ready_z(heat_z), ready_z(sugar_z)

    def plane(x, carry):
        accs, misfit, part = carry
        here = pl.ds(x * ny, ny)
        heat = at_plane(x, nx, heat_x) + at_rows(x, rows_ref, 0, nx, row, ny)
        diff = at_plane(x, nx, sugar_x) + at_rows(x, rows_ref, 1, nx, row, ny)
        some_t = mtp_ref[here, :] + WARMTH_ADVANCE * heat
        some_s = msp_ref[here, :] + STEP_SOLUTE * diff
        heat = jnp.where(edge, unpack_z(in_heat, x), 0.0)
        diff = jnp.where(edge, unpack_z(in_sugar, x), 0.0)
        mt = some_t + WARMTH_ADVANCE * heat
        ms = some_s + STEP_SOLUTE * diff
        mt_ref[here, :], ms_ref[here, :] = mt, ms
        misfit = misfit + (mt * mt + ms * ms)
        pull = HIDDEN_WARMTH * mt + REJECT * ms
        part = part + (mt * with_miss_ref[here, :] - pull * with_pull_ref[here, :])
        for f, v in enumerate((mt, ms)):
            own.rows(f, x, v)
        accs = tuple(pack_z(a, z, x, lane) for a, z in zip(accs, (some_t, some_s)))
        return accs, misfit, part

    zero = jnp.zeros((ny, LANES), F32)
    accs, misfit, part = lax.fori_loop(
        0, nx, plane, ((zero, zero), zero, zero), unroll=unroll
    )
    packs = (
        accs[0] + WARMTH_ADVANCE * turn_z(heat_z),
        accs[1] + STEP_SOLUTE * turn_z(sugar_z),
    )
    own.finish((mt_ref, ms_ref), packs)
    part = part + turn_z(packs[0]) * (heat_z + WARMTH_ADVANCE * again_z)
    rows = None
    for side in (0, 1):
        part = part + own.x[side, pl.ds(0, ny), :] * (
            heat_x[side] + WARMTH_ADVANCE * again_x[side]
        )
        line = own.y[side, pl.ds(0, nx), :] * (heat_y[side] + WARMTH_ADVANCE * again_y[side])
        rows = line if rows is None else rows + line
    for first in range(0, nx, ny):
        part = part + rows[first : first + ny]
    lane_row = lax.broadcasted_iota(jnp.int32, (1, LANES), 1)
    line = jnp.where(lane_row == 0, 0.5 * jnp.sum(misfit), 0.0)
    line = jnp.where(lane_row == 1, WARMTH_ADVANCE * jnp.sum(part), line)
    sums_ref[...] = jnp.broadcast_to(line, sums_ref.shape)


FLUX_WEIGHT = 0.5 * WARMTH_ADVANCE
SUGAR_WEIGHT = REJECT * STEP_SOLUTE


def crossing(k, t, mt, kn, tn, mtn, msn):
    return FLUX_WEIGHT * (mtn - mt) * (0.5 * (k + kn) + (t - tn)) + SUGAR_WEIGHT * msn


def third_inner_kernel(dims, unroll, *refs):
    nx, ny = dims
    t_ref, k_ref, mt_ref, ms_ref, w_ref, by_pull_ref = refs[:6]
    out_ref, x_ref, y_ref = refs[6:]
    row, lane = grid_iota(ny)
    x_ref[0], x_ref[1] = mt_ref[pl.ds(0, ny), :], mt_ref[pl.ds((nx - 1) * ny, ny), :]

    def plane(x, carry):
        t, k, mt, ms, from_prev = carry
        here = pl.ds(x * ny, ny)
        then = pl.ds(jnp.minimum(x + 1, nx - 1) * ny, ny)
        tn, kn, mtn, msn = [r[then, :] for r in (t_ref, k_ref, mt_ref, ms_ref)]
        y_ref[0, pl.ds(x, 1), :], y_ref[1, pl.ds(x, 1), :] = mt[:1, :], mt[ny - 1 :, :]
        total = from_prev - (6.0 * SUGAR_WEIGHT) * ms
        total = total + jnp.where(x == nx - 1, 0.0, crossing(k, t, mt, kn, tn, mtn, msn))
        to_next = crossing(kn, tn, mtn, k, t, mt, ms)
        for axis, index in ((0, row), (1, lane)):
            size = ny if axis == 0 else LANES
            ta, ka, mta, msa = [ahead(v, axis) for v in (t, k, mt, ms)]
            up = crossing(k, t, mt, ka, ta, mta, msa)
            down = crossing(ka, ta, mta, k, t, mt, ms)
            total = total + jnp.where(index == size - 1, 0.0, up)
            total = total + jnp.where(index == 0, 0.0, pltpu.roll(down, 1, axis))
        pull = HIDDEN_WARMTH * mt + REJECT * ms
        out_ref[here, :] = by_pull_ref[here, :] * pull + w_ref[here, :] * total
        return tn, kn, mtn, msn, to_next

    top = pl.ds(0, ny)
    start = [r[top, :] for r in (t_ref, k_ref, mt_ref, ms_ref)]
    lax.fori_loop(0, nx, plane, (*start, jnp.zeros((ny, LANES), F32)), unroll=unroll)


def finish_kernel(dims, counts, unroll, *refs):
    nx, ny = dims
    ngot = sum(swaps(n) for n in counts)
    w_ref, sense_ref = refs[:2]
    meet = refs[2:5]
    faces = Faces(dims, counts, refs[5:8], refs[8 : 8 + ngot])
    out_ref, rows_ref = refs[8 + ngot :]
    row, lane = grid_iota(ny)
    edge = (lane == 0) | (lane == LANES - 1)

    def into(axis):
        own, near, sugar = faces.own(axis, 0), faces.near(axis, 0), faces.near(axis, 1)
        if axis == 2:
            return FLUX_WEIGHT * (near - own) * meet[2][...] + SUGAR_WEIGHT * sugar
        return [
            FLUX_WEIGHT * (near[side] - own[side]) * meet[axis][side] + SUGAR_WEIGHT * sugar[side]
            for side in (0, 1)
        ]

    into_x, into_y, into_z = into(0), into(1), ready_z(into(2))
    rows_ref[0], rows_ref[1] = into_y

    def plane(x, _):
        here = pl.ds(x * ny, ny)
        value = jnp.where(edge, unpack_z(into_z, x), 0.0) + at_plane(x, nx, into_x)
        value = value + at_rows(x, rows_ref, 0, nx, row, ny)
        out_ref[here, :] = sense_ref[here, :] + w_ref[here, :] * value
        return 0

    lax.fori_loop(0, nx, plane, 0, unroll=unroll)


def totals_kernel(cells, sums_ref, misfit_ref, gradient_ref):
    sums = sums_ref[...]
    which = lax.broadcasted_iota(jnp.int32, sums.shape, 1)
    misfit_ref[0, 0] = jnp.sum(jnp.where(which == 0, sums, 0.0)) / cells
    gradient_ref[0, 0] = jnp.sum(jnp.where(which == 1, sums, 0.0)) / cells


VM = pl.BlockSpec(memory_space=pltpu.VMEM)
SM = pl.BlockSpec(memory_space=pltpu.SMEM)


def call(kernel, out, args, name, scratch=(), in_specs=None, out_specs=None, vmem=32, flops=0, aliases={}):
    size = sum(int(np.prod(a.shape)) * a.dtype.itemsize for a in args)
    return pl.pallas_call(
        kernel,
        out_shape=[jax.ShapeDtypeStruct(s, d) for s, d in out],
        in_specs=in_specs or [VM] * len(args),
        out_specs=out_specs or [VM] * len(out),
        scratch_shapes=list(scratch),
        name=name,
        input_output_aliases=aliases,
        cost_estimate=pl.CostEstimate(flops=flops, bytes_accessed=size, transcendentals=0),
        compiler_params=pltpu.CompilerParams(vmem_limit_bytes=vmem << 20),
    )(*args)


def per_device(counts, warmth, sugar, population, coefficient, sensors):
    nx, ny, nz = warmth.shape
    assert nz == LANES and 2 * nx <= LANES
    bins = population.shape[0]
    dims = (nx, ny)
    cells = nx * ny
    t, s, g = [v.reshape(cells, nz) for v in (warmth, sugar, coefficient)]
    c = population.reshape(bins, cells, nz)
    r = sensors.reshape(2, cells, nz)
    field = ((cells, nz), F32)
    hbm = pl.BlockSpec(memory_space=pl.ANY)
    work = cells * nz * 100

    chunks = 8
    res = call(
        functools.partial(prepare_kernel, dims, counts, bins, chunks),
        [field] * 5 + own_shapes(dims, counts, 3),
        (c, t, s),
        "prepare",
        [pltpu.VMEM((bins, cells, nz), F32), pltpu.SemaphoreType.DMA((chunks + 2,))],
        in_specs=[hbm] * 3,
        vmem=51,
    )
    k, l, m, t, s = res[:5]
    own = res[5:]
    got = send_faces(own, counts)
    pack = ((4 * ny, nz), F32)
    tp, sp, hp, k1, l1, w, v, packs = call(
        functools.partial(first_inner_kernel, dims, 8),
        [field] * 7 + [pack],
        (t, s, k, l, m, g),
        "first_inner",
        flops=work,
    )
    res = call(
        functools.partial(first_edge_kernel, dims, counts, 64),
        [field] * 3 + own_shapes(dims, counts, 4),
        (tp, sp, hp, k1, packs, *own[:3], *got),
        "first_edge",
        [pltpu.VMEM((2, 2 * nx, nz), F32)],
    )
    t1, s1, h0 = res[:3]
    own1 = res[3:]
    got1 = send_faces(own1, counts)
    mtp, msp, by_pull, *inner = call(
        functools.partial(second_inner_kernel, dims, 8),
        [field] * 5,
        (t1, s1, k1, h0, l1, w, v, g, r),
        "second_inner",
        flops=work,
    )
    devices = int(np.prod(counts))
    line = ((devices, LANES), F32)
    meet_shapes = own_shapes(dims, counts, 1)[:3]
    second_own = own_shapes(dims, counts, 2)
    second_own = second_own[2 : 3 + swaps(counts[0])] + [second_own[1]]
    res = call(
        functools.partial(second_edge_kernel, dims, counts, 64),
        [field] * 2 + [line] + meet_shapes + second_own,
        (mtp, msp, *inner, *own1[:3], *got1),
        "second_edge",
        [pltpu.VMEM(v, F32) for v in ((2, 2 * nx, nz), (2, 2 * ny, nz))],
    )
    mt, ms, sums = res[:3]
    meet, sent = res[3:6], list(res[6:])
    sums = lax.all_to_all(sums, AXES, 0, 0, tiled=True)
    a = swaps(counts[0])
    sent[1 + a :] = call(
        functools.partial(choose_kernel, counts),
        own_shapes(dims, counts, 2)[3 + a :],
        (sent[1 + a],),
        "choose",
    )
    got2 = send_faces((None, None, *sent), counts)
    sense, *kept = call(
        functools.partial(third_inner_kernel, dims, 16),
        [field] + meet_shapes[:2],
        (t1, k1, mt, ms, w, by_pull),
        "third_inner",
        aliases={5: 0},
        flops=work,
    )
    (sens,) = call(
        functools.partial(finish_kernel, dims, counts, 64),
        [field],
        (w, sense, *meet, *kept, sent[0], *got2),
        "finish",
        [pltpu.VMEM((2, nx, nz), F32)],
        flops=work,
    )
    sums, sens = lax.optimization_barrier((sums, sens))
    misfit, gradient = call(
        functools.partial(totals_kernel, float(cells * nz * devices)),
        [((1, 1), F32), ((1, 1), F32)],
        (sums,),
        "totals",
        out_specs=[SM, SM],
    )
    return sens.reshape(nx, ny, nz), misfit.reshape(()), gradient.reshape(())


def solution(mesh):
    counts = tuple(mesh.shape[a] for a in AXES)
    placed = (
        P("gx", "gy", "gz"),
        P("gx", "gy", "gz"),
        P(None, "gx", "gy", "gz"),
        P("gx", "gy", "gz"),
        P(None, "gx", "gy", "gz"),
    )
    return jax.shard_map(
        functools.partial(per_device, counts),
        mesh=mesh,
        in_specs=placed,
        out_specs=(P("gx", "gy", "gz"), P(), P()),
        check_vma=False,
    )
```
